32 devices in a mesh: fsdp: 16 (over z, y, core), tp: 2 (over x).
Axes of the slice: x: 2, y: 2, z: 4, core: 2. Of those that a mesh axis runs over, the one named last changes fastest.
Arguments:
- tokens: bfloat16 [3, 16, 1280, 1024], P(None, 'fsdp', 'tp'), may hold values from -6 to 6
- segments: int32 [3, 16, 1280], P(None, 'fsdp', 'tp'), may hold values from 0 to 12, as said below
- parents: int32 [3, 16, 13], P(None, 'fsdp'), may hold values from 0 to 4, as said below
- norm_gains: float32 [4, 1024], replicated, may hold values from 0.5 to 1.5
- norm_biases: float32 [4, 1024], replicated, may hold values from -1.8 to 1.8
- w_qkv: bfloat16 [1024, 3, 1024], P('fsdp', None, 'tp'), may hold values from -0.1875 to 0.1875
- w_out: bfloat16 [1024, 1024], P('tp', 'fsdp'), may hold values from -0.1875 to 0.1875
- w_up: bfloat16 [1024, 4096], P('fsdp', 'tp'), may hold values from -0.1875 to 0.1875
- w_down: bfloat16 [4096, 1024], P('tp', 'fsdp'), may hold values from -0.09375 to 0.09375
- cotangent: bfloat16 [3, 16, 1280, 1024], P(None, 'fsdp', 'tp'), may hold values from -12 to 12
Outputs:
- out: bfloat16 [3, 16, 1280, 1024], P(None, 'fsdp', 'tp')
- input_grad: float32 [3, 16, 1280, 1024], P(None, 'fsdp', 'tp')
- grad_w_qkv: float32 [1024, 3, 1024], P('fsdp', None, 'tp')
- grad_w_out: float32 [1024, 1024], P('tp', 'fsdp')
- grad_w_up: float32 [1024, 4096], P('fsdp', 'tp')
- grad_w_down: float32 [4096, 1024], P('tp', 'fsdp')
- grad_gains: float32 [4, 1024], replicated
- grad_biases: float32 [4, 1024], replicated
The draws below stay inside these ranges and needn't reach their ends.
Inputs may be any that keep to these rules, and one draw needn't show every extreme that they name: Along each tree the segment number never falls; segment 0, the trunk, begins the tree and holds between 384 and 768 tokens; segments 1 to 4 are branches and 5 to 12 leaves, each after its parent. parents[m, t, s] is the parent segment of segment s: 0 for segments 0 to 4 (the trunk is its own), a branch for each leaf, each branch the parent of exactly two leaves.
All inputs are finite; a program needn't handle non-finite values.
Results may differ from the reference program's by a relative error of at most 0.017.
Values may be sent and summed in bfloat16 or wider, within the bound.
A program may use at most 512 MiB of HBM per device.

```python
import math
import jax
import jax.numpy as jnp
from jax import lax

D = 1024
HEADS = 16
HEAD_DIM = 64
FF = 4096
NSEG = 13
MICRO = 3
SEG = 64
TREE_LEN = 1280
TREES = 16


def tree_layout(key):
    trunk_key = jax.random.fold_in(key, 71)
    share_key = jax.random.fold_in(key, 72)
    order_key = jax.random.fold_in(key, 73)
    trunk_len = SEG * jax.random.randint(trunk_key, (MICRO, TREES, 1), 6, 13)
    rest_len = TREE_LEN - trunk_len
    shares = jax.random.randint(share_key, (MICRO, TREES, 12), 1, 4)
    cumulative = jnp.cumsum(shares, axis=-1)
    starts = trunk_len + rest_len * (cumulative - shares) // cumulative[:, :, 11:12]
    starts = jnp.concatenate([jnp.zeros((MICRO, TREES, 1), jnp.int32), starts.astype(jnp.int32)], axis=-1)
    positions = jnp.arange(TREE_LEN, dtype=jnp.int32)
    segment_ids = jnp.sum((positions[None, None, :, None] >= starts[:, :, None, :]).astype(jnp.int32), axis=-1) - 1
    rank_keys = jax.random.randint(order_key, (MICRO, TREES, 8), 0, 1 << 20) * 8 + jnp.arange(8, dtype=jnp.int32)
    leaf_order = jnp.argsort(rank_keys, axis=-1).astype(jnp.int32)
    parent_ids = jnp.concatenate([jnp.zeros((MICRO, TREES, 5), jnp.int32), 1 + leaf_order // 2], axis=-1)
    return (segment_ids.astype(jnp.int32), parent_ids.astype(jnp.int32))


def draw_segments(key, part):
    return tree_layout(key)[0]


def draw_parents(key, part):
    return tree_layout(key)[1]


def draw_cotangent(key, part):
    tree_rise = 1.0 + 2.0 * jnp.arange(TREES, dtype=jnp.float32) / max(TREES - 1, 1)
    full_shape = (MICRO, TREES, TREE_LEN, D)
    draw_base = jnp.clip(jax.random.normal(key, full_shape, jnp.float32), -4.0, 4.0)
    return (draw_base * tree_rise[None, :, None, None]).astype(jnp.bfloat16)


def shard_levels(own_key, shape, cuts, low, largest):
    level, own = 1.0, jax.random.fold_in(own_key, 6)
    for position, shards_of in cuts:
        heights = jnp.exp(jax.random.uniform(jax.random.fold_in(own, position), (shards_of,), jnp.float32, low / len(cuts), largest / len(cuts)))
        level = level * jnp.repeat(heights, shape[position] // shards_of).reshape([-1 if axis == position else 1 for axis in range(len(shape))])
    return level


def scatter_about(stream_key, dims, width, most, cuts=(), held_as=jnp.bfloat16):
    values = jax.random.normal(stream_key, dims, jnp.float32) * width
    if len(cuts) > 0:
        values = shard_levels(stream_key, dims, cuts, -0.22, 0.18) * values
    return jnp.clip(values, min=-most, max=most).astype(held_as)


def setup_inputs(seed: int = 0) -> dict:
    splits = jax.random.split(jax.random.key(seed), 11)
    tokens = scatter_about(splits[0], (MICRO, TREES, TREE_LEN, D), 1.0, 6.0, ((1, 16), (2, 2)))
    segments = draw_segments(jax.random.fold_in(splits[10], 71), 0)
    parents = draw_parents(jax.random.fold_in(splits[10], 71), 0)
    norm_gains = jnp.clip(1.0 + 0.1 * jax.random.normal(splits[3], (4, D), jnp.float32), 0.5, 1.5)
    norm_biases = scatter_about(splits[4], (4, D), 0.3, 1.8, (), jnp.float32)
    w_qkv = scatter_about(splits[5], (D, 3, D), D ** -0.5, 0.1875, ((0, 16), (2, 2)))
    w_out = scatter_about(splits[6], (D, D), D ** -0.5, 0.1875, ((0, 2), (1, 16)))
    w_up = scatter_about(splits[7], (D, FF), D ** -0.5, 0.1875, ((0, 16), (1, 2)))
    w_down = scatter_about(splits[8], (FF, D), FF ** -0.5, 0.09375, ((0, 2), (1, 16)))
    cotangent = draw_cotangent(jax.random.fold_in(splits[10], 71), 0)
    return {"tokens": tokens, "segments": segments, "parents": parents, "norm_gains": norm_gains, "norm_biases": norm_biases, "w_qkv": w_qkv, "w_out": w_out, "w_up": w_up, "w_down": w_down, "cotangent": cotangent}


relax_alpha = 32.0
norm_eps = 1e-05
masked_value = -1e+30
highest = lax.Precision.HIGHEST

@jax.custom_vjp
def low(v):
    return lax.optimization_barrier(v.astype(jnp.bfloat16)).astype(jnp.float32)

@jax.custom_vjp
def low_back(v):
    return v

def low_keep(v):
    return (low(v), None)

def low_pass(kept, grad):
    return (grad,)

def back_keep(v):
    return (v, None)

def back_low(kept, grad):
    return (low(grad),)
low.defvjp(low_keep, low_pass)
low_back.defvjp(back_keep, back_low)

def layer_norm(values, gain, shift):
    mean_row = lax.optimization_barrier(jnp.mean(values, axis=-1, keepdims=True))
    centered = values - mean_row
    variance = lax.optimization_barrier(jnp.mean(centered * centered, axis=-1, keepdims=True))
    return centered * lax.rsqrt(variance + norm_eps) * gain + shift

def gelu_tanh(values):
    return jax.nn.gelu(values, approximate=True)

def path_allowed(seg_rows, row_start, seg_all, parents):
    seg_count = parents.shape[0]
    labels = jnp.arange(seg_count, dtype=jnp.int32)
    parent_row = lax.optimization_barrier(jnp.sum(jnp.where(seg_rows[:, None] == labels[None, :], parents[None, :], 0), axis=1))
    grand_row = lax.optimization_barrier(jnp.sum(jnp.where(parent_row[:, None] == labels[None, :], parents[None, :], 0), axis=1))
    column = seg_all[None, :]
    on_path = (column == seg_rows[:, None]) | (column == parent_row[:, None]) | (column == grand_row[:, None])
    row_pos = row_start + jnp.arange(seg_rows.shape[0], dtype=jnp.int32)
    col_pos = jnp.arange(seg_all.shape[0], dtype=jnp.int32)
    return on_path & (col_pos[None, :] <= row_pos[:, None])

def forward(params, tree_input, seg_all, parents):
    norm_gains, norm_biases, w_qkv, w_out, w_up, w_down = params
    tree_len = tree_input.shape[0]
    model_width = tree_input.shape[1]
    block_rows = tree_len // 2
    query_scale = 1.0 / (relax_alpha * math.sqrt(HEAD_DIM))
    normed_a = low(layer_norm(tree_input, norm_gains[0], norm_biases[0]))
    qkv_proj = jnp.dot(normed_a, w_qkv.reshape(model_width, 3 * model_width), precision=highest)
    qkv_proj = qkv_proj.reshape(tree_len, 3, HEADS, HEAD_DIM)
    query_low = low(low_back(qkv_proj[:, 0] * query_scale)).transpose(1, 0, 2)
    key_all = low(low_back(qkv_proj[:, 1])).transpose(1, 0, 2)
    val_all = low(low_back(qkv_proj[:, 2])).transpose(1, 0, 2)

    def one_block(block_index):
        row_start = block_index * block_rows
        qry_blk = lax.dynamic_slice_in_dim(query_low, row_start, block_rows, 1)
        seg_rows = lax.dynamic_slice_in_dim(seg_all, row_start, block_rows, 0)
        scores = low_back(relax_alpha * jnp.einsum('hqd,hkd->hqk', qry_blk, key_all, precision=highest))
        allowed = path_allowed(seg_rows, row_start, seg_all, parents)
        masked = jnp.where(allowed[None], scores, masked_value)
        top_row = lax.optimization_barrier(jnp.max(masked, axis=-1, keepdims=True))
        exp_rows = jnp.exp(masked - top_row)
        prob_rows = exp_rows / lax.optimization_barrier(jnp.sum(exp_rows, axis=-1, keepdims=True))
        return jnp.einsum('hqk,hkd->hqd', low(prob_rows), val_all, precision=highest)
    blocks = lax.map(jax.checkpoint(one_block), jnp.arange(2, dtype=jnp.int32))
    attended = blocks.transpose(0, 2, 1, 3).reshape(tree_len, model_width)
    attended_low = low(low_back(attended))
    branch_a = low_back(jnp.dot(attended_low, w_out, precision=highest))
    residual = tree_input + layer_norm(branch_a, norm_gains[1], norm_biases[1])
    normed_f = low(layer_norm(residual, norm_gains[2], norm_biases[2]))
    up_proj = low_back(jnp.dot(normed_f, w_up, precision=highest))
    hidden = low(gelu_tanh(up_proj))
    branch_f = low_back(jnp.dot(hidden, w_down, precision=highest))
    return residual + layer_norm(branch_f, norm_gains[3], norm_biases[3])

def reference(tokens, segments, parents, norm_gains, norm_biases, w_qkv, w_out, w_up, w_down, cotangent):
    params = (norm_gains.astype(jnp.float32), norm_biases.astype(jnp.float32), w_qkv.astype(jnp.float32), w_out.astype(jnp.float32), w_up.astype(jnp.float32), w_down.astype(jnp.float32))
    tree_count = MICRO * TREES
    flat_tokens = tokens.reshape(tree_count, TREE_LEN, D)
    flat_segs = segments.reshape(tree_count, TREE_LEN)
    flat_parents = parents.reshape(tree_count, NSEG)
    flat_cot = cotangent.reshape(tree_count, TREE_LEN, D)

    def one_tree(running, tree_items):
        tree_tokens, tree_segs, tree_parents, tree_cot = tree_items

        def run_tree(prm, tree_input):
            return forward(prm, tree_input, tree_segs, tree_parents)
        result, pullback = jax.vjp(run_tree, params, tree_tokens.astype(jnp.float32))
        grad_params, grad_input = pullback(tree_cot.astype(jnp.float32))
        running = jax.tree.map(jnp.add, running, grad_params)
        return (running, (result.astype(jnp.bfloat16), grad_input))
    start_sums = jax.tree.map(jnp.zeros_like, params)
    grad_sums, (out_rows, grads_in) = lax.scan(one_tree, start_sums, (flat_tokens, flat_segs, flat_parents, flat_cot))
    return (out_rows.reshape(MICRO, TREES, TREE_LEN, D), grads_in.reshape(MICRO, TREES, TREE_LEN, D), grad_sums[2], grad_sums[3], grad_sums[4], grad_sums[5], grad_sums[0], grad_sums[1])
```

```python
import math

import jax
import jax.numpy as jnp
from jax import lax
from jax.experimental import pallas as pl
from jax.experimental.pallas import tpu as pltpu
from jax.sharding import PartitionSpec as P

HEAD_DIM = 64
norm_eps = 1e-05
masked_value = -1e30
f32 = jnp.float32
bf16 = jnp.bfloat16
exp2_scale = math.log2(math.e) / math.sqrt(HEAD_DIM)
grad_scale = 1.0 / math.sqrt(HEAD_DIM)


def dot_nn(a, b):
    return lax.dot_general(a, b, (((1,), (0,)), ((), ())), preferred_element_type=f32)


def dot_nt(a, b):
    return lax.dot_general(a, b, (((1,), (1,)), ((), ())), preferred_element_type=f32)


def dot_tn(a, b):
    return lax.dot_general(a, b, (((0,), (0,)), ((), ())), preferred_element_type=f32)


def split_heads(x):
    lane = lax.broadcasted_iota(jnp.int32, x.shape, 1)
    zero = jnp.zeros_like(x)
    return jnp.where(lane < HEAD_DIM, x, zero), jnp.where(lane >= HEAD_DIM, x, zero)


def block_rows(tree_len):
    return 256 if tree_len % 256 == 0 else 128


def attention_forward_kernel(q_ref, k_ref, v_ref, col_ref, row_ref, o_ref, lse_ref, bias):
    tree_len = q_ref.shape[0]
    rows = block_rows(tree_len)

    @pl.when(pl.program_id(0) == 0)
    def _():
        for start in range(0, tree_len, rows):
            stop = start + rows
            key_seg = row_ref[0:1, :stop]
            ok = col_ref[start:stop, 0:1] == key_seg
            ok = ok | (col_ref[start:stop, 1:2] == key_seg)
            ok = ok | (col_ref[start:stop, 2:3] == key_seg)
            i = lax.broadcasted_iota(jnp.int32, (rows, stop), 0) + start
            j = lax.broadcasted_iota(jnp.int32, (rows, stop), 1)
            bias[start:stop, :stop] = jnp.where(ok & (j <= i), 0.0, masked_value).astype(f32)

    for start in range(0, tree_len, rows):
        stop = start + rows
        queries = split_heads(q_ref[start:stop, :])
        outs = []
        for h in range(2):
            scores = dot_nt(queries[h], k_ref[:stop, :]) + bias[start:stop, :stop]
            top = jnp.max(scores, axis=1, keepdims=True)
            weights = jnp.exp2((scores - top) * exp2_scale)
            total = jnp.sum(weights, axis=1, keepdims=True)
            outs.append(dot_nn(weights.astype(bf16), v_ref[:stop, :]) / total)
            lse = jnp.broadcast_to(top * exp2_scale + jnp.log2(total), (rows, 128))
            lse_ref[0, h : h + 1, start:stop] = jnp.transpose(lse)[0:1, :]
        lane = lax.broadcasted_iota(jnp.int32, (rows, 128), 1)
        o_ref[start:stop, :] = jnp.where(lane < HEAD_DIM, outs[0], outs[1]).astype(bf16)


def attention_forward(qkv, cols, rows):
    tree_len, width = qkv.shape
    pairs = width // 384
    tile = (tree_len, 128)
    return pl.pallas_call(
        attention_forward_kernel,
        name="attention_forward",
        out_shape=(
            jax.ShapeDtypeStruct((tree_len, width // 3), bf16),
            jax.ShapeDtypeStruct((pairs, 8, tree_len), f32),
        ),
        grid=(pairs,),
        in_specs=[
            pl.BlockSpec(tile, lambda p: (0, p)),
            pl.BlockSpec(tile, lambda p: (0, pairs + p)),
            pl.BlockSpec(tile, lambda p: (0, 2 * pairs + p)),
            pl.BlockSpec(cols.shape, lambda p: (0, 0)),
            pl.BlockSpec(rows.shape, lambda p: (0, 0)),
        ],
        out_specs=(
            pl.BlockSpec(tile, lambda p: (0, p)),
            pl.BlockSpec((1, 8, tree_len), lambda p: (p, 0, 0)),
        ),
        scratch_shapes=[pltpu.VMEM((tree_len, tree_len), f32)],
        compiler_params=pltpu.CompilerParams(vmem_limit_bytes=40 << 20),
        cost_estimate=pl.CostEstimate(
            flops=int(0.6 * 2 * pairs * 4 * tree_len * tree_len * 256),
            bytes_accessed=tree_len * width * 3,
            transcendentals=pairs * tree_len * tree_len,
        ),
    )(qkv, qkv, qkv, cols, rows)


def attention_backward_kernel(
    q_ref, k_ref, v_ref, do_ref, o_ref, lse_ref, col_ref, row_ref, dx_ref, bias, split_k, dk, dv
):
    tree_len = q_ref.shape[0]
    rows = block_rows(tree_len)
    pair = pl.program_id(0)
    pairs = pl.num_programs(0)

    @pl.when(pair == 0)
    def _():
        for start in range(0, tree_len, rows):
            stop = start + rows
            key_seg = col_ref[:stop, 0:1]
            ok = row_ref[0:1, start:stop] == key_seg
            ok = ok | (row_ref[1:2, start:stop] == key_seg)
            ok = ok | (row_ref[2:3, start:stop] == key_seg)
            j = lax.broadcasted_iota(jnp.int32, (stop, rows), 0)
            i = lax.broadcasted_iota(jnp.int32, (stop, rows), 1) + start
            bias[:stop, start:stop] = jnp.where(ok & (j <= i), 0.0, masked_value).astype(f32)

    split_k[0], split_k[1] = split_heads(k_ref[...])
    dk[...] = jnp.zeros_like(dk)
    dv[...] = jnp.zeros_like(dv)
    sub = lax.broadcasted_iota(jnp.int32, (8, 128), 0)
    lane = lax.broadcasted_iota(jnp.int32, (8, 128), 1)
    own = jnp.where(lane // HEAD_DIM == sub, 1.0, 0.0).astype(f32)
    for start in range(0, tree_len, rows):
        stop = start + rows
        queries = split_heads(q_ref[start:stop, :])
        grads = split_heads(do_ref[start:stop, :])
        product = do_ref[start:stop, :].astype(f32) * o_ref[start:stop, :].astype(f32)
        row_dot = lax.dot_general(
            own,
            product,
            (((1,), (1,)), ((), ())),
            precision=lax.Precision.HIGHEST,
            preferred_element_type=f32,
        )
        probs_low = []
        grad_scores = []
        for h in range(2):
            shift = bias[:stop, start:stop] - lse_ref[0, h : h + 1, start:stop]
            probs = jnp.exp2(dot_nt(k_ref[:stop, :], queries[h]) * exp2_scale + shift)
            grad_probs = dot_nt(v_ref[:stop, :], grads[h])
            probs_low.append(probs.astype(bf16))
            grad_scores.append((probs * (grad_probs - row_dot[h : h + 1, :])).astype(bf16))
        dv[:stop, :] += dot_nn(jnp.concatenate(probs_low, 1), jnp.concatenate(grads, 0))
        dk[:stop, :] += dot_nn(jnp.concatenate(grad_scores, 1), jnp.concatenate(queries, 0))
        dq = dot_tn(grad_scores[0], split_k[0, :stop, :])
        dq = dq + dot_tn(grad_scores[1], split_k[1, :stop, :])
        dq = (dq.astype(bf16).astype(f32) * grad_scale).astype(bf16)
        dx_ref[start:stop, pl.ds(pl.multiple_of(pair * 128, 128), 128)] = dq
    dx_ref[:, pl.ds(pl.multiple_of((pairs + pair) * 128, 128), 128)] = (
        dk[...] * grad_scale
    ).astype(bf16)
    dx_ref[:, pl.ds(pl.multiple_of((2 * pairs + pair) * 128, 128), 128)] = dv[...].astype(bf16)


def attention_backward(qkv, grad, out, lse, cols, rows):
    tree_len, width = qkv.shape
    pairs = width // 384
    tile = (tree_len, 128)
    return pl.pallas_call(
        attention_backward_kernel,
        name="attention_backward",
        out_shape=jax.ShapeDtypeStruct((tree_len, width), bf16),
        grid=(pairs,),
        in_specs=[
            pl.BlockSpec(tile, lambda p: (0, p)),
            pl.BlockSpec(tile, lambda p: (0, pairs + p)),
            pl.BlockSpec(tile, lambda p: (0, 2 * pairs + p)),
            pl.BlockSpec(tile, lambda p: (0, p)),
            pl.BlockSpec(tile, lambda p: (0, p)),
            pl.BlockSpec((1, 8, tree_len), lambda p: (p, 0, 0)),
            pl.BlockSpec(cols.shape, lambda p: (0, 0)),
            pl.BlockSpec(rows.shape, lambda p: (0, 0)),
        ],
        out_specs=pl.BlockSpec((tree_len, width), lambda p: (0, 0)),
        scratch_shapes=[
            pltpu.VMEM((tree_len, tree_len), f32),
            pltpu.VMEM((2, tree_len, 128), bf16),
            pltpu.VMEM(tile, f32),
            pltpu.VMEM(tile, f32),
        ],
        compiler_params=pltpu.CompilerParams(vmem_limit_bytes=40 << 20),
        cost_estimate=pl.CostEstimate(
            flops=int(0.6 * 5 * pairs * 4 * tree_len * tree_len * 256),
            bytes_accessed=tree_len * width * 6,
            transcendentals=pairs * tree_len * tree_len,
        ),
    )(qkv, qkv, qkv, grad, out, lse, cols, rows)


def norm_parts(values):
    centered = values - jnp.mean(values, axis=-1, keepdims=True)
    scale = lax.rsqrt(jnp.mean(centered * centered, axis=-1, keepdims=True) + norm_eps)
    return centered * scale, scale


def norm_forward(values, gain, shift):
    return norm_parts(values)[0] * gain + shift


def norm_backward(values, gain, grad):
    xhat, scale = norm_parts(values)
    h = grad * gain
    inner = h - jnp.mean(h, axis=-1, keepdims=True)
    inner = inner - xhat * jnp.mean(h * xhat, axis=-1, keepdims=True)
    return scale * inner, jnp.stack([jnp.sum(grad * xhat, axis=0), jnp.sum(grad, axis=0)])


def gelu_tanh(values):
    return jax.nn.gelu(values, approximate=True)


def pick(pieces, position):
    chosen = pieces[0]
    for number in range(1, len(pieces)):
        chosen = jnp.where(position == number, pieces[number], chosen)
    return chosen


def swap_tp(pieces):
    count = len(pieces)
    here = lax.axis_index("tp")
    arrived = [pick(pieces, here)]
    for step in range(1, count):
        pairs = [(s, (s + step) % count) for s in range(count)]
        sent = pick(pieces, (here + step) % count)
        low = sent.astype(bf16) if sent.dtype == f32 else sent
        arrived.append(lax.ppermute(low, "tp", pairs).astype(sent.dtype))
    return [pick(arrived, (here - s) % count) for s in range(count)]


def sum_everywhere(values):
    for axis in ("tp", "fsdp"):
        count = lax.axis_size(axis)
        if count & (count - 1):
            values = lax.psum(values, axis)
            continue
        step = 1
        while step < count:
            values = values + lax.ppermute(values, axis, [(s, s ^ step) for s in range(count)])
            step *= 2
    return values


def gather_weight(shard):
    return lax.all_gather(shard, ("tp", "fsdp"), axis=0, tiled=True)


def scatter_grad(parts):
    whole = jnp.concatenate([part.astype(bf16) for part in parts], axis=0)
    return lax.psum_scatter(whole, ("tp", "fsdp"), scatter_dimension=0, tiled=True).astype(f32)


def segment_tables(segments, parents):
    labels = jnp.arange(parents.shape[0], dtype=jnp.int32)
    up = lambda seg: jnp.sum(jnp.where(seg[:, None] == labels, parents, 0), axis=1)
    parent = up(segments)
    table = jnp.stack([segments, parent, up(parent)])
    return jnp.pad(table.T, ((0, 0), (0, 5))), jnp.pad(table, ((0, 5), (0, 0)))


def on_device(
    tokens, segments, parents, norm_gains, norm_biases, w_qkv, w_out, w_up, w_down, cotangent
):
    tp = lax.axis_size("tp")
    here = lax.axis_index("tp")
    micro = tokens.shape[0]
    own_rows = tokens.shape[2]
    width = tokens.shape[3]
    tree_len = own_rows * tp
    head_width = w_out.shape[0]
    whole = micro // tp
    shared = list(range(whole * tp, micro))
    halves = range(tp)

    def tree_rows(values):
        rows = []
        for n in range(whole):
            rows += swap_tp([values[n * tp + s, 0] for s in halves])
        return rows, [values[m, 0] for m in shared]

    def rows_back(values):
        back = [None] * micro
        for n in range(whole):
            tree = values[n * tree_len : (n + 1) * tree_len]
            parts = swap_tp([tree[s * own_rows : (s + 1) * own_rows] for s in halves])
            for s in halves:
                back[n * tp + s] = parts[s]
        for number, m in enumerate(shared):
            start = whole * tree_len + number * own_rows
            back[m] = values[start : start + own_rows]
        return back

    weight = lambda gathered: [gathered[t * width : (t + 1) * width] for t in halves]
    full_qkv = weight(gather_weight(w_qkv.reshape(w_qkv.shape[0], -1)))
    full_out = weight(gather_weight(w_out.T))
    full_up = weight(gather_weight(w_up))
    full_down = weight(gather_weight(w_down.T))

    seg_all = jnp.concatenate(swap_tp([segments[:, 0]] * tp), axis=1)
    whole_tokens, share_tokens = tree_rows(tokens)
    whole_cot, share_cot = tree_rows(cotangent)
    whole_tables = []
    for n in range(whole):
        seg = pick([seg_all[n * tp + s] for s in halves], here)
        par = pick([parents[n * tp + s, 0] for s in halves], here)
        whole_tables.append(segment_tables(seg, par))
    share_tables = [segment_tables(seg_all[m], parents[m, 0]) for m in shared]

    share_count = len(shared)
    x = jnp.concatenate(whole_tokens + share_tokens, axis=0).astype(f32)
    split = whole * tree_len

    normed = norm_forward(x, norm_gains[0], norm_biases[0]).astype(bf16)
    share_qkv = [dot_nn(normed[split:], w).astype(bf16) for w in full_qkv]
    whole_qkv = [dot_nn(normed[:split], w).astype(bf16) for w in full_qkv] if whole else []
    share_calls = []
    for n in range(share_count):
        cut = slice(n * own_rows, (n + 1) * own_rows)
        share_calls.append(jnp.concatenate(swap_tp([part[cut] for part in share_qkv]), axis=0))
    whole_out = [[] for _ in halves]
    saved = {}
    for n in range(whole):
        for t in halves:
            qkv = whole_qkv[t][n * tree_len : (n + 1) * tree_len]
            out, lse = attention_forward(qkv, *whole_tables[n])
            saved[n, t] = (qkv, out, lse)
            whole_out[t].append(out)
    share_out = [[] for _ in halves]
    for n in range(share_count):
        out, lse = attention_forward(share_calls[n], *share_tables[n])
        saved[n] = (share_calls[n], out, lse)
        parts = swap_tp([out[s * own_rows : (s + 1) * own_rows] for s in halves])
        for t in halves:
            share_out[t].append(parts[t])
    attended = [jnp.concatenate(whole_out[t] + share_out[t], axis=0) for t in halves]
    branch_a = sum(dot_nt(attended[t], full_out[t]) for t in halves)
    residual = x + norm_forward(branch_a, norm_gains[1], norm_biases[1])

    normed_f = norm_forward(residual, norm_gains[2], norm_biases[2]).astype(bf16)
    up_low = []
    hidden = []
    for t in halves:
        up = dot_nn(normed_f, full_up[t])
        hidden.append(gelu_tanh(up).astype(bf16))
        up_low.append(up.astype(bf16))
    branch_f = sum(dot_nt(hidden[t], full_down[t]) for t in halves)
    out = (residual + norm_forward(branch_f, norm_gains[3], norm_biases[3])).astype(bf16)
    out_rows = jnp.stack(rows_back(out))[:, None]

    grad_out = jnp.concatenate(whole_cot + share_cot, axis=0).astype(f32)
    grad_branch_f, sums_3 = norm_backward(branch_f, norm_gains[3], grad_out)
    grad_branch_f = grad_branch_f.astype(bf16)
    grad_down = scatter_grad([dot_tn(grad_branch_f, hidden[t]) for t in halves])
    grad_up = []
    for t in halves:
        pull = jax.vjp(gelu_tanh, up_low[t].astype(f32))[1]
        grad_up.append(pull(dot_nn(grad_branch_f, full_down[t]))[0].astype(bf16))
    grad_w_up = scatter_grad([dot_tn(normed_f, grad_up[t]) for t in halves])
    grad_normed_f = sum(dot_nt(grad_up[t], full_up[t]) for t in halves)
    grad_part, sums_2 = norm_backward(residual, norm_gains[2], grad_normed_f)
    grad_residual = grad_out + grad_part

    grad_branch_a, sums_1 = norm_backward(branch_a, norm_gains[1], grad_residual)
    grad_branch_a = grad_branch_a.astype(bf16)
    share_grad = [dot_nn(grad_branch_a[split:], w).astype(bf16) for w in full_out]
    share_do = []
    for n in range(share_count):
        cut = slice(n * own_rows, (n + 1) * own_rows)
        share_do.append(jnp.concatenate(swap_tp([part[cut] for part in share_grad]), axis=0))
    grad_w_out = scatter_grad([dot_tn(grad_branch_a, attended[t]) for t in halves])
    whole_grad = [dot_nn(grad_branch_a[:split], w).astype(bf16) for w in full_out] if whole else []
    grad_qkv = [[] for _ in halves]
    share_parts = [[] for _ in halves]
    for n in range(share_count):
        qkv, att, lse = saved[n]
        dx = attention_backward(qkv, share_do[n], att, lse, *share_tables[n])
        parts = swap_tp([dx[s * own_rows : (s + 1) * own_rows] for s in halves])
        for t in halves:
            share_parts[t].append(parts[t])
    for n in range(whole):
        for t in halves:
            qkv, att, lse = saved[n, t]
            do = whole_grad[t][n * tree_len : (n + 1) * tree_len]
            grad_qkv[t].append(attention_backward(qkv, do, att, lse, *whole_tables[n]))
    grad_qkv = [jnp.concatenate(grad_qkv[t] + share_parts[t], axis=0) for t in halves]
    grad_w_qkv = scatter_grad([dot_tn(normed, grad_qkv[t]) for t in halves])
    grad_normed = sum(dot_nt(grad_qkv[t], full_qkv[t]) for t in halves)
    grad_part, sums_0 = norm_backward(x, norm_gains[0], grad_normed)
    grad_x = grad_residual + grad_part
    input_rows = jnp.stack(rows_back(grad_x))[:, None]
    early = sum_everywhere(jnp.stack([sums_1, sums_2, sums_3]))
    late = sum_everywhere(sums_0[None])
    sums = jnp.concatenate([late, early], axis=0)
    return (
        out_rows,
        input_rows,
        grad_w_qkv.reshape(w_qkv.shape),
        grad_w_out.T,
        grad_w_up,
        grad_down.T,
        sums[:, 0],
        sums[:, 1],
    )


def solution(mesh):
    in_specs = (
        P(None, "fsdp", "tp", None),
        P(None, "fsdp", "tp"),
        P(None, "fsdp", None),
        P(),
        P(),
        P("fsdp", None, "tp"),
        P("tp", "fsdp"),
        P("fsdp", "tp"),
        P("tp", "fsdp"),
        P(None, "fsdp", "tp", None),
    )
    out_specs = (
        P(None, "fsdp", "tp", None),
        P(None, "fsdp", "tp", None),
        P("fsdp", None, "tp"),
        P("tp", "fsdp"),
        P("fsdp", "tp"),
        P("tp", "fsdp"),
        P(),
        P(),
    )
    return jax.shard_map(
        on_device, mesh=mesh, in_specs=in_specs, out_specs=out_specs, check_vma=False
    )
```

```python
import math

import jax
import jax.numpy as jnp
from jax import lax
from jax.experimental import pallas as pl
from jax.experimental.pallas import tpu as pltpu
from jax.sharding import PartitionSpec as P

HEAD_DIM = 64
norm_eps = 1e-05
masked_value = -1e30
f32 = jnp.float32
bf16 = jnp.bfloat16
exp2_scale = math.log2(math.e) / math.sqrt(HEAD_DIM)
grad_scale = 1.0 / math.sqrt(HEAD_DIM)


def dot_nn(a, b):
    return lax.dot_general(a, b, (((1,), (0,)), ((), ())), preferred_element_type=f32)


def dot_nt(a, b):
    return lax.dot_general(a, b, (((1,), (1,)), ((), ())), preferred_element_type=f32)


def dot_tn(a, b):
    return lax.dot_general(a, b, (((0,), (0,)), ((), ())), preferred_element_type=f32)


def split_heads(x):
    lane = lax.broadcasted_iota(jnp.int32, x.shape, 1)
    zero = jnp.zeros_like(x)
    return jnp.where(lane < HEAD_DIM, x, zero), jnp.where(lane >= HEAD_DIM, x, zero)


def block_rows(tree_len):
    return 256 if tree_len % 256 == 0 else 128


def attention_forward_kernel(q_ref, k_ref, v_ref, col_ref, row_ref, o_ref, lse_ref, bias):
    tree_len = q_ref.shape[0]
    rows = block_rows(tree_len)

    @pl.when(pl.program_id(0) == 0)
    def _():
        for start in range(0, tree_len, rows):
            stop = start + rows
            key_seg = row_ref[0:1, :stop]
            ok = col_ref[start:stop, 0:1] == key_seg
            ok = ok | (col_ref[start:stop, 1:2] == key_seg)
            ok = ok | (col_ref[start:stop, 2:3] == key_seg)
            i = lax.broadcasted_iota(jnp.int32, (rows, stop), 0) + start
            j = lax.broadcasted_iota(jnp.int32, (rows, stop), 1)
            bias[start:stop, :stop] = jnp.where(ok & (j <= i), 0.0, masked_value).astype(f32)

    for start in range(0, tree_len, rows):
        stop = start + rows
        queries = split_heads(q_ref[start:stop, :])
        outs = []
        for h in range(2):
            scores = dot_nt(queries[h], k_ref[:stop, :]) + bias[start:stop, :stop]
            top = jnp.max(scores, axis=1, keepdims=True)
            weights = jnp.exp2((scores - top) * exp2_scale)
            total = jnp.sum(weights, axis=1, keepdims=True)
            outs.append(dot_nn(weights.astype(bf16), v_ref[:stop, :]) / total)
            lse = jnp.broadcast_to(top * exp2_scale + jnp.log2(total), (rows, 128))
            lse_ref[0, h : h + 1, start:stop] = jnp.transpose(lse)[0:1, :]
        lane = lax.broadcasted_iota(jnp.int32, (rows, 128), 1)
        o_ref[start:stop, :] = jnp.where(lane < HEAD_DIM, outs[0], outs[1]).astype(bf16)


def attention_forward(qkv, cols, rows):
    tree_len, width = qkv.shape
    pairs = width // 384
    tile = (tree_len, 128)
    return pl.pallas_call(
        attention_forward_kernel,
        name="attention_forward",
        out_shape=(
            jax.ShapeDtypeStruct((tree_len, width // 3), bf16),
            jax.ShapeDtypeStruct((pairs, 8, tree_len), f32),
        ),
        grid=(pairs,),
        in_specs=[
            pl.BlockSpec(tile, lambda p: (0, p)),
            pl.BlockSpec(tile, lambda p: (0, pairs + p)),
            pl.BlockSpec(tile, lambda p: (0, 2 * pairs + p)),
            pl.BlockSpec(cols.shape, lambda p: (0, 0)),
            pl.BlockSpec(rows.shape, lambda p: (0, 0)),
        ],
        out_specs=(
            pl.BlockSpec(tile, lambda p: (0, p)),
            pl.BlockSpec((1, 8, tree_len), lambda p: (p, 0, 0)),
        ),
        scratch_shapes=[pltpu.VMEM((tree_len, tree_len), f32)],
        compiler_params=pltpu.CompilerParams(vmem_limit_bytes=40 << 20),
        cost_estimate=pl.CostEstimate(
            flops=int(0.6 * 2 * pairs * 4 * tree_len * tree_len * 256),
            bytes_accessed=tree_len * width * 3,
            transcendentals=pairs * tree_len * tree_len,
        ),
    )(qkv, qkv, qkv, cols, rows)


def attention_backward_kernel(
    q_ref, k_ref, v_ref, do_ref, o_ref, lse_ref, col_ref, row_ref, dx_ref, bias, split_k, dk, dv
):
    tree_len = q_ref.shape[0]
    rows = block_rows(tree_len)
    pair = pl.program_id(0)
    pairs = pl.num_programs(0)

    @pl.when(pair == 0)
    def _():
        for start in range(0, tree_len, rows):
            stop = start + rows
            key_seg = col_ref[:stop, 0:1]
            ok = row_ref[0:1, start:stop] == key_seg
            ok = ok | (row_ref[1:2, start:stop] == key_seg)
            ok = ok | (row_ref[2:3, start:stop] == key_seg)
            j = lax.broadcasted_iota(jnp.int32, (stop, rows), 0)
            i = lax.broadcasted_iota(jnp.int32, (stop, rows), 1) + start
            bias[:stop, start:stop] = jnp.where(ok & (j <= i), 0.0, masked_value).astype(f32)

    split_k[0], split_k[1] = split_heads(k_ref[...])
    dk[...] = jnp.zeros_like(dk)
    dv[...] = jnp.zeros_like(dv)
    sub = lax.broadcasted_iota(jnp.int32, (8, 128), 0)
    lane = lax.broadcasted_iota(jnp.int32, (8, 128), 1)
    own = jnp.where(lane // HEAD_DIM == sub, 1.0, 0.0).astype(f32)
    for start in range(0, tree_len, rows):
        stop = start + rows
        queries = split_heads(q_ref[start:stop, :])
        grads = split_heads(do_ref[start:stop, :])
        product = do_ref[start:stop, :].astype(f32) * o_ref[start:stop, :].astype(f32)
        row_dot = lax.dot_general(
            own,
            product,
            (((1,), (1,)), ((), ())),
            precision=lax.Precision.HIGHEST,
            preferred_element_type=f32,
        )
        probs_low = []
        grad_scores = []
        for h in range(2):
            shift = bias[:stop, start:stop] - lse_ref[0, h : h + 1, start:stop]
            probs = jnp.exp2(dot_nt(k_ref[:stop, :], queries[h]) * exp2_scale + shift)
            grad_probs = dot_nt(v_ref[:stop, :], grads[h])
            probs_low.append(probs.astype(bf16))
            grad_scores.append((probs * (grad_probs - row_dot[h : h + 1, :])).astype(bf16))
        dv[:stop, :] += dot_nn(jnp.concatenate(probs_low, 1), jnp.concatenate(grads, 0))
        dk[:stop, :] += dot_nn(jnp.concatenate(grad_scores, 1), jnp.concatenate(queries, 0))
        dq = dot_tn(grad_scores[0], split_k[0, :stop, :])
        dq = dq + dot_tn(grad_scores[1], split_k[1, :stop, :])
        dq = (dq.astype(bf16).astype(f32) * grad_scale).astype(bf16)
        dx_ref[start:stop, pl.ds(pl.multiple_of(pair * 128, 128), 128)] = dq
    dx_ref[:, pl.ds(pl.multiple_of((pairs + pair) * 128, 128), 128)] = (
        dk[...] * grad_scale
    ).astype(bf16)
    dx_ref[:, pl.ds(pl.multiple_of((2 * pairs + pair) * 128, 128), 128)] = dv[...].astype(bf16)


def attention_backward(qkv, grad, out, lse, cols, rows):
    tree_len, width = qkv.shape
    pairs = width // 384
    tile = (tree_len, 128)
    return pl.pallas_call(
        attention_backward_kernel,
        name="attention_backward",
        out_shape=jax.ShapeDtypeStruct((tree_len, width), bf16),
        grid=(pairs,),
        in_specs=[
            pl.BlockSpec(tile, lambda p: (0, p)),
            pl.BlockSpec(tile, lambda p: (0, pairs + p)),
            pl.BlockSpec(tile, lambda p: (0, 2 * pairs + p)),
            pl.BlockSpec(tile, lambda p: (0, p)),
            pl.BlockSpec(tile, lambda p: (0, p)),
            pl.BlockSpec((1, 8, tree_len), lambda p: (p, 0, 0)),
            pl.BlockSpec(cols.shape, lambda p: (0, 0)),
            pl.BlockSpec(rows.shape, lambda p: (0, 0)),
        ],
        out_specs=pl.BlockSpec((tree_len, width), lambda p: (0, 0)),
        scratch_shapes=[
            pltpu.VMEM((tree_len, tree_len), f32),
            pltpu.VMEM((2, tree_len, 128), bf16),
            pltpu.VMEM(tile, f32),
            pltpu.VMEM(tile, f32),
        ],
        compiler_params=pltpu.CompilerParams(vmem_limit_bytes=40 << 20),
        cost_estimate=pl.CostEstimate(
            flops=int(0.6 * 5 * pairs * 4 * tree_len * tree_len * 256),
            bytes_accessed=tree_len * width * 6,
            transcendentals=pairs * tree_len * tree_len,
        ),
    )(qkv, qkv, qkv, grad, out, lse, cols, rows)


def norm_parts(values):
    centered = values - jnp.mean(values, axis=-1, keepdims=True)
    scale = lax.rsqrt(jnp.mean(centered * centered, axis=-1, keepdims=True) + norm_eps)
    return centered * scale, scale


def norm_forward(values, gain, shift):
    return norm_parts(values)[0] * gain + shift


def norm_backward(values, gain, grad):
    xhat, scale = norm_parts(values)
    h = grad * gain
    inner = h - jnp.mean(h, axis=-1, keepdims=True)
    inner = inner - xhat * jnp.mean(h * xhat, axis=-1, keepdims=True)
    return scale * inner, jnp.stack([jnp.sum(grad * xhat, axis=0), jnp.sum(grad, axis=0)])


def gelu_tanh(values):
    return jax.nn.gelu(values, approximate=True)


def width_orders():
    count = lax.axis_size("z")
    z, y, core = (lax.axis_index(name) for name in ("z", "y", "core"))
    place = jnp.arange(4 * count, dtype=jnp.int32)
    inward = ((z ^ (place % count)) * 2 + (y ^ (place // count % 2))) * 2
    inward = inward + (core ^ (place // (2 * count)))
    outward = ((core ^ (place % 2)) * 2 + (y ^ (place // 2 % 2))) * count
    outward = outward + (z ^ (place // 4))
    return inward, outward


def arrange_small(values, source):
    blocks = values.reshape(values.shape[0], 1, source.shape[0], -1)
    hit = source[:, None] == jnp.arange(source.shape[0], dtype=jnp.int32)
    return jnp.sum(jnp.where(hit[None, :, :, None], blocks, 0.0), axis=2).reshape(values.shape)


def arrange_kernel(source, first_at, second_at, use_second, first_ref, second_ref, out_ref):
    rows, width = out_ref.shape
    block = width // source.shape[0]
    per = 128 // block
    lane = lax.broadcasted_iota(jnp.int32, (rows, 128), 1)

    def fill(ref):
        for tile in range(width // 128):
            made = None
            for part in range(per):
                at = source[tile * per + part]
                start = pl.multiple_of(lax.div(at, per) * 128, 128)
                values = ref[:, pl.ds(start, 128)].astype(f32)
                turn = lax.rem(part - lax.rem(at, per) + per, per) * block
                values = pltpu.roll(values, turn, 1)
                made = values if part == 0 else jnp.where(lane >= part * block, values, made)
            out_ref[:, tile * 128 : (tile + 1) * 128] = made.astype(out_ref.dtype)

    second = use_second[pl.program_id(0)]

    @pl.when(second == 0)
    def _():
        fill(first_ref)

    @pl.when(second != 0)
    def _():
        fill(second_ref)


def arrange(first, second, source, plan, rows, out_type):
    width = first.shape[1]
    first_at, second_at, use_second = (jnp.stack(list(column)).astype(jnp.int32) for column in zip(*plan))
    return pl.pallas_call(
        arrange_kernel,
        name="arrange",
        out_shape=jax.ShapeDtypeStruct((len(plan) * rows, width), out_type),
        grid_spec=pltpu.PrefetchScalarGridSpec(
            num_scalar_prefetch=4,
            grid=(len(plan),),
            in_specs=[
                pl.BlockSpec((rows, width), lambda i, s, a, b, u: (a[i], 0)),
                pl.BlockSpec((rows, width), lambda i, s, a, b, u: (b[i], 0)),
            ],
            out_specs=pl.BlockSpec((rows, width), lambda i, s, a, b, u: (i, 0)),
        ),
        cost_estimate=pl.CostEstimate(
            flops=len(plan) * rows * width * 8,
            bytes_accessed=len(plan) * rows * width * 8,
            transcendentals=0,
        ),
    )(source, first_at, second_at, use_second, first, second)


def send(values, axes, distance):
    count = 1
    for axis in (axes,) if isinstance(axes, str) else axes:
        count *= lax.axis_size(axis)
    return lax.ppermute(values, axes, [(s, s ^ distance) for s in range(count)])


def after(values, *others):
    return lax.optimization_barrier((values,) + others)[0]


def pick(pieces, position):
    chosen = pieces[0]
    for number in range(1, len(pieces)):
        chosen = jnp.where(position == number, pieces[number], chosen)
    return chosen


def exchange_tp(pieces):
    return pieces[:1] + [send(pieces[k], "tp", k) for k in range(1, len(pieces))]


def in_place_order(pieces):
    here = lax.axis_index("tp")
    return jnp.concatenate([pick(pieces, here ^ s) for s in range(len(pieces))], axis=0)


def sum_everywhere(values):
    for axes in (("y", "tp"), ("z",), ("core",)):
        count = 1
        for axis in axes:
            count *= lax.axis_size(axis)
        values = sum([send(values, axes, k) for k in range(1, count)], values)
    return values


def gather_z(shard):
    count = lax.axis_size("z")
    return jnp.concatenate([shard] + [send(shard, "z", k) for k in range(1, count)], axis=0)


def gather_plane(block):
    count = lax.axis_size("tp")
    places = [(k // 2, k % 2) for k in range(1, 2 * count)]
    return [block] + [send(block, ("y", "tp"), y * count + t) for t, y in places]


def gather_core(blocks):
    other = [send(block, "core", 1) for block in blocks]
    halves = range(len(blocks) // 2)
    pair = lambda pieces, t: pieces[2 * t : 2 * t + 2]
    return [jnp.concatenate(pair(blocks, t) + pair(other, t), axis=0) for t in halves]


def scatter_core(part):
    half = part.shape[0] // 2
    came = send(part[half:], "core", 1)
    return (part[:half].astype(f32) + came.astype(f32)).astype(bf16)


def scatter_plane(parts):
    half = parts[0].shape[0] // 2
    total = parts[0][:half].astype(f32)
    for k in range(2 * len(parts) - 1, 0, -1):
        piece = parts[k // 2][k % 2 * half : (k % 2 + 1) * half]
        total = total + send(piece, ("y", "tp"), k % 2 * len(parts) + k // 2).astype(f32)
    return total.astype(bf16)


def scatter_z(part):
    count = lax.axis_size("z")
    rows = part.shape[0] // count
    total = part[:rows].astype(f32)
    for k in range(1, count):
        total = total + send(part[k * rows : (k + 1) * rows], "z", k).astype(f32)
    return total


def scatter_grad(parts):
    return scatter_z(scatter_plane([scatter_core(part.astype(bf16)) for part in parts]))


def segment_tables(segments, parents):
    labels = jnp.arange(parents.shape[0], dtype=jnp.int32)
    up = lambda seg: jnp.sum(jnp.where(seg[:, None] == labels, parents, 0), axis=1)
    parent = up(segments)
    table = jnp.stack([segments, parent, up(parent)])
    return jnp.pad(table.T, ((0, 0), (0, 5))), jnp.pad(table, ((0, 5), (0, 0)))


def on_device(
    tokens, segments, parents, norm_gains, norm_biases, w_qkv, w_out, w_up, w_down, cotangent
):
    tp = lax.axis_size("tp")
    here = lax.axis_index("tp")
    micro = tokens.shape[0]
    own_rows = tokens.shape[2]
    width = tokens.shape[3]
    tree_len = own_rows * tp
    whole = micro // tp
    shared = list(range(whole * tp, micro))
    share_count = len(shared)
    halves = range(tp)
    inward, outward = width_orders()
    split = whole * tree_len

    zero = jnp.int32(0)
    in_plan = []
    for n in range(whole):
        for s in halves:
            far = here ^ s
            in_plan.append((n * tp + here, n * (tp - 1) + jnp.maximum(far - 1, 0), far != 0))
    in_plan += [(zero + m, zero, zero != 0) for m in shared]
    out_plan = []
    for n in range(whole):
        for s in halves:
            far = here ^ s
            out_plan.append((n * tp + here, n * (tp - 1) + jnp.maximum(far - 1, 0), far != 0))
    out_plan += [(zero + m, zero, zero != 0) for m in shared]

    def tree_rows(values):
        flat = values.reshape(micro * own_rows, width)
        came = []
        for n in range(whole):
            for k in range(1, tp):
                start = (n * tp + (here ^ k)) * own_rows
                came.append(send(lax.dynamic_slice_in_dim(flat, start, own_rows), "tp", k))
        came = jnp.concatenate(came, axis=0) if came else flat
        return arrange(flat, came, inward, in_plan, own_rows, bf16)

    def rows_back(values, out_type):
        came = []
        for n in range(whole):
            for k in range(1, tp):
                start = (n * tp + (here ^ k)) * own_rows
                piece = lax.dynamic_slice_in_dim(values, start, own_rows).astype(bf16)
                came.append(send(piece, "tp", k))
        came = jnp.concatenate(came, axis=0) if came else values
        back = arrange(values, came, outward, out_plan, own_rows, out_type)
        return back.reshape(micro, 1, own_rows, width)

    qkv_z = gather_z(w_qkv.reshape(w_qkv.shape[0], -1))
    qkv_plane = gather_plane(qkv_z)
    full_qkv = gather_core(qkv_plane)
    out_z = gather_z(after(w_out.T, qkv_z))
    up_z = gather_z(after(w_up, qkv_z))
    out_plane = gather_plane(after(out_z, qkv_plane[1]))
    up_plane = gather_plane(after(up_z, qkv_plane[1]))
    down_z = gather_z(after(w_down.T, qkv_plane[1]))
    full_out = gather_core(out_plane)
    full_up = gather_core(up_plane)
    full_down = gather_core(gather_plane(after(down_z, up_plane[1])))

    seg_came = exchange_tp([segments[:, 0]] * tp)
    seg_all = jnp.concatenate([pick(seg_came, here ^ s) for s in halves], axis=1)
    gains = arrange_small(norm_gains, inward)
    biases = arrange_small(norm_biases, inward)
    x = tree_rows(tokens).astype(f32)
    whole_tables = []
    for n in range(whole):
        seg = pick([seg_all[n * tp + s] for s in halves], here)
        par = pick([parents[n * tp + s, 0] for s in halves], here)
        whole_tables.append(segment_tables(seg, par))
    share_tables = [segment_tables(seg_all[m], parents[m, 0]) for m in shared]

    def share_rows(values, k):
        return lax.dynamic_slice_in_dim(values, (here ^ k) * own_rows, own_rows)

    normed = norm_forward(x, gains[0], biases[0]).astype(bf16)
    share_qkv = [dot_nn(normed[split:], w).astype(bf16) for w in full_qkv]
    whole_qkv = [dot_nn(normed[:split], w).astype(bf16) for w in full_qkv] if whole else []
    share_calls = []
    for n in range(share_count):
        cut = slice(n * own_rows, (n + 1) * own_rows)
        share_calls.append(in_place_order(exchange_tp([part[cut] for part in share_qkv])))
    whole_out = [[] for _ in halves]
    saved = {}
    for n in range(whole):
        for t in halves:
            qkv = whole_qkv[t][n * tree_len : (n + 1) * tree_len]
            out, lse = attention_forward(qkv, *whole_tables[n])
            saved[n, t] = (qkv, out, lse)
            whole_out[t].append(out)
    share_out = [[] for _ in halves]
    for n in range(share_count):
        out, lse = attention_forward(share_calls[n], *share_tables[n])
        saved[n] = (share_calls[n], out, lse)
        parts = exchange_tp([share_rows(out, k) for k in halves])
        for t in halves:
            share_out[t].append(parts[t])
    attended = [jnp.concatenate(whole_out[t] + share_out[t], axis=0) for t in halves]
    branch_a = sum(dot_nt(attended[t], full_out[t]) for t in halves)
    residual = x + norm_forward(branch_a, gains[1], biases[1])

    normed_f = norm_forward(residual, gains[2], biases[2]).astype(bf16)
    up_low = []
    hidden = []
    for t in halves:
        up = dot_nn(normed_f, full_up[t])
        hidden.append(gelu_tanh(up).astype(bf16))
        up_low.append(up.astype(bf16))
    branch_f = sum(dot_nt(hidden[t], full_down[t]) for t in halves)
    out = (residual + norm_forward(branch_f, gains[3], biases[3])).astype(bf16)
    out_rows = rows_back(out, bf16)

    grad_out = tree_rows(after(cotangent, full_qkv[0])).astype(f32)
    grad_branch_f, sums_3 = norm_backward(branch_f, gains[3], grad_out)
    grad_branch_f = grad_branch_f.astype(bf16)
    grad_down = scatter_grad([dot_tn(grad_branch_f, hidden[t]) for t in halves])
    grad_up = []
    for t in halves:
        pull = jax.vjp(gelu_tanh, up_low[t].astype(f32))[1]
        grad_up.append(pull(dot_nn(grad_branch_f, full_down[t]))[0].astype(bf16))
    grad_w_up = scatter_grad([dot_tn(normed_f, grad_up[t]) for t in halves])
    grad_normed_f = sum(dot_nt(grad_up[t], full_up[t]) for t in halves)
    grad_part, sums_2 = norm_backward(residual, gains[2], grad_normed_f)
    grad_residual = grad_out + grad_part

    grad_branch_a, sums_1 = norm_backward(branch_a, gains[1], grad_residual)
    grad_branch_a = grad_branch_a.astype(bf16)
    share_grad = [dot_nn(grad_branch_a[split:], w).astype(bf16) for w in full_out]
    share_do = []
    for n in range(share_count):
        cut = slice(n * own_rows, (n + 1) * own_rows)
        share_do.append(in_place_order(exchange_tp([part[cut] for part in share_grad])))
    grad_w_out = scatter_grad([dot_tn(grad_branch_a, attended[t]) for t in halves])
    whole_grad = [dot_nn(grad_branch_a[:split], w).astype(bf16) for w in full_out] if whole else []
    grad_qkv = [[] for _ in halves]
    share_parts = [[] for _ in halves]
    for n in range(share_count):
        qkv, att, lse = saved[n]
        dx = attention_backward(qkv, share_do[n], att, lse, *share_tables[n])
        parts = exchange_tp([share_rows(dx, k) for k in halves])
        for t in halves:
            share_parts[t].append(parts[t])
    for n in range(whole):
        for t in halves:
            qkv, att, lse = saved[n, t]
            do = whole_grad[t][n * tree_len : (n + 1) * tree_len]
            grad_qkv[t].append(attention_backward(qkv, do, att, lse, *whole_tables[n]))
    grad_qkv = [jnp.concatenate(grad_qkv[t] + share_parts[t], axis=0) for t in halves]
    grad_w_qkv = scatter_grad([dot_tn(normed, grad_qkv[t]) for t in halves])
    grad_normed = sum(dot_nt(grad_qkv[t], full_qkv[t]) for t in halves)
    grad_part, sums_0 = norm_backward(x, gains[0], grad_normed)
    input_rows = rows_back(grad_residual + grad_part, f32)
    early = sum_everywhere(arrange_small(jnp.concatenate([sums_1, sums_2, sums_3]), outward))
    late = sum_everywhere(arrange_small(sums_0, outward))
    sums = jnp.concatenate([late, early], axis=0).reshape(4, 2, width)
    return (
        out_rows,
        input_rows,
        grad_w_qkv.reshape(w_qkv.shape),
        grad_w_out.T,
        grad_w_up,
        grad_down.T,
        sums[:, 0],
        sums[:, 1],
    )


def solution(mesh):
    groups, tp = mesh.devices.shape
    fine = jax.sharding.Mesh(mesh.devices.reshape(groups // 4, 2, 2, tp), ("z", "y", "core", "tp"))
    fsdp = ("z", "y", "core")
    in_specs = (
        P(None, fsdp, "tp", None),
        P(None, fsdp, "tp"),
        P(None, fsdp, None),
        P(),
        P(),
        P(fsdp, None, "tp"),
        P("tp", fsdp),
        P(fsdp, "tp"),
        P("tp", fsdp),
        P(None, fsdp, "tp", None),
    )
    out_specs = (
        P(None, fsdp, "tp", None),
        P(None, fsdp, "tp", None),
        P(fsdp, None, "tp"),
        P("tp", fsdp),
        P(fsdp, "tp"),
        P("tp", fsdp),
        P(),
        P(),
    )
    return jax.shard_map(
        on_device, mesh=fine, in_specs=in_specs, out_specs=out_specs, check_vma=False
    )
```

```python
import functools
import math

import jax
import jax.numpy as jnp
from jax import lax
from jax.experimental import pallas as pl
from jax.experimental.pallas import tpu as pltpu
from jax.sharding import PartitionSpec as P

HEAD_DIM = 64
norm_eps = 1e-05
masked_value = -1e30
f32 = jnp.float32
bf16 = jnp.bfloat16
exp2_scale = math.log2(math.e) / math.sqrt(HEAD_DIM)
grad_scale = 1.0 / math.sqrt(HEAD_DIM)
gelu_scale = math.sqrt(2.0 / math.pi)
gelu_cubic = 0.044715


def dot_nn(a, b):
    return lax.dot_general(a, b, (((1,), (0,)), ((), ())), preferred_element_type=f32)


def dot_nt(a, b):
    return lax.dot_general(a, b, (((1,), (1,)), ((), ())), preferred_element_type=f32)


def dot_tn(a, b):
    return lax.dot_general(a, b, (((0,), (0,)), ((), ())), preferred_element_type=f32)


def split_heads(x):
    lane = lax.broadcasted_iota(jnp.int32, x.shape, 1)
    zero = jnp.zeros_like(x)
    return jnp.where(lane < HEAD_DIM, x, zero), jnp.where(lane >= HEAD_DIM, x, zero)


def block_rows(tree_len):
    return 256 if tree_len % 256 == 0 else 128


def attention_forward_kernel(q_ref, k_ref, v_ref, col_ref, row_ref, o_ref, lse_ref, bias):
    tree_len = q_ref.shape[0]
    rows = block_rows(tree_len)

    @pl.when(pl.program_id(0) == 0)
    def _():
        for start in range(0, tree_len, rows):
            stop = start + rows
            key_seg = row_ref[0:1, :stop]
            ok = col_ref[start:stop, 0:1] == key_seg
            ok = ok | (col_ref[start:stop, 1:2] == key_seg)
            ok = ok | (col_ref[start:stop, 2:3] == key_seg)
            i = lax.broadcasted_iota(jnp.int32, (rows, stop), 0) + start
            j = lax.broadcasted_iota(jnp.int32, (rows, stop), 1)
            bias[start:stop, :stop] = jnp.where(ok & (j <= i), 0.0, masked_value).astype(f32)

    for start in range(0, tree_len, rows):
        stop = start + rows
        queries = split_heads(q_ref[start:stop, :])
        outs = []
        for h in range(2):
            scores = dot_nt(queries[h], k_ref[:stop, :]) + bias[start:stop, :stop]
            top = jnp.max(scores, axis=1, keepdims=True)
            weights = jnp.exp2((scores - top) * exp2_scale)
            total = jnp.sum(weights, axis=1, keepdims=True)
            outs.append(dot_nn(weights.astype(bf16), v_ref[:stop, :]) / total)
            lse = jnp.broadcast_to(top * exp2_scale + jnp.log2(total), (rows, 128))
            lse_ref[0, h : h + 1, start:stop] = jnp.transpose(lse)[0:1, :]
        lane = lax.broadcasted_iota(jnp.int32, (rows, 128), 1)
        o_ref[start:stop, :] = jnp.where(lane < HEAD_DIM, outs[0], outs[1]).astype(bf16)


def attention_forward(qkv, cols, rows):
    tree_len, width = qkv.shape
    pairs = width // 384
    tile = (tree_len, 128)
    return pl.pallas_call(
        attention_forward_kernel,
        name="attention_forward",
        out_shape=(
            jax.ShapeDtypeStruct((tree_len, width // 3), bf16),
            jax.ShapeDtypeStruct((pairs, 8, tree_len), f32),
        ),
        grid=(pairs,),
        in_specs=[
            pl.BlockSpec(tile, lambda p: (0, p)),
            pl.BlockSpec(tile, lambda p: (0, pairs + p)),
            pl.BlockSpec(tile, lambda p: (0, 2 * pairs + p)),
            pl.BlockSpec(cols.shape, lambda p: (0, 0)),
            pl.BlockSpec(rows.shape, lambda p: (0, 0)),
        ],
        out_specs=(
            pl.BlockSpec(tile, lambda p: (0, p)),
            pl.BlockSpec((1, 8, tree_len), lambda p: (p, 0, 0)),
        ),
        scratch_shapes=[pltpu.VMEM((tree_len, tree_len), f32)],
        compiler_params=pltpu.CompilerParams(vmem_limit_bytes=40 << 20),
        cost_estimate=pl.CostEstimate(
            flops=int(0.6 * 2 * pairs * 4 * tree_len * tree_len * 256),
            bytes_accessed=tree_len * width * 3,
            transcendentals=pairs * tree_len * tree_len,
        ),
    )(qkv, qkv, qkv, cols, rows)


def attention_backward_kernel(
    q_ref, k_ref, v_ref, do_ref, o_ref, lse_ref, col_ref, row_ref, dx_ref, bias, split_k, dk, dv
):
    tree_len = q_ref.shape[0]
    rows = block_rows(tree_len)
    pair = pl.program_id(0)
    pairs = pl.num_programs(0)

    @pl.when(pair == 0)
    def _():
        for start in range(0, tree_len, rows):
            stop = start + rows
            key_seg = col_ref[:stop, 0:1]
            ok = row_ref[0:1, start:stop] == key_seg
            ok = ok | (row_ref[1:2, start:stop] == key_seg)
            ok = ok | (row_ref[2:3, start:stop] == key_seg)
            j = lax.broadcasted_iota(jnp.int32, (stop, rows), 0)
            i = lax.broadcasted_iota(jnp.int32, (stop, rows), 1) + start
            bias[:stop, start:stop] = jnp.where(ok & (j <= i), 0.0, masked_value).astype(f32)

    split_k[0], split_k[1] = split_heads(k_ref[...])
    dk[...] = jnp.zeros_like(dk)
    dv[...] = jnp.zeros_like(dv)
    sub = lax.broadcasted_iota(jnp.int32, (8, 128), 0)
    lane = lax.broadcasted_iota(jnp.int32, (8, 128), 1)
    own = jnp.where(lane // HEAD_DIM == sub, 1.0, 0.0).astype(f32)
    for start in range(0, tree_len, rows):
        stop = start + rows
        queries = split_heads(q_ref[start:stop, :])
        grads = split_heads(do_ref[start:stop, :])
        product = do_ref[start:stop, :].astype(f32) * o_ref[start:stop, :].astype(f32)
        row_dot = lax.dot_general(
            own,
            product,
            (((1,), (1,)), ((), ())),
            precision=lax.Precision.HIGHEST,
            preferred_element_type=f32,
        )
        probs_low = []
        grad_scores = []
        for h in range(2):
            shift = bias[:stop, start:stop] - lse_ref[0, h : h + 1, start:stop]
            probs = jnp.exp2(dot_nt(k_ref[:stop, :], queries[h]) * exp2_scale + shift)
            grad_probs = dot_nt(v_ref[:stop, :], grads[h])
            probs_low.append(probs.astype(bf16))
            grad_scores.append((probs * (grad_probs - row_dot[h : h + 1, :])).astype(bf16))
        dv[:stop, :] += dot_nn(jnp.concatenate(probs_low, 1), jnp.concatenate(grads, 0))
        dk[:stop, :] += dot_nn(jnp.concatenate(grad_scores, 1), jnp.concatenate(queries, 0))
        dq = dot_tn(grad_scores[0], split_k[0, :stop, :])
        dq = dq + dot_tn(grad_scores[1], split_k[1, :stop, :])
        dq = (dq.astype(bf16).astype(f32) * grad_scale).astype(bf16)
        dx_ref[start:stop, pl.ds(pl.multiple_of(pair * 128, 128), 128)] = dq
    dx_ref[:, pl.ds(pl.multiple_of((pairs + pair) * 128, 128), 128)] = (
        dk[...] * grad_scale
    ).astype(bf16)
    dx_ref[:, pl.ds(pl.multiple_of((2 * pairs + pair) * 128, 128), 128)] = dv[...].astype(bf16)


def attention_backward(qkv, grad, out, lse, cols, rows):
    tree_len, width = qkv.shape
    pairs = width // 384
    tile = (tree_len, 128)
    return pl.pallas_call(
        attention_backward_kernel,
        name="attention_backward",
        out_shape=jax.ShapeDtypeStruct((tree_len, width), bf16),
        grid=(pairs,),
        in_specs=[
            pl.BlockSpec(tile, lambda p: (0, p)),
            pl.BlockSpec(tile, lambda p: (0, pairs + p)),
            pl.BlockSpec(tile, lambda p: (0, 2 * pairs + p)),
            pl.BlockSpec(tile, lambda p: (0, p)),
            pl.BlockSpec(tile, lambda p: (0, p)),
            pl.BlockSpec((1, 8, tree_len), lambda p: (p, 0, 0)),
            pl.BlockSpec(cols.shape, lambda p: (0, 0)),
            pl.BlockSpec(rows.shape, lambda p: (0, 0)),
        ],
        out_specs=pl.BlockSpec((tree_len, width), lambda p: (0, 0)),
        scratch_shapes=[
            pltpu.VMEM((tree_len, tree_len), f32),
            pltpu.VMEM((2, tree_len, 128), bf16),
            pltpu.VMEM(tile, f32),
            pltpu.VMEM(tile, f32),
        ],
        compiler_params=pltpu.CompilerParams(vmem_limit_bytes=40 << 20),
        cost_estimate=pl.CostEstimate(
            flops=int(0.6 * 5 * pairs * 4 * tree_len * tree_len * 256),
            bytes_accessed=tree_len * width * 6,
            transcendentals=pairs * tree_len * tree_len,
        ),
    )(qkv, qkv, qkv, grad, out, lse, cols, rows)


def norm_parts(values):
    centered = values - jnp.mean(values, axis=-1, keepdims=True)
    scale = lax.rsqrt(jnp.mean(centered * centered, axis=-1, keepdims=True) + norm_eps)
    return centered * scale, scale


def norm_forward(values, gain, shift):
    return norm_parts(values)[0] * gain + shift


def norm_backward(values, gain, grad):
    xhat, scale = norm_parts(values)
    h = grad * gain
    inner = h - jnp.mean(h, axis=-1, keepdims=True)
    inner = inner - xhat * jnp.mean(h * xhat, axis=-1, keepdims=True)
    return scale * inner, jnp.stack([jnp.sum(grad * xhat, axis=0), jnp.sum(grad, axis=0)])


def gelu_and_slope(values):
    square = values * values
    bent = jnp.tanh(gelu_scale * values * (1.0 + gelu_cubic * square))
    half = 0.5 + 0.5 * bent
    slope = half + 2.0 * gelu_scale * values * half * (1.0 - half) * (1.0 + 3.0 * gelu_cubic * square)
    return values * half, slope


def gather_kernel(chunks, weights, extra, *refs):
    shards, refs = refs[: weights + extra], refs[weights + extra :]
    tp = lax.axis_size("tp")
    depth = lax.axis_size("z")
    outs, refs = refs[: weights * tp + extra], refs[weights * tp + extra :]
    send_sems, recv_sems, local_sems = refs
    z, y, core, x = (lax.axis_index(name) for name in ("z", "y", "core", "tp"))

    barrier = pltpu.get_barrier_semaphore()
    partners = [{"z": z ^ k} for k in range(1, depth)] + [{"tp": x ^ k} for k in range(1, tp)]
    partners += [{"y": y ^ 1}, {"core": core ^ 1}]
    for partner in partners:
        pl.semaphore_signal(barrier, inc=1, device_id=partner, device_id_type=pl.DeviceIdType.MESH)
    pl.semaphore_wait(barrier, len(partners))

    first = (0, depth // 2)
    second = (depth // 2, depth - depth // 2)
    started = []

    def copy(source, target, partner):
        slot = len(started)
        made = pltpu.make_async_remote_copy(
            src_ref=source,
            dst_ref=target,
            send_sem=send_sems.at[slot],
            recv_sem=recv_sems.at[slot],
            device_id=partner,
            device_id_type=pl.DeviceIdType.MESH,
        )
        made.start()
        started.append(made)
        return made

    def part(number, t, c, j, span):
        weight, low, rows = chunks[number]
        start = (2 * c + j) * depth + span[0]
        return outs[weight * tp + t].at[pl.ds(start, span[1]), pl.ds(low, rows)]

    def along_z(number):
        weight, low, rows = chunks[number]
        own = shards[weight].at[pl.ds(low, rows)]
        keep = pltpu.make_async_copy(
            own, outs[weight * tp].at[0, pl.ds(low, rows)], local_sems.at[number]
        )
        keep.start()
        sent = [
            copy(own, outs[weight * tp].at[k, pl.ds(low, rows)], {"z": z ^ k})
            for k in range(1, depth)
        ]
        return keep, sent

    crossed = []

    def to_core(number, t, j, span):
        made = copy(part(number, t, 0, j, span), part(number, t, 1, j, span), {"core": core ^ 1})
        crossed.append(made)

    def plane_start(number, keep, sent):
        keep.wait()
        for k in range(1, depth // 2):
            sent[k - 1].wait_recv()
        over_x = [
            copy(part(number, 0, 0, 0, first), part(number, k, 0, 0, first), {"tp": x ^ k})
            for k in range(1, tp)
        ]
        for k in range(max(depth // 2, 1), depth):
            sent[k - 1].wait_recv()
        over_y = copy(part(number, 0, 0, 0, second), part(number, 0, 0, 1, second), {"y": y ^ 1})
        made = copy(part(number, 0, 0, 0, first), part(number, 0, 0, 1, first), {"y": y ^ 1})
        last = [(made, 0, 1, first)]
        for k in range(1, tp):
            made = copy(part(number, 0, 0, 0, second), part(number, k, 0, 0, second), {"tp": x ^ k})
            last.append((made, k, 0, second))
        to_core(number, 0, 0, first)
        to_core(number, 0, 0, second)
        return over_x, over_y, last

    def plane_turn(number, over_x, over_y, last):
        for k in range(1, tp):
            over_x[k - 1].wait_recv()
            made = copy(part(number, k, 0, 0, first), part(number, k, 0, 1, first), {"y": y ^ 1})
            last.append((made, k, 1, first))
            to_core(number, k, 0, first)
        over_y.wait_recv()
        for k in range(1, tp):
            made = copy(part(number, 0, 0, 1, second), part(number, k, 0, 1, second), {"tp": x ^ k})
            last.append((made, k, 1, second))
        to_core(number, 0, 1, second)
        return last

    def plane_end(number, last):
        for made, t, j, span in last:
            made.wait_recv()
            to_core(number, t, j, span)

    count = len(chunks)
    state = {0: along_z(0)}
    columns = []
    for step in range(count + 2):
        if step < count:
            state[step] = plane_start(step, *state[step])
            if step + 1 < count:
                state[step + 1] = along_z(step + 1)
            else:
                for number in range(extra):
                    own, made = shards[weights + number], outs[weights * tp + number]
                    keep = pltpu.make_async_copy(own, made.at[0], local_sems.at[count + number])
                    keep.start()
                    columns.append(keep)
                    columns += [copy(own, made.at[k], {"z": z ^ k}) for k in range(1, depth)]
        if 0 <= step - 1 < count:
            state[step - 1] = plane_turn(step - 1, *state[step - 1])
        if 0 <= step - 2 < count:
            plane_end(step - 2, state[step - 2])
    for made in crossed:
        made.wait_recv()
    for number, made in enumerate(columns):
        if number % depth:
            made.wait_recv()
        else:
            made.wait()
    for made in started:
        made.wait_send()


def gather_weights(shards, pieces, extra=()):
    tp = lax.axis_size("tp")
    depth = lax.axis_size("z")
    chunks = []
    for number, (shard, split) in enumerate(zip(shards, pieces)):
        rows = shard.shape[0] // split
        chunks += [(number, piece * rows, rows) for piece in range(split)]
    copies = len(chunks) * (depth + 1 + 4 * (tp - 1) + 4 * tp) + len(extra) * (depth - 1)
    shapes = [
        jax.ShapeDtypeStruct((4 * depth,) + shard.shape, shard.dtype)
        for shard in shards
        for _ in range(tp)
    ]
    shapes += [jax.ShapeDtypeStruct((depth,) + shard.shape, shard.dtype) for shard in extra]
    sent = sum(shape.size for shape in shapes) * 2
    whole = pl.pallas_call(
        functools.partial(gather_kernel, chunks, len(shards), len(extra)),
        name="gather_weights",
        out_shape=shapes,
        in_specs=[pl.BlockSpec(memory_space=pltpu.VMEM)] * (len(shards) + len(extra)),
        out_specs=[pl.BlockSpec(memory_space=pl.ANY)] * len(shapes),
        scratch_shapes=[
            pltpu.SemaphoreType.DMA((copies,)),
            pltpu.SemaphoreType.DMA((copies,)),
            pltpu.SemaphoreType.DMA((len(chunks) + len(extra),)),
        ],
        compiler_params=pltpu.CompilerParams(collective_id=0, has_side_effects=True),
        cost_estimate=pl.CostEstimate(flops=0, bytes_accessed=2 * sent, transcendentals=0),
    )(*shards, *extra)
    made = [array.reshape(-1, array.shape[2]) for array in whole]
    gathered = [made[number * tp : (number + 1) * tp] for number in range(len(shards))]
    return gathered, made[len(shards) * tp :]


def width_orders():
    count = lax.axis_size("z")
    z, y, core = (lax.axis_index(name) for name in ("z", "y", "core"))
    place = jnp.arange(4 * count, dtype=jnp.int32)
    inward = ((z ^ (place % count)) * 2 + (y ^ (place // count % 2))) * 2
    inward = inward + (core ^ (place // (2 * count)))
    outward = ((core ^ (place % 2)) * 2 + (y ^ (place // 2 % 2))) * count
    outward = outward + (z ^ (place // 4))
    return inward, outward


def arrange_small(values, source):
    blocks = values.reshape(values.shape[0], 1, source.shape[0], -1)
    hit = source[:, None] == jnp.arange(source.shape[0], dtype=jnp.int32)
    return jnp.sum(jnp.where(hit[None, :, :, None], blocks, 0.0), axis=2).reshape(values.shape)


def arrange_kernel(source, first_at, second_at, use_second, first_ref, second_ref, out_ref):
    rows, width = out_ref.shape
    block = width // source.shape[0]
    per = 128 // block
    lane = lax.broadcasted_iota(jnp.int32, (rows, 128), 1)

    def fill(ref):
        for tile in range(width // 128):
            made = None
            for part in range(per):
                at = source[tile * per + part]
                start = pl.multiple_of(lax.div(at, per) * 128, 128)
                values = ref[:, pl.ds(start, 128)].astype(f32)
                turn = lax.rem(part - lax.rem(at, per) + per, per) * block
                values = pltpu.roll(values, turn, 1)
                made = values if part == 0 else jnp.where(lane >= part * block, values, made)
            out_ref[:, tile * 128 : (tile + 1) * 128] = made.astype(out_ref.dtype)

    second = use_second[pl.program_id(0)]

    @pl.when(second == 0)
    def _():
        fill(first_ref)

    @pl.when(second != 0)
    def _():
        fill(second_ref)


def arrange(first, second, source, plan, rows, out_type):
    width = first.shape[1]
    cuts = 4 if rows % 64 == 0 else 1
    rows //= cuts
    plan = [(a * cuts + cut, b * cuts + cut, u) for a, b, u in plan for cut in range(cuts)]
    columns = [jnp.stack(list(column)).astype(jnp.int32) for column in zip(*plan)]
    first_at, second_at, use_second = columns
    return pl.pallas_call(
        arrange_kernel,
        name="arrange",
        out_shape=jax.ShapeDtypeStruct((len(plan) * rows, width), out_type),
        grid_spec=pltpu.PrefetchScalarGridSpec(
            num_scalar_prefetch=4,
            grid=(len(plan),),
            in_specs=[
                pl.BlockSpec((rows, width), lambda i, s, a, b, u: (a[i], 0)),
                pl.BlockSpec((rows, width), lambda i, s, a, b, u: (b[i], 0)),
            ],
            out_specs=pl.BlockSpec((rows, width), lambda i, s, a, b, u: (i, 0)),
        ),
        cost_estimate=pl.CostEstimate(
            flops=len(plan) * rows * width * 8,
            bytes_accessed=len(plan) * rows * width * 8,
            transcendentals=0,
        ),
    )(source, first_at, second_at, use_second, first, second)


def send(values, axes, distance):
    count = 1
    for axis in (axes,) if isinstance(axes, str) else axes:
        count *= lax.axis_size(axis)
    return lax.ppermute(values, axes, [(s, s ^ distance) for s in range(count)])


def after(values, *others):
    return lax.optimization_barrier((values,) + others)[0]


def pick(pieces, position):
    chosen = pieces[0]
    for number in range(1, len(pieces)):
        chosen = jnp.where(position == number, pieces[number], chosen)
    return chosen


def exchange_tp(pieces):
    return pieces[:1] + [send(pieces[k], "tp", k) for k in range(1, len(pieces))]


def in_place_order(pieces):
    here = lax.axis_index("tp")
    return jnp.concatenate([pick(pieces, here ^ s) for s in range(len(pieces))], axis=0)


def sum_everywhere(values):
    for axes in (("y", "tp"), ("z",), ("core",)):
        count = 1
        for axis in axes:
            count *= lax.axis_size(axis)
        values = sum([send(values, axes, k) for k in range(1, count)], values)
    return values


def gather_plane(block):
    count = lax.axis_size("tp")
    places = [(k // 2, k % 2) for k in range(1, 2 * count)]
    return [block] + [send(block, ("y", "tp"), y * count + t) for t, y in places]


def gather_core(blocks):
    return list(blocks), [send(block, "core", 1) for block in blocks]


def assemble(blocks, columns):
    own, other = blocks
    made = []
    for t in range(len(own) // 2):
        pair = own[2 * t : 2 * t + 2] + other[2 * t : 2 * t + 2]
        made.append(jnp.concatenate([block[:, columns] for block in pair], axis=0))
    return jnp.concatenate(made, axis=1)


def scatter_core(part):
    half = part.shape[0] // 2
    came = send(part[half:], "core", 1)
    return (part[:half].astype(f32) + came.astype(f32)).astype(bf16)


def scatter_plane(part):
    tp = lax.axis_size("tp")
    rows, columns = part.shape[0] // 2, part.shape[1] // tp
    straight, across = [part[:rows, :columns]], []
    for t in range(tp):
        for y in range(2):
            if t or y:
                piece = part[y * rows : (y + 1) * rows, t * columns : (t + 1) * columns]
                came = send(piece, ("y", "tp"), y * tp + t)
                (across if t and y else straight).append(came)
    return straight, across


def total(pieces):
    return sum([piece.astype(f32) for piece in pieces[1:]], pieces[0].astype(f32)).astype(bf16)


def scatter_z(part):
    count = lax.axis_size("z")
    rows = part.shape[0] // count
    made = part[:rows].astype(f32)
    for k in range(1, count):
        made = made + send(part[k * rows : (k + 1) * rows], "z", k).astype(f32)
    return made


def segment_tables(segments, parents):
    labels = jnp.arange(parents.shape[0], dtype=jnp.int32)
    up = lambda seg: jnp.sum(jnp.where(seg[:, None] == labels, parents, 0), axis=1)
    parent = up(segments)
    table = jnp.stack([segments, parent, up(parent)])
    return jnp.pad(table.T, ((0, 0), (0, 5))), jnp.pad(table, ((0, 5), (0, 0)))


def on_device(
    tokens, segments, parents, norm_gains, norm_biases, w_qkv, w_out, w_up, w_down, cotangent
):
    tp = lax.axis_size("tp")
    here = lax.axis_index("tp")
    micro = tokens.shape[0]
    own_rows = tokens.shape[2]
    width = tokens.shape[3]
    tree_len = own_rows * tp
    whole = micro // tp
    shared = list(range(whole * tp, micro))
    share_count = len(shared)
    halves = range(tp)
    inward, outward = width_orders()
    split = whole * tree_len

    zero = jnp.int32(0)
    in_plan = []
    for n in range(whole):
        for s in halves:
            far = here ^ s
            in_plan.append((n * tp + here, n * (tp - 1) + jnp.maximum(far - 1, 0), far != 0))
    in_plan += [(zero + m, zero, zero != 0) for m in shared]
    out_plan = []
    for n in range(whole):
        for s in halves:
            far = here ^ s
            out_plan.append((n * tp + here, n * (tp - 1) + jnp.maximum(far - 1, 0), far != 0))
    out_plan += [(zero + m, zero, zero != 0) for m in shared]

    def tree_rows(values):
        flat = values.reshape(micro * own_rows, width)
        came = []
        for n in range(whole):
            for k in range(1, tp):
                start = (n * tp + (here ^ k)) * own_rows
                came.append(send(lax.dynamic_slice_in_dim(flat, start, own_rows), "tp", k))
        came = jnp.concatenate(came, axis=0) if came else flat
        return arrange(flat, came, inward, in_plan, own_rows, bf16)

    def rows_back(values, out_type):
        came = []
        for n in range(whole):
            for k in range(1, tp):
                start = (n * tp + (here ^ k)) * own_rows
                piece = lax.dynamic_slice_in_dim(values, start, own_rows).astype(bf16)
                came.append(send(piece, "tp", k))
        came = jnp.concatenate(came, axis=0) if came else values
        back = arrange(values, came, outward, out_plan, own_rows, out_type)
        return back.reshape(micro, 1, own_rows, width)

    head_width = w_out.shape[0]
    shard_qkv = w_qkv.reshape(w_qkv.shape[0], -1)
    shard_mid = jnp.concatenate([w_out.T, w_up], axis=1)
    (full_qkv,), (mid_z, down_z) = gather_weights([shard_qkv], [4], [shard_mid, w_down.T])

    seg_came = exchange_tp([segments[:, 0]] * tp)
    seg_all = jnp.concatenate([pick(seg_came, here ^ s) for s in halves], axis=1)
    gains = arrange_small(norm_gains, inward)
    biases = arrange_small(norm_biases, inward)
    x = tree_rows(tokens).astype(f32)
    whole_tables = []
    for n in range(whole):
        seg = pick([seg_all[n * tp + s] for s in halves], here)
        par = pick([parents[n * tp + s, 0] for s in halves], here)
        whole_tables.append(segment_tables(seg, par))
    share_tables = [segment_tables(seg_all[m], parents[m, 0]) for m in shared]

    def share_rows(values, k):
        return lax.dynamic_slice_in_dim(values, (here ^ k) * own_rows, own_rows)

    normed = norm_forward(x, gains[0], biases[0]).astype(bf16)
    share_qkv = [dot_nn(normed[split:], w).astype(bf16) for w in full_qkv]
    whole_qkv = [dot_nn(normed[:split], w).astype(bf16) for w in full_qkv] if whole else []
    share_calls = []
    for n in range(share_count):
        cut = slice(n * own_rows, (n + 1) * own_rows)
        share_calls.append(in_place_order(exchange_tp([part[cut] for part in share_qkv])))
    whole_out = [[] for _ in halves]
    share_out = [[] for _ in halves]
    saved = {}
    share_made = []
    mid_plane = gather_plane(mid_z)
    for n in range(whole):
        for t in halves:
            qkv = whole_qkv[t][n * tree_len : (n + 1) * tree_len]
            out, lse = attention_forward(qkv, *whole_tables[n])
            saved[n, t] = (qkv, out, lse)
            whole_out[t].append(out)
    share_calls = [after(call, *mid_plane[1:], *whole_out[0]) for call in share_calls]
    mid_core = gather_core(mid_plane)
    down_plane = gather_plane(after(down_z, mid_plane[1]))
    for n in range(share_count):
        out, lse = attention_forward(share_calls[n], *share_tables[n])
        saved[n] = (share_calls[n], out, lse)
        parts = exchange_tp([share_rows(out, k) for k in halves])
        for t in halves:
            share_out[t].append(parts[t])
    full_out = assemble(mid_core, slice(0, head_width))
    full_up = assemble(mid_core, slice(head_width, None))
    full_down = assemble(gather_core(down_plane), slice(None))
    attended = [jnp.concatenate(whole_out[t] + share_out[t], axis=0) for t in halves]
    attended = jnp.concatenate(attended, axis=1)
    branch_a = dot_nt(attended, full_out)
    residual = x + norm_forward(branch_a, gains[1], biases[1])

    normed_f = norm_forward(residual, gains[2], biases[2]).astype(bf16)
    hidden, slope = gelu_and_slope(dot_nn(normed_f, full_up))
    hidden, slope = lax.optimization_barrier((hidden.astype(bf16), slope.astype(bf16)))
    branch_f = dot_nt(hidden, full_down)
    out = (residual + norm_forward(branch_f, gains[3], biases[3])).astype(bf16)
    out_rows = rows_back(out, bf16)

    grad_out = tree_rows(after(cotangent, full_qkv[0])).astype(f32)
    grad_branch_f, sums_3 = norm_backward(branch_f, gains[3], grad_out)
    grad_branch_f = grad_branch_f.astype(bf16)
    core_down = scatter_core(dot_tn(grad_branch_f, hidden).astype(bf16))
    grad_up = (dot_nn(grad_branch_f, full_down) * slope.astype(f32)).astype(bf16)
    grad_up = after(grad_up, core_down)
    straight_down, across_down = scatter_plane(core_down)
    dw_up = dot_tn(normed_f, grad_up).astype(bf16)
    core_up = scatter_core(dw_up)
    grad_normed_f = dot_nt(after(grad_up, dw_up, *straight_down), full_up)
    grad_part, sums_2 = norm_backward(residual, gains[2], grad_normed_f)
    grad_residual = grad_out + grad_part

    grad_branch_a, sums_1 = norm_backward(branch_a, gains[1], grad_residual)
    grad_branch_a = after(grad_branch_a.astype(bf16), core_up, *across_down)
    z_down = scatter_z(total(straight_down + across_down))
    straight_up, across_up = scatter_plane(core_up)
    grad_attended = dot_nn(grad_branch_a, full_out).astype(bf16)
    share_grad = [grad_attended[split:, t * head_width : (t + 1) * head_width] for t in halves]
    share_do = []
    for n in range(share_count):
        cut = slice(n * own_rows, (n + 1) * own_rows)
        share_do.append(in_place_order(exchange_tp([part[cut] for part in share_grad])))
    core_out = scatter_core(dot_tn(grad_branch_a, attended).astype(bf16))
    grad_qkv = [[] for _ in halves]
    share_parts = [[] for _ in halves]

    def whole_backward(t, *others):
        for n in range(whole):
            qkv, att, lse = saved[n, t]
            do = grad_attended[n * tree_len : (n + 1) * tree_len, t * head_width : (t + 1) * head_width]
            made = attention_backward(qkv, after(do, *others), att, lse, *whole_tables[n])
            grad_qkv[t].append(made)
        return grad_qkv[t]

    made = []
    for t in range(1, tp):
        made += whole_backward(t)
    for n in range(share_count):
        qkv, att, lse = saved[n]
        do = after(share_do[n], z_down, *made)
        dx = attention_backward(qkv, do, att, lse, *share_tables[n])
        made = [dx]
        parts = exchange_tp([share_rows(dx, k) for k in halves])
        for t in halves:
            share_parts[t].append(parts[t])
    made = whole_backward(0, core_out, *straight_up, *made)
    straight_out, across_out = scatter_plane(core_out)
    ready = [*across_up, *straight_out, *across_out, *made]
    grad_qkv = [after(jnp.concatenate(grad_qkv[t] + share_parts[t], axis=0), *ready) for t in halves]
    z_up = scatter_z(total(straight_up + across_up))
    z_out = scatter_z(total(straight_out + across_out))
    core_qkv = [scatter_core(dot_tn(normed, grad_qkv[t]).astype(bf16)) for t in reversed(halves)]
    straight_qkv, across_qkv = scatter_plane(jnp.concatenate(core_qkv[::-1], axis=1))
    z_qkv = scatter_z(total(straight_qkv + across_qkv))
    grad_normed = sum(dot_nt(grad_qkv[t], full_qkv[t]) for t in halves)
    grad_part, sums_0 = norm_backward(x, gains[0], grad_normed)
    input_rows = rows_back(grad_residual + grad_part, f32)
    sums = jnp.concatenate([sums_0, sums_1, sums_2, sums_3])
    sums = sum_everywhere(arrange_small(sums, outward)).reshape(4, 2, width)
    return (
        out_rows,
        input_rows,
        z_qkv.reshape(w_qkv.shape),
        z_out.T,
        z_up,
        z_down.T,
        sums[:, 0],
        sums[:, 1],
    )


def solution(mesh):
    groups, tp = mesh.devices.shape
    fine = jax.sharding.Mesh(mesh.devices.reshape(groups // 4, 2, 2, tp), ("z", "y", "core", "tp"))
    fsdp = ("z", "y", "core")
    in_specs = (
        P(None, fsdp, "tp", None),
        P(None, fsdp, "tp"),
        P(None, fsdp, None),
        P(),
        P(),
        P(fsdp, None, "tp"),
        P("tp", fsdp),
        P(fsdp, "tp"),
        P("tp", fsdp),
        P(None, fsdp, "tp", None),
    )
    out_specs = (
        P(None, fsdp, "tp", None),
        P(None, fsdp, "tp", None),
        P(fsdp, None, "tp"),
        P("tp", fsdp),
        P(fsdp, "tp"),
        P("tp", fsdp),
        P(),
        P(),
    )
    return jax.shard_map(
        on_device, mesh=fine, in_specs=in_specs, out_specs=out_specs, check_vma=False
    )
```

```python
import functools
import math

import jax
import jax.numpy as jnp
from jax import lax
from jax.experimental import pallas as pl
from jax.experimental.pallas import tpu as pltpu
from jax.sharding import PartitionSpec as P

HEAD_DIM = 64
norm_eps = 1e-05
masked_value = -1e30
f32 = jnp.float32
bf16 = jnp.bfloat16
exp2_scale = math.log2(math.e) / math.sqrt(HEAD_DIM)
grad_scale = 1.0 / math.sqrt(HEAD_DIM)
gelu_scale = math.sqrt(2.0 / math.pi)
gelu_cubic = 0.044715


def dot_nn(a, b):
    return lax.dot_general(a, b, (((1,), (0,)), ((), ())), preferred_element_type=f32)


def dot_nt(a, b):
    return lax.dot_general(a, b, (((1,), (1,)), ((), ())), preferred_element_type=f32)


def dot_tn(a, b):
    return lax.dot_general(a, b, (((0,), (0,)), ((), ())), preferred_element_type=f32)


def split_heads(x):
    lane = lax.broadcasted_iota(jnp.int32, x.shape, 1)
    zero = jnp.zeros_like(x)
    return jnp.where(lane < HEAD_DIM, x, zero), jnp.where(lane >= HEAD_DIM, x, zero)


def block_rows(tree_len):
    return 256 if tree_len % 256 == 0 else 128


def attention_forward_kernel(q_ref, k_ref, v_ref, col_ref, row_ref, o_ref, lse_ref, bias):
    tree_len = q_ref.shape[0]
    rows = block_rows(tree_len)

    @pl.when(pl.program_id(0) == 0)
    def _():
        for start in range(0, tree_len, rows):
            stop = start + rows
            key_seg = row_ref[0:1, :stop]
            ok = col_ref[start:stop, 0:1] == key_seg
            ok = ok | (col_ref[start:stop, 1:2] == key_seg)
            ok = ok | (col_ref[start:stop, 2:3] == key_seg)
            i = lax.broadcasted_iota(jnp.int32, (rows, stop), 0) + start
            j = lax.broadcasted_iota(jnp.int32, (rows, stop), 1)
            bias[start:stop, :stop] = jnp.where(ok & (j <= i), 0.0, masked_value).astype(f32)

    for start in range(0, tree_len, rows):
        stop = start + rows
        queries = split_heads(q_ref[start:stop, :])
        outs = []
        for h in range(2):
            scores = dot_nt(queries[h], k_ref[:stop, :]) + bias[start:stop, :stop]
            top = jnp.max(scores, axis=1, keepdims=True)
            weights = jnp.exp2((scores - top) * exp2_scale)
            total = jnp.sum(weights, axis=1, keepdims=True)
            outs.append(dot_nn(weights.astype(bf16), v_ref[:stop, :]) / total)
            lse = jnp.broadcast_to(top * exp2_scale + jnp.log2(total), (rows, 128))
            lse_ref[0, h : h + 1, start:stop] = jnp.transpose(lse)[0:1, :]
        lane = lax.broadcasted_iota(jnp.int32, (rows, 128), 1)
        o_ref[start:stop, :] = jnp.where(lane < HEAD_DIM, outs[0], outs[1]).astype(bf16)


def attention_forward(qkv, cols, rows):
    tree_len, width = qkv.shape
    pairs = width // 384
    tile = (tree_len, 128)
    return pl.pallas_call(
        attention_forward_kernel,
        name="attention_forward",
        out_shape=(
            jax.ShapeDtypeStruct((tree_len, width // 3), bf16),
            jax.ShapeDtypeStruct((pairs, 8, tree_len), f32),
        ),
        grid=(pairs,),
        in_specs=[
            pl.BlockSpec(tile, lambda p: (0, p)),
            pl.BlockSpec(tile, lambda p: (0, pairs + p)),
            pl.BlockSpec(tile, lambda p: (0, 2 * pairs + p)),
            pl.BlockSpec(cols.shape, lambda p: (0, 0)),
            pl.BlockSpec(rows.shape, lambda p: (0, 0)),
        ],
        out_specs=(
            pl.BlockSpec(tile, lambda p: (0, p)),
            pl.BlockSpec((1, 8, tree_len), lambda p: (p, 0, 0)),
        ),
        scratch_shapes=[pltpu.VMEM((tree_len, tree_len), f32)],
        compiler_params=pltpu.CompilerParams(vmem_limit_bytes=40 << 20),
        cost_estimate=pl.CostEstimate(
            flops=int(0.6 * 2 * pairs * 4 * tree_len * tree_len * 256),
            bytes_accessed=tree_len * width * 3,
            transcendentals=pairs * tree_len * tree_len,
        ),
    )(qkv, qkv, qkv, cols, rows)


def attention_backward_kernel(
    q_ref, k_ref, v_ref, do_ref, o_ref, lse_ref, col_ref, row_ref, dx_ref, bias, split_k, dk, dv
):
    tree_len = q_ref.shape[0]
    rows = block_rows(tree_len)
    pair = pl.program_id(0)
    pairs = pl.num_programs(0)

    @pl.when(pair == 0)
    def _():
        for start in range(0, tree_len, rows):
            stop = start + rows
            key_seg = col_ref[:stop, 0:1]
            ok = row_ref[0:1, start:stop] == key_seg
            ok = ok | (row_ref[1:2, start:stop] == key_seg)
            ok = ok | (row_ref[2:3, start:stop] == key_seg)
            j = lax.broadcasted_iota(jnp.int32, (stop, rows), 0)
            i = lax.broadcasted_iota(jnp.int32, (stop, rows), 1) + start
            bias[:stop, start:stop] = jnp.where(ok & (j <= i), 0.0, masked_value).astype(f32)

    split_k[0], split_k[1] = split_heads(k_ref[...])
    dk[...] = jnp.zeros_like(dk)
    dv[...] = jnp.zeros_like(dv)
    sub = lax.broadcasted_iota(jnp.int32, (8, 128), 0)
    lane = lax.broadcasted_iota(jnp.int32, (8, 128), 1)
    own = jnp.where(lane // HEAD_DIM == sub, 1.0, 0.0).astype(f32)
    for start in range(0, tree_len, rows):
        stop = start + rows
        queries = split_heads(q_ref[start:stop, :])
        grads = split_heads(do_ref[start:stop, :])
        product = do_ref[start:stop, :].astype(f32) * o_ref[start:stop, :].astype(f32)
        row_dot = lax.dot_general(
            own,
            product,
            (((1,), (1,)), ((), ())),
            precision=lax.Precision.HIGHEST,
            preferred_element_type=f32,
        )
        probs_low = []
        grad_scores = []
        for h in range(2):
            shift = bias[:stop, start:stop] - lse_ref[0, h : h + 1, start:stop]
            probs = jnp.exp2(dot_nt(k_ref[:stop, :], queries[h]) * exp2_scale + shift)
            grad_probs = dot_nt(v_ref[:stop, :], grads[h])
            probs_low.append(probs.astype(bf16))
            grad_scores.append((probs * (grad_probs - row_dot[h : h + 1, :])).astype(bf16))
        dv[:stop, :] += dot_nn(jnp.concatenate(probs_low, 1), jnp.concatenate(grads, 0))
        dk[:stop, :] += dot_nn(jnp.concatenate(grad_scores, 1), jnp.concatenate(queries, 0))
        dq = dot_tn(grad_scores[0], split_k[0, :stop, :])
        dq = dq + dot_tn(grad_scores[1], split_k[1, :stop, :])
        dq = (dq.astype(bf16).astype(f32) * grad_scale).astype(bf16)
        dx_ref[start:stop, pl.ds(pl.multiple_of(pair * 128, 128), 128)] = dq
    dx_ref[:, pl.ds(pl.multiple_of((pairs + pair) * 128, 128), 128)] = (
        dk[...] * grad_scale
    ).astype(bf16)
    dx_ref[:, pl.ds(pl.multiple_of((2 * pairs + pair) * 128, 128), 128)] = dv[...].astype(bf16)


def attention_backward(qkv, grad, out, lse, cols, rows):
    tree_len, width = qkv.shape
    pairs = width // 384
    tile = (tree_len, 128)
    return pl.pallas_call(
        attention_backward_kernel,
        name="attention_backward",
        out_shape=jax.ShapeDtypeStruct((tree_len, width), bf16),
        grid=(pairs,),
        in_specs=[
            pl.BlockSpec(tile, lambda p: (0, p)),
            pl.BlockSpec(tile, lambda p: (0, pairs + p)),
            pl.BlockSpec(tile, lambda p: (0, 2 * pairs + p)),
            pl.BlockSpec(tile, lambda p: (0, p)),
            pl.BlockSpec(tile, lambda p: (0, p)),
            pl.BlockSpec((1, 8, tree_len), lambda p: (p, 0, 0)),
            pl.BlockSpec(cols.shape, lambda p: (0, 0)),
            pl.BlockSpec(rows.shape, lambda p: (0, 0)),
        ],
        out_specs=pl.BlockSpec((tree_len, width), lambda p: (0, 0)),
        scratch_shapes=[
            pltpu.VMEM((tree_len, tree_len), f32),
            pltpu.VMEM((2, tree_len, 128), bf16),
            pltpu.VMEM(tile, f32),
            pltpu.VMEM(tile, f32),
        ],
        compiler_params=pltpu.CompilerParams(vmem_limit_bytes=40 << 20),
        cost_estimate=pl.CostEstimate(
            flops=int(0.6 * 5 * pairs * 4 * tree_len * tree_len * 256),
            bytes_accessed=tree_len * width * 6,
            transcendentals=pairs * tree_len * tree_len,
        ),
    )(qkv, qkv, qkv, grad, out, lse, cols, rows)


def norm_parts(values):
    centered = values - jnp.mean(values, axis=-1, keepdims=True)
    scale = lax.rsqrt(jnp.mean(centered * centered, axis=-1, keepdims=True) + norm_eps)
    return centered * scale, scale


def norm_forward(values, gain, shift):
    return norm_parts(values)[0] * gain + shift


def norm_backward(values, gain, grad):
    xhat, scale = norm_parts(values)
    h = grad * gain
    inner = h - jnp.mean(h, axis=-1, keepdims=True)
    inner = inner - xhat * jnp.mean(h * xhat, axis=-1, keepdims=True)
    return scale * inner, jnp.stack([jnp.sum(grad * xhat, axis=0), jnp.sum(grad, axis=0)])


def gelu_and_slope(values):
    square = values * values
    bent = jnp.tanh(gelu_scale * values * (1.0 + gelu_cubic * square))
    half = 0.5 + 0.5 * bent
    slope = half + 2.0 * gelu_scale * values * half * (1.0 - half) * (1.0 + 3.0 * gelu_cubic * square)
    return values * half, slope


def apart(position, distance):
    bit = 1
    while bit <= distance:
        if distance & bit:
            position = position + bit - 2 * bit * (position // bit % 2)
        bit *= 2
    return position


def gather_kernel(chunks, weights, moved, *refs):
    shards, refs = refs[:weights], refs[weights:]
    tokens, segments, refs = refs[0], refs[1], refs[2:]
    tp = lax.axis_size("tp")
    depth = lax.axis_size("z")
    outs, refs = refs[: weights * tp], refs[weights * tp :]
    segments_out, refs = refs[0], refs[1:]
    tokens_out, refs = (refs[0], refs[1:]) if moved else (None, refs)
    send_sems, recv_sems, local_sems = refs
    z, y, core, x = (lax.axis_index(name) for name in ("z", "y", "core", "tp"))

    barrier = pltpu.get_barrier_semaphore()
    partners = [{"z": apart(z, k)} for k in range(1, depth)]
    partners += [{"tp": apart(x, k)} for k in range(1, tp)]
    partners += [{"y": 1 - y}, {"core": 1 - core}]
    for partner in partners:
        pl.semaphore_signal(barrier, inc=1, device_id=partner, device_id_type=pl.DeviceIdType.MESH)
    pl.semaphore_wait(barrier, len(partners))

    half = depth // 2
    first = pl.ds(z // half * half, half)
    second = pl.ds(half - z // half * half, half)
    started = []

    def copy(source, target, partner):
        slot = len(started)
        made = pltpu.make_async_remote_copy(
            src_ref=source,
            dst_ref=target,
            send_sem=send_sems.at[slot],
            recv_sem=recv_sems.at[slot],
            device_id=partner,
            device_id_type=pl.DeviceIdType.MESH,
        )
        made.start()
        started.append(made)
        return made

    crossed = []
    for k in range(1, tp):
        partner = {"tp": apart(x, k)}
        crossed.append(copy(segments, segments_out.at[k - 1], partner))
        for n in range(moved):
            source = tokens.at[n * tp + apart(x, k)]
            crossed.append(copy(source, tokens_out.at[n * (tp - 1) + k - 1], partner))

    def part(number, t, at_y, span):
        weight, low, rows = chunks[number]
        return outs[weight * tp + t].at[span, at_y, core, pl.ds(low, rows)]

    def along_z(number):
        weight, low, rows = chunks[number]
        own = shards[weight].at[pl.ds(low, rows)]
        target = outs[weight * tp].at[z, y, core, pl.ds(low, rows)]
        keep = pltpu.make_async_copy(own, target, local_sems.at[number])
        keep.start()
        return keep, [copy(own, target, {"z": apart(z, k)}) for k in range(1, depth)]

    def over(number, t, target_t, at_y, span, partner):
        return copy(part(number, t, at_y, span), part(number, target_t, at_y, span), partner)

    def to_core(number, t, at_y, span):
        crossed.append(over(number, t, t, at_y, span, {"core": 1 - core}))

    def plane_start(number, keep, sent):
        keep.wait()
        for k in range(1, half):
            sent[k - 1].wait_recv()
        over_x = [over(number, 0, k, y, first, {"tp": apart(x, k)}) for k in range(1, tp)]
        for k in range(half, depth):
            sent[k - 1].wait_recv()
        over_y = over(number, 0, 0, y, second, {"y": 1 - y})
        last = [(over(number, 0, 0, y, first, {"y": 1 - y}), 0, 1 - y, first)]
        for k in range(1, tp):
            made = over(number, 0, k, y, second, {"tp": apart(x, k)})
            last.append((made, k, y, second))
        to_core(number, 0, y, first)
        to_core(number, 0, y, second)
        return over_x, over_y, last

    def plane_turn(number, over_x, over_y, last):
        for k in range(1, tp):
            over_x[k - 1].wait_recv()
            made = over(number, k, k, y, first, {"y": 1 - y})
            last.append((made, k, 1 - y, first))
            to_core(number, k, y, first)
        over_y.wait_recv()
        for k in range(1, tp):
            made = over(number, 0, k, 1 - y, second, {"tp": apart(x, k)})
            last.append((made, k, 1 - y, second))
        to_core(number, 0, 1 - y, second)
        return last

    def plane_end(number, last):
        for made, t, at_y, span in last:
            made.wait_recv()
            to_core(number, t, at_y, span)

    count = len(chunks)
    state = {0: along_z(0)}
    for step in range(count + 2):
        if step < count:
            state[step] = plane_start(step, *state[step])
            if step + 1 < count:
                state[step + 1] = along_z(step + 1)
        if 0 <= step - 1 < count:
            state[step - 1] = plane_turn(step - 1, *state[step - 1])
        if 0 <= step - 2 < count:
            plane_end(step - 2, state[step - 2])
    for made in crossed:
        made.wait_recv()
    for made in started:
        made.wait_send()


def gather_weights(shards, pieces, tokens, segments):
    tp = lax.axis_size("tp")
    depth = lax.axis_size("z")
    moved = tokens.shape[0] // tp
    chunks = []
    for number, (shard, split) in enumerate(zip(shards, pieces)):
        rows = shard.shape[0] // split
        chunks += [(number, piece * rows, rows) for piece in range(split)]
    copies = len(chunks) * (depth + 1 + 4 * (tp - 1) + 4 * tp)
    copies += (moved + 1) * (tp - 1)
    shapes = [
        jax.ShapeDtypeStruct((depth, 2, 2) + shard.shape, shard.dtype)
        for shard in shards
        for _ in range(tp)
    ]
    sent = sum(shape.size for shape in shapes) * 2
    shapes += [jax.ShapeDtypeStruct((tp - 1,) + segments.shape, segments.dtype)]
    if moved:
        shapes += [jax.ShapeDtypeStruct((moved * (tp - 1),) + tokens.shape[1:], tokens.dtype)]
    inside = pl.BlockSpec(memory_space=pltpu.VMEM)
    outside = pl.BlockSpec(memory_space=pl.ANY)
    made = pl.pallas_call(
        functools.partial(gather_kernel, chunks, len(shards), moved),
        name="gather_weights",
        out_shape=shapes,
        in_specs=[inside] * len(shards) + [outside, inside],
        out_specs=[outside] * len(shapes),
        scratch_shapes=[
            pltpu.SemaphoreType.DMA((copies,)),
            pltpu.SemaphoreType.DMA((copies,)),
            pltpu.SemaphoreType.DMA((len(chunks),)),
        ],
        compiler_params=pltpu.CompilerParams(collective_id=0, has_side_effects=True),
        cost_estimate=pl.CostEstimate(flops=0, bytes_accessed=2 * sent, transcendentals=0),
    )(*shards, tokens, segments)
    count = len(shards) * tp
    full = [array.reshape(-1, array.shape[-1]) for array in made[:count]]
    full = [full[number * tp : (number + 1) * tp] for number in range(len(shards))]
    crossed = made[count:]
    came = [crossed[1][number] for number in range(moved * (tp - 1))] if moved else []
    return full, [crossed[0][k] for k in range(tp - 1)], came


def send(values, axes, distance):
    count = 1
    for axis in (axes,) if isinstance(axes, str) else axes:
        count *= lax.axis_size(axis)
    return lax.ppermute(values, axes, [(s, s ^ distance) for s in range(count)])


def after(values, *others):
    return lax.optimization_barrier((values,) + others)[0]


def pick(pieces, position):
    chosen = pieces[0]
    for number in range(1, len(pieces)):
        chosen = jnp.where(position == number, pieces[number], chosen)
    return chosen


def exchange_tp(pieces):
    return pieces[:1] + [send(pieces[k], "tp", k) for k in range(1, len(pieces))]


def in_place_order(pieces):
    here = lax.axis_index("tp")
    return jnp.concatenate([pick(pieces, here ^ s) for s in range(len(pieces))], axis=0)


def sum_everywhere(values):
    for axes in (("y", "tp"), ("z",), ("core",)):
        count = 1
        for axis in axes:
            count *= lax.axis_size(axis)
        values = sum([send(values, axes, k) for k in range(1, count)], values)
    return values


def block_at(values, axis, index):
    return lax.dynamic_index_in_dim(values, index, axis, keepdims=False)


def scatter_core(part):
    depth, core = lax.axis_size("z"), lax.axis_index("core")
    blocks = part.reshape(depth, 2, 2, -1, part.shape[1])
    came = send(block_at(blocks, 2, 1 - core), "core", 1)
    return (block_at(blocks, 2, core).astype(f32) + came.astype(f32)).astype(bf16)


def scatter_plane(parts):
    y = lax.axis_index("y")
    straight, across = [block_at(parts[0], 1, y)], []
    for t in range(len(parts)):
        for j in range(2):
            if t or j:
                came = send(block_at(parts[t], 1, y ^ j), ("y", "tp"), j * len(parts) + t)
                (across if t and j else straight).append(came)
    return straight, across


def total(pieces):
    return sum([piece.astype(f32) for piece in pieces[1:]], pieces[0].astype(f32)).astype(bf16)


def scatter_z(part):
    z = lax.axis_index("z")
    made = block_at(part, 0, z).astype(f32)
    for k in range(1, part.shape[0]):
        made = made + send(block_at(part, 0, z ^ k), "z", k).astype(f32)
    return made


def segment_tables(segments, parents):
    labels = jnp.arange(parents.shape[0], dtype=jnp.int32)
    up = lambda seg: jnp.sum(jnp.where(seg[:, None] == labels, parents, 0), axis=1)
    parent = up(segments)
    table = jnp.stack([segments, parent, up(parent)])
    return jnp.pad(table.T, ((0, 0), (0, 5))), jnp.pad(table, ((0, 5), (0, 0)))


def on_device(
    tokens, segments, parents, norm_gains, norm_biases, w_qkv, w_out, w_up, w_down, cotangent
):
    tp = lax.axis_size("tp")
    here = lax.axis_index("tp")
    micro = tokens.shape[0]
    own_rows = tokens.shape[2]
    width = tokens.shape[3]
    head_width = w_out.shape[0]
    tree_len = own_rows * tp
    whole = micro // tp
    shared = list(range(whole * tp, micro))
    share_count = len(shared)
    halves = range(tp)
    split = whole * tree_len

    def outgoing(values):
        return [block_at(values, 0, n * tp + (here ^ k)) for n in range(whole) for k in range(1, tp)]

    def tree_rows(values, came):
        rows = []
        for n in range(whole):
            near = [block_at(values, 0, n * tp + here)]
            rows.append(in_place_order(near + came[n * (tp - 1) : (n + 1) * (tp - 1)]))
        return lax.optimization_barrier(jnp.concatenate(rows + [values[m] for m in shared], axis=0))

    def rows_back(values):
        trees = values.reshape(micro, own_rows, width)
        back = []
        for n in range(whole):
            pieces = [block_at(trees, 0, n * tp + here)]
            for k in range(1, tp):
                low = block_at(trees, 0, n * tp + (here ^ k)).astype(bf16)
                pieces.append(send(low, "tp", k).astype(values.dtype))
            back += [pick(pieces, here ^ s) for s in halves]
        return jnp.stack(back + [trees[m] for m in shared])[:, None]

    def share_rows(values, k):
        return lax.dynamic_slice_in_dim(values, (here ^ k) * own_rows, own_rows)

    shard_qkv = w_qkv.reshape(w_qkv.shape[0], -1)
    (full_qkv, full_out, full_up, full_down), seg_came, tokens_came = gather_weights(
        [shard_qkv, w_out.T, w_up, w_down.T], [4, 1, 4, 4], tokens[:, 0], segments[:, 0]
    )
    seg_came = [segments[:, 0]] + seg_came
    seg_all = jnp.concatenate([pick(seg_came, here ^ s) for s in halves], axis=1)
    x = tree_rows(tokens[:, 0], tokens_came).astype(f32)
    whole_tables = []
    for n in range(whole):
        seg = pick([seg_all[n * tp + s] for s in halves], here)
        par = pick([parents[n * tp + s, 0] for s in halves], here)
        whole_tables.append(segment_tables(seg, par))
    share_tables = [segment_tables(seg_all[m], parents[m, 0]) for m in shared]

    normed = norm_forward(x, norm_gains[0], norm_biases[0]).astype(bf16)
    share_qkv = [dot_nn(normed[split:], w).astype(bf16) for w in full_qkv]
    whole_qkv = [dot_nn(normed[:split], w).astype(bf16) for w in full_qkv] if whole else []
    share_calls = []
    for n in range(share_count):
        cut = slice(n * own_rows, (n + 1) * own_rows)
        share_calls.append(in_place_order(exchange_tp([part[cut] for part in share_qkv])))
    whole_out = [[] for _ in halves]
    share_out = [[] for _ in halves]
    saved = {}
    for n in range(whole):
        for t in halves:
            qkv = whole_qkv[t][n * tree_len : (n + 1) * tree_len]
            out, lse = attention_forward(qkv, *whole_tables[n])
            saved[n, t] = (qkv, out, lse)
            whole_out[t].append(out)
    share_calls = [after(call, *whole_out[0]) for call in share_calls]
    for n in range(share_count):
        out, lse = attention_forward(share_calls[n], *share_tables[n])
        saved[n] = (share_calls[n], out, lse)
        parts = exchange_tp([share_rows(out, k) for k in halves])
        for t in halves:
            share_out[t].append(parts[t])
    attended = [jnp.concatenate(whole_out[t] + share_out[t], axis=0) for t in halves]
    cotangent = after(cotangent[:, 0], *attended)
    cotangent_came = [send(piece, "tp", n % (tp - 1) + 1) for n, piece in enumerate(outgoing(cotangent))]
    branch_a = sum(dot_nt(attended[t], full_out[t]) for t in halves)
    residual = x + norm_forward(branch_a, norm_gains[1], norm_biases[1])

    normed_f = norm_forward(residual, norm_gains[2], norm_biases[2]).astype(bf16)
    hidden = []
    slope = []
    for t in halves:
        values, bent = gelu_and_slope(dot_nn(normed_f, full_up[t]))
        values, bent = lax.optimization_barrier((values.astype(bf16), bent.astype(bf16)))
        hidden.append(values)
        slope.append(bent)
    branch_f = sum(dot_nt(hidden[t], full_down[t]) for t in halves)
    out = (residual + norm_forward(branch_f, norm_gains[3], norm_biases[3])).astype(bf16)
    out_rows = rows_back(out)

    grad_out = tree_rows(cotangent, cotangent_came).astype(f32)
    grad_branch_f, sums_3 = norm_backward(branch_f, norm_gains[3], grad_out)
    grad_branch_f = grad_branch_f.astype(bf16)
    core_down = [scatter_core(dot_tn(grad_branch_f, hidden[t]).astype(bf16)) for t in halves]
    grad_up = [
        (dot_nn(grad_branch_f, full_down[t]) * slope[t].astype(f32)).astype(bf16) for t in halves
    ]
    grad_up = [after(values, *core_down) for values in grad_up]
    straight_down, across_down = scatter_plane(core_down)
    dw_up = [dot_tn(normed_f, grad_up[t]).astype(bf16) for t in halves]
    core_up = [scatter_core(part) for part in dw_up]
    ready = [*dw_up, *straight_down]
    grad_normed_f = sum(dot_nt(after(grad_up[t], *ready), full_up[t]) for t in halves)
    grad_part, sums_2 = norm_backward(residual, norm_gains[2], grad_normed_f)
    grad_residual = grad_out + grad_part

    grad_branch_a, sums_1 = norm_backward(branch_a, norm_gains[1], grad_residual)
    grad_branch_a = after(grad_branch_a.astype(bf16), *core_up, *across_down)
    z_down = scatter_z(total(straight_down + across_down))
    straight_up, across_up = scatter_plane(core_up)
    share_grad = [dot_nn(grad_branch_a[split:], w).astype(bf16) for w in full_out]
    whole_grad = [dot_nn(grad_branch_a[:split], w).astype(bf16) for w in full_out] if whole else []
    share_do = []
    for n in range(share_count):
        cut = slice(n * own_rows, (n + 1) * own_rows)
        share_do.append(in_place_order(exchange_tp([part[cut] for part in share_grad])))
    core_out = [scatter_core(dot_tn(grad_branch_a, part).astype(bf16)) for part in attended]
    grad_qkv = [[] for _ in halves]
    share_parts = [[] for _ in halves]

    def whole_backward(t, *others):
        for n in range(whole):
            qkv, att, lse = saved[n, t]
            do = whole_grad[t][n * tree_len : (n + 1) * tree_len]
            made = attention_backward(qkv, after(do, *others), att, lse, *whole_tables[n])
            grad_qkv[t].append(made)
        return grad_qkv[t]

    made = []
    for t in range(1, tp):
        made += whole_backward(t)
    for n in range(share_count):
        qkv, att, lse = saved[n]
        do = after(share_do[n], z_down, *made)
        dx = attention_backward(qkv, do, att, lse, *share_tables[n])
        made = [dx]
        parts = exchange_tp([share_rows(dx, k) for k in halves])
        for t in halves:
            share_parts[t].append(parts[t])
    made = whole_backward(0, *core_out, *straight_up, *made)
    straight_out, across_out = scatter_plane(core_out)
    ready = [*across_up, *straight_out, *across_out, *made]
    grad_qkv = [after(jnp.concatenate(grad_qkv[t] + share_parts[t], axis=0), *ready) for t in halves]
    z_up = scatter_z(total(straight_up + across_up))
    z_out = scatter_z(total(straight_out + across_out))
    dw_qkv = [dot_tn(normed, grad_qkv[t]).astype(bf16) for t in halves]
    straight_qkv, across_qkv = scatter_plane([scatter_core(part) for part in dw_qkv])
    z_qkv = scatter_z(total(straight_qkv + across_qkv))
    grad_normed = sum(dot_nt(after(grad_qkv[t], *dw_qkv), full_qkv[t]) for t in halves)
    grad_part, sums_0 = norm_backward(x, norm_gains[0], grad_normed)
    input_rows = rows_back(grad_residual + grad_part)
    sums = jnp.concatenate([sums_0, sums_1, sums_2, sums_3])
    sums = sum_everywhere(sums).reshape(4, 2, width)
    return (
        out_rows,
        input_rows,
        z_qkv.reshape(w_qkv.shape),
        z_out.T,
        z_up,
        z_down.T,
        sums[:, 0],
        sums[:, 1],
    )


def solution(mesh):
    groups, tp = mesh.devices.shape
    fine = jax.sharding.Mesh(mesh.devices.reshape(groups // 4, 2, 2, tp), ("z", "y", "core", "tp"))
    fsdp = ("z", "y", "core")
    in_specs = (
        P(None, fsdp, "tp", None),
        P(None, fsdp, "tp"),
        P(None, fsdp, None),
        P(),
        P(),
        P(fsdp, None, "tp"),
        P("tp", fsdp),
        P(fsdp, "tp"),
        P("tp", fsdp),
        P(None, fsdp, "tp", None),
    )
    out_specs = (
        P(None, fsdp, "tp", None),
        P(None, fsdp, "tp", None),
        P(fsdp, None, "tp"),
        P("tp", fsdp),
        P(fsdp, "tp"),
        P("tp", fsdp),
        P(),
        P(),
    )
    return jax.shard_map(
        on_device, mesh=fine, in_specs=in_specs, out_specs=out_specs, check_vma=False
    )
```

```python
import functools
import math

import jax
import jax.numpy as jnp
from jax import lax
from jax.experimental import pallas as pl
from jax.experimental.pallas import tpu as pltpu
from jax.sharding import PartitionSpec as P

HEAD_DIM = 64
norm_eps = 1e-05
masked_value = -1e30
f32 = jnp.float32
bf16 = jnp.bfloat16
exp2_scale = math.log2(math.e) / math.sqrt(HEAD_DIM)
grad_scale = 1.0 / math.sqrt(HEAD_DIM)
gelu_scale = math.sqrt(2.0 / math.pi)
gelu_cubic = 0.044715


def dot_nn(a, b):
    return lax.dot_general(a, b, (((1,), (0,)), ((), ())), preferred_element_type=f32)


def dot_nt(a, b):
    return lax.dot_general(a, b, (((1,), (1,)), ((), ())), preferred_element_type=f32)


def dot_tn(a, b):
    return lax.dot_general(a, b, (((0,), (0,)), ((), ())), preferred_element_type=f32)


def split_heads(x):
    lane = lax.broadcasted_iota(jnp.int32, x.shape, 1)
    zero = jnp.zeros_like(x)
    return jnp.where(lane < HEAD_DIM, x, zero), jnp.where(lane >= HEAD_DIM, x, zero)


def block_rows(tree_len):
    return 256 if tree_len % 256 == 0 else 128


def attention_forward_kernel(q_ref, k_ref, v_ref, col_ref, row_ref, o_ref, lse_ref, bias):
    tree_len = q_ref.shape[0]
    rows = block_rows(tree_len)

    @pl.when(pl.program_id(0) == 0)
    def _():
        for start in range(0, tree_len, rows):
            stop = start + rows
            key_seg = row_ref[0:1, :stop]
            ok = col_ref[start:stop, 0:1] == key_seg
            ok = ok | (col_ref[start:stop, 1:2] == key_seg)
            ok = ok | (col_ref[start:stop, 2:3] == key_seg)
            i = lax.broadcasted_iota(jnp.int32, (rows, stop), 0) + start
            j = lax.broadcasted_iota(jnp.int32, (rows, stop), 1)
            bias[start:stop, :stop] = jnp.where(ok & (j <= i), 0.0, masked_value).astype(f32)

    for start in range(0, tree_len, rows):
        stop = start + rows
        queries = split_heads(q_ref[start:stop, :])
        outs = []
        for h in range(2):
            scores = dot_nt(queries[h], k_ref[:stop, :]) + bias[start:stop, :stop]
            top = jnp.max(scores, axis=1, keepdims=True)
            weights = jnp.exp2((scores - top) * exp2_scale)
            total = jnp.sum(weights, axis=1, keepdims=True)
            outs.append(dot_nn(weights.astype(bf16), v_ref[:stop, :]) / total)
            lse = jnp.broadcast_to(top * exp2_scale + jnp.log2(total), (rows, 128))
            lse_ref[0, h : h + 1, start:stop] = jnp.transpose(lse)[0:1, :]
        lane = lax.broadcasted_iota(jnp.int32, (rows, 128), 1)
        o_ref[start:stop, :] = jnp.where(lane < HEAD_DIM, outs[0], outs[1]).astype(bf16)


def attention_forward(qkv, cols, rows):
    tree_len, width = qkv.shape
    pairs = width // 384
    tile = (tree_len, 128)
    return pl.pallas_call(
        attention_forward_kernel,
        name="attention_forward",
        out_shape=(
            jax.ShapeDtypeStruct((tree_len, width // 3), bf16),
            jax.ShapeDtypeStruct((pairs, 8, tree_len), f32),
        ),
        grid=(pairs,),
        in_specs=[
            pl.BlockSpec(tile, lambda p: (0, p)),
            pl.BlockSpec(tile, lambda p: (0, pairs + p)),
            pl.BlockSpec(tile, lambda p: (0, 2 * pairs + p)),
            pl.BlockSpec(cols.shape, lambda p: (0, 0)),
            pl.BlockSpec(rows.shape, lambda p: (0, 0)),
        ],
        out_specs=(
            pl.BlockSpec(tile, lambda p: (0, p)),
            pl.BlockSpec((1, 8, tree_len), lambda p: (p, 0, 0)),
        ),
        scratch_shapes=[pltpu.VMEM((tree_len, tree_len), f32)],
        compiler_params=pltpu.CompilerParams(vmem_limit_bytes=40 << 20),
        cost_estimate=pl.CostEstimate(
            flops=int(0.6 * 2 * pairs * 4 * tree_len * tree_len * 256),
            bytes_accessed=tree_len * width * 3,
            transcendentals=pairs * tree_len * tree_len,
        ),
    )(qkv, qkv, qkv, cols, rows)


def attention_backward_kernel(
    q_ref, k_ref, v_ref, do_ref, o_ref, lse_ref, col_ref, row_ref, dx_ref, bias, split_k, dk, dv
):
    tree_len = q_ref.shape[0]
    rows = block_rows(tree_len)
    pair = pl.program_id(0)
    pairs = pl.num_programs(0)

    @pl.when(pair == 0)
    def _():
        for start in range(0, tree_len, rows):
            stop = start + rows
            key_seg = col_ref[:stop, 0:1]
            ok = row_ref[0:1, start:stop] == key_seg
            ok = ok | (row_ref[1:2, start:stop] == key_seg)
            ok = ok | (row_ref[2:3, start:stop] == key_seg)
            j = lax.broadcasted_iota(jnp.int32, (stop, rows), 0)
            i = lax.broadcasted_iota(jnp.int32, (stop, rows), 1) + start
            bias[:stop, start:stop] = jnp.where(ok & (j <= i), 0.0, masked_value).astype(f32)

    split_k[0], split_k[1] = split_heads(k_ref[...])
    dk[...] = jnp.zeros_like(dk)
    dv[...] = jnp.zeros_like(dv)
    sub = lax.broadcasted_iota(jnp.int32, (8, 128), 0)
    lane = lax.broadcasted_iota(jnp.int32, (8, 128), 1)
    own = jnp.where(lane // HEAD_DIM == sub, 1.0, 0.0).astype(f32)
    for start in range(0, tree_len, rows):
        stop = start + rows
        queries = split_heads(q_ref[start:stop, :])
        grads = split_heads(do_ref[start:stop, :])
        product = do_ref[start:stop, :].astype(f32) * o_ref[start:stop, :].astype(f32)
        row_dot = lax.dot_general(
            own,
            product,
            (((1,), (1,)), ((), ())),
            precision=lax.Precision.HIGHEST,
            preferred_element_type=f32,
        )
        probs_low = []
        grad_scores = []
        for h in range(2):
            shift = bias[:stop, start:stop] - lse_ref[0, h : h + 1, start:stop]
            probs = jnp.exp2(dot_nt(k_ref[:stop, :], queries[h]) * exp2_scale + shift)
            grad_probs = dot_nt(v_ref[:stop, :], grads[h])
            probs_low.append(probs.astype(bf16))
            grad_scores.append((probs * (grad_probs - row_dot[h : h + 1, :])).astype(bf16))
        dv[:stop, :] += dot_nn(jnp.concatenate(probs_low, 1), jnp.concatenate(grads, 0))
        dk[:stop, :] += dot_nn(jnp.concatenate(grad_scores, 1), jnp.concatenate(queries, 0))
        dq = dot_tn(grad_scores[0], split_k[0, :stop, :])
        dq = dq + dot_tn(grad_scores[1], split_k[1, :stop, :])
        dq = (dq.astype(bf16).astype(f32) * grad_scale).astype(bf16)
        dx_ref[start:stop, pl.ds(pl.multiple_of(pair * 128, 128), 128)] = dq
    dx_ref[:, pl.ds(pl.multiple_of((pairs + pair) * 128, 128), 128)] = (
        dk[...] * grad_scale
    ).astype(bf16)
    dx_ref[:, pl.ds(pl.multiple_of((2 * pairs + pair) * 128, 128), 128)] = dv[...].astype(bf16)


def attention_backward(qkv, grad, out, lse, cols, rows):
    tree_len, width = qkv.shape
    pairs = width // 384
    tile = (tree_len, 128)
    return pl.pallas_call(
        attention_backward_kernel,
        name="attention_backward",
        out_shape=jax.ShapeDtypeStruct((tree_len, width), bf16),
        grid=(pairs,),
        in_specs=[
            pl.BlockSpec(tile, lambda p: (0, p)),
            pl.BlockSpec(tile, lambda p: (0, pairs + p)),
            pl.BlockSpec(tile, lambda p: (0, 2 * pairs + p)),
            pl.BlockSpec(tile, lambda p: (0, p)),
            pl.BlockSpec(tile, lambda p: (0, p)),
            pl.BlockSpec((1, 8, tree_len), lambda p: (p, 0, 0)),
            pl.BlockSpec(cols.shape, lambda p: (0, 0)),
            pl.BlockSpec(rows.shape, lambda p: (0, 0)),
        ],
        out_specs=pl.BlockSpec((tree_len, width), lambda p: (0, 0)),
        scratch_shapes=[
            pltpu.VMEM((tree_len, tree_len), f32),
            pltpu.VMEM((2, tree_len, 128), bf16),
            pltpu.VMEM(tile, f32),
            pltpu.VMEM(tile, f32),
        ],
        compiler_params=pltpu.CompilerParams(vmem_limit_bytes=40 << 20),
        cost_estimate=pl.CostEstimate(
            flops=int(0.6 * 5 * pairs * 4 * tree_len * tree_len * 256),
            bytes_accessed=tree_len * width * 6,
            transcendentals=pairs * tree_len * tree_len,
        ),
    )(qkv, qkv, qkv, grad, out, lse, cols, rows)


def norm_parts(values):
    centered = values - jnp.mean(values, axis=-1, keepdims=True)
    scale = lax.rsqrt(jnp.mean(centered * centered, axis=-1, keepdims=True) + norm_eps)
    return centered * scale, scale


def norm_forward(values, gain, shift):
    return norm_parts(values)[0] * gain + shift


def norm_backward(values, gain, grad):
    xhat, scale = norm_parts(values)
    h = grad * gain
    inner = h - jnp.mean(h, axis=-1, keepdims=True)
    inner = inner - xhat * jnp.mean(h * xhat, axis=-1, keepdims=True)
    return scale * inner, jnp.stack([jnp.sum(grad * xhat, axis=0), jnp.sum(grad, axis=0)])


def gelu_and_slope(values):
    square = values * values
    bent = jnp.tanh(gelu_scale * values * (1.0 + gelu_cubic * square))
    half = 0.5 + 0.5 * bent
    slope = half + 2.0 * gelu_scale * values * half * (1.0 - half) * (1.0 + 3.0 * gelu_cubic * square)
    return values * half, slope


def apart(position, distance):
    bit = 1
    while bit <= distance:
        if distance & bit:
            position = position + bit - 2 * bit * (position // bit % 2)
        bit *= 2
    return position


def gather_kernel(chunks, weights, *refs):
    shards, refs = refs[:weights], refs[weights:]
    tokens, segments, refs = refs[0], refs[1], refs[2:]
    tp = lax.axis_size("tp")
    depth = lax.axis_size("z")
    outs, refs = refs[: weights * tp], refs[weights * tp :]
    segments_out, tokens_out, send_sems, recv_sems, local_sems = refs
    z, y, core, x = (lax.axis_index(name) for name in ("z", "y", "core", "tp"))

    barrier = pltpu.get_barrier_semaphore()
    partners = [{"z": apart(z, k)} for k in range(1, depth)]
    partners += [{"tp": apart(x, k)} for k in range(1, tp)]
    partners += [{"y": 1 - y}, {"core": 1 - core}]
    for partner in partners:
        pl.semaphore_signal(barrier, inc=1, device_id=partner, device_id_type=pl.DeviceIdType.MESH)
    pl.semaphore_wait(barrier, len(partners))

    half = depth // 2
    first = pl.ds(z // half * half, half)
    second = pl.ds(half - z // half * half, half)
    started = []

    def copy(source, target, partner):
        slot = len(started)
        made = pltpu.make_async_remote_copy(
            src_ref=source,
            dst_ref=target,
            send_sem=send_sems.at[slot],
            recv_sem=recv_sems.at[slot],
            device_id=partner,
            device_id_type=pl.DeviceIdType.MESH,
        )
        made.start()
        started.append(made)
        return made

    crossed = []
    for k in range(1, tp):
        partner = {"tp": apart(x, k)}
        crossed.append(copy(segments, segments_out.at[k - 1], partner))
        micro = tokens.shape[0]
        sources = [n * tp + apart(x, k) for n in range(micro // tp)]
        sources += range(micro // tp * tp, micro)
        for n, source in enumerate(sources):
            target = tokens_out.at[n * (tp - 1) + k - 1]
            crossed.append(copy(tokens.at[source], target, partner))

    def part(number, t, at_y, span):
        weight, low, rows = chunks[number]
        return outs[weight * tp + t].at[span, at_y, core, pl.ds(low, rows)]

    def along_z(number):
        weight, low, rows = chunks[number]
        own = shards[weight].at[pl.ds(low, rows)]
        target = outs[weight * tp].at[z, y, core, pl.ds(low, rows)]
        keep = pltpu.make_async_copy(own, target, local_sems.at[number])
        keep.start()
        return keep, [copy(own, target, {"z": apart(z, k)}) for k in range(1, depth)]

    def over(number, t, target_t, at_y, span, partner):
        return copy(part(number, t, at_y, span), part(number, target_t, at_y, span), partner)

    def to_core(number, t, at_y, span):
        crossed.append(over(number, t, t, at_y, span, {"core": 1 - core}))

    def plane_start(number, keep, sent):
        keep.wait()
        for k in range(1, half):
            sent[k - 1].wait_recv()
        over_x = [over(number, 0, k, y, first, {"tp": apart(x, k)}) for k in range(1, tp)]
        for k in range(half, depth):
            sent[k - 1].wait_recv()
        over_y = over(number, 0, 0, y, second, {"y": 1 - y})
        last = [(over(number, 0, 0, y, first, {"y": 1 - y}), 0, 1 - y, first)]
        for k in range(1, tp):
            made = over(number, 0, k, y, second, {"tp": apart(x, k)})
            last.append((made, k, y, second))
        to_core(number, 0, y, first)
        to_core(number, 0, y, second)
        return over_x, over_y, last

    def plane_turn(number, over_x, over_y, last):
        for k in range(1, tp):
            over_x[k - 1].wait_recv()
            made = over(number, k, k, y, first, {"y": 1 - y})
            last.append((made, k, 1 - y, first))
            to_core(number, k, y, first)
        over_y.wait_recv()
        for k in range(1, tp):
            made = over(number, 0, k, 1 - y, second, {"tp": apart(x, k)})
            last.append((made, k, 1 - y, second))
        to_core(number, 0, 1 - y, second)
        return last

    def plane_end(number, last):
        for made, t, at_y, span in last:
            made.wait_recv()
            to_core(number, t, at_y, span)

    count = len(chunks)
    state = {0: along_z(0)}
    for step in range(count + 2):
        if step < count:
            state[step] = plane_start(step, *state[step])
            if step + 1 < count:
                state[step + 1] = along_z(step + 1)
        if 0 <= step - 1 < count:
            state[step - 1] = plane_turn(step - 1, *state[step - 1])
        if 0 <= step - 2 < count:
            plane_end(step - 2, state[step - 2])
    for made in crossed:
        made.wait_recv()
    for made in started:
        made.wait_send()


def gather_weights(shards, pieces, tokens, segments):
    tp = lax.axis_size("tp")
    depth = lax.axis_size("z")
    moved = tokens.shape[0] // tp + tokens.shape[0] % tp
    chunks = []
    for number, (shard, split) in enumerate(zip(shards, pieces)):
        rows = shard.shape[0] // split
        chunks += [(number, piece * rows, rows) for piece in range(split)]
    copies = len(chunks) * (depth + 1 + 4 * (tp - 1) + 4 * tp)
    copies += (moved + 1) * (tp - 1)
    shapes = [
        jax.ShapeDtypeStruct((depth, 2, 2) + shard.shape, shard.dtype)
        for shard in shards
        for _ in range(tp)
    ]
    sent = sum(shape.size for shape in shapes) * 2
    shapes += [jax.ShapeDtypeStruct((tp - 1,) + segments.shape, segments.dtype)]
    shapes += [jax.ShapeDtypeStruct((moved * (tp - 1),) + tokens.shape[1:], tokens.dtype)]
    inside = pl.BlockSpec(memory_space=pltpu.VMEM)
    outside = pl.BlockSpec(memory_space=pl.ANY)
    made = pl.pallas_call(
        functools.partial(gather_kernel, chunks, len(shards)),
        name="gather_weights",
        out_shape=shapes,
        in_specs=[inside] * len(shards) + [outside, inside],
        out_specs=[outside] * len(shapes),
        scratch_shapes=[
            pltpu.SemaphoreType.DMA((copies,)),
            pltpu.SemaphoreType.DMA((copies,)),
            pltpu.SemaphoreType.DMA((len(chunks),)),
        ],
        compiler_params=pltpu.CompilerParams(collective_id=0, has_side_effects=True),
        cost_estimate=pl.CostEstimate(flops=0, bytes_accessed=2 * sent, transcendentals=0),
    )(*shards, tokens, segments)
    count = len(shards) * tp
    full = [array.reshape(-1, array.shape[-1]) for array in made[:count]]
    full = [full[number * tp : (number + 1) * tp] for number in range(len(shards))]
    crossed = made[count:]
    came = [crossed[1][number] for number in range(moved * (tp - 1))]
    return full, [crossed[0][k] for k in range(tp - 1)], came


def send(values, axes, distance):
    count = 1
    for axis in (axes,) if isinstance(axes, str) else axes:
        count *= lax.axis_size(axis)
    return lax.ppermute(values, axes, [(s, s ^ distance) for s in range(count)])


def after(values, *others):
    return lax.optimization_barrier((values,) + others)[0]


def pick(pieces, position):
    chosen = pieces[0]
    for number in range(1, len(pieces)):
        chosen = jnp.where(position == number, pieces[number], chosen)
    return chosen


def exchange_tp(pieces):
    return pieces[:1] + [send(pieces[k], "tp", k) for k in range(1, len(pieces))]


def in_place_order(pieces):
    here = lax.axis_index("tp")
    return jnp.concatenate([pick(pieces, here ^ s) for s in range(len(pieces))], axis=0)


def sum_everywhere(values):
    for axes in (("y", "tp"), ("z",), ("core",)):
        count = 1
        for axis in axes:
            count *= lax.axis_size(axis)
        values = sum([send(values, axes, k) for k in range(1, count)], values)
    return values


def block_at(values, axis, index):
    return lax.dynamic_index_in_dim(values, index, axis, keepdims=False)


def scatter_core(part):
    depth, core = lax.axis_size("z"), lax.axis_index("core")
    blocks = part.reshape(depth, 2, 2, -1, part.shape[1])
    came = send(block_at(blocks, 2, 1 - core), "core", 1)
    return (block_at(blocks, 2, core).astype(f32) + came.astype(f32)).astype(bf16)


def scatter_plane(parts):
    y = lax.axis_index("y")
    straight, across = [block_at(parts[0], 1, y)], []
    for t in range(len(parts)):
        for j in range(2):
            if t or j:
                came = send(block_at(parts[t], 1, y ^ j), ("y", "tp"), j * len(parts) + t)
                (across if t and j else straight).append(came)
    return straight, across


def total(pieces):
    return sum([piece.astype(f32) for piece in pieces[1:]], pieces[0].astype(f32)).astype(bf16)


def scatter_z(part):
    z = lax.axis_index("z")
    made = block_at(part, 0, z).astype(f32)
    for k in range(1, part.shape[0]):
        made = made + send(block_at(part, 0, z ^ k), "z", k).astype(f32)
    return made


def segment_tables(segments, parents):
    labels = jnp.arange(parents.shape[0], dtype=jnp.int32)
    up = lambda seg: jnp.sum(jnp.where(seg[:, None] == labels, parents, 0), axis=1)
    parent = up(segments)
    table = jnp.stack([segments, parent, up(parent)])
    return jnp.pad(table.T, ((0, 0), (0, 5))), jnp.pad(table, ((0, 5), (0, 0)))


def on_device(
    tokens, segments, parents, norm_gains, norm_biases, w_qkv, w_out, w_up, w_down, cotangent
):
    tp = lax.axis_size("tp")
    here = lax.axis_index("tp")
    micro = tokens.shape[0]
    own_rows = tokens.shape[2]
    width = tokens.shape[3]
    head_width = w_out.shape[0]
    tree_len = own_rows * tp
    whole = micro // tp
    shared = list(range(whole * tp, micro))
    share_count = len(shared)
    halves = range(tp)
    split = whole * tree_len

    def outgoing(values):
        return [block_at(values, 0, n * tp + (here ^ k)) for n in range(whole) for k in range(1, tp)]

    def whole_trees(values, came):
        rows = []
        for n in range(whole):
            near = [block_at(values, 0, n * tp + here)]
            rows.append(in_place_order(near + came[n * (tp - 1) : (n + 1) * (tp - 1)]))
        return rows

    def rows_back(values):
        trees = values.reshape(micro, own_rows, width)
        back = []
        for n in range(whole):
            pieces = [block_at(trees, 0, n * tp + here)]
            for k in range(1, tp):
                low = block_at(trees, 0, n * tp + (here ^ k)).astype(bf16)
                pieces.append(send(low, "tp", k).astype(values.dtype))
            back += [pick(pieces, here ^ s) for s in halves]
        return jnp.stack(back + [trees[m] for m in shared])[:, None]

    def share_rows(values, k):
        return lax.dynamic_slice_in_dim(values, (here ^ k) * own_rows, own_rows)

    shard_qkv = w_qkv.reshape(w_qkv.shape[0], -1)
    (full_qkv, full_out, full_up), seg_came, tokens_came = gather_weights(
        [shard_qkv, w_out.T, w_up], [4, 1, 4], tokens[:, 0], segments[:, 0]
    )
    down = lax.all_gather(
        after(w_down.T, full_qkv[0]), ("tp", "z", "y", "core"), axis=0, tiled=True
    ).reshape(tp, width, -1)
    full_down = [pick([down[s] for s in halves], here ^ t) for t in halves]
    seg_came = [segments[:, 0]] + seg_came
    seg_all = jnp.concatenate([pick(seg_came, here ^ s) for s in halves], axis=1)
    all_rows = whole_trees(tokens[:, 0], tokens_came)
    for n, m in enumerate(shared):
        start = (whole + n) * (tp - 1)
        all_rows.append(in_place_order([tokens[m, 0]] + tokens_came[start : start + tp - 1]))
    all_rows = lax.optimization_barrier(jnp.concatenate(all_rows, axis=0))
    x = jnp.concatenate([all_rows[:split]] + [tokens[m, 0] for m in shared], axis=0).astype(f32)
    whole_tables = []
    for n in range(whole):
        seg = pick([seg_all[n * tp + s] for s in halves], here)
        par = pick([parents[n * tp + s, 0] for s in halves], here)
        whole_tables.append(segment_tables(seg, par))
    share_tables = [segment_tables(seg_all[m], parents[m, 0]) for m in shared]

    normed = norm_forward(all_rows.astype(f32), norm_gains[0], norm_biases[0]).astype(bf16)
    normed_shared = normed[split:]
    normed_whole = normed[:split]
    shared_qkv = dot_nn(normed_shared, full_qkv[0]).astype(bf16)
    whole_qkv = [dot_nn(normed_whole, w).astype(bf16) for w in full_qkv] if whole else []
    whole_out = [[] for _ in halves]
    share_out = [[] for _ in halves]
    saved = {}
    for n in range(share_count):
        qkv = shared_qkv[n * tree_len : (n + 1) * tree_len]
        out, lse = attention_forward(qkv, *share_tables[n])
        saved[n] = (qkv, out, lse)
        parts = exchange_tp([share_rows(out, k) for k in halves])
        for t in halves:
            share_out[t].append(parts[t])
    first = [saved[n][1] for n in range(share_count)]
    for n in range(whole):
        for t in halves:
            qkv = after(whole_qkv[t][n * tree_len : (n + 1) * tree_len], *first)
            out, lse = attention_forward(qkv, *whole_tables[n])
            saved[n, t] = (qkv, out, lse)
            whole_out[t].append(out)
    attended = [jnp.concatenate(whole_out[t] + share_out[t], axis=0) for t in halves]
    cotangent = after(cotangent[:, 0], *attended)
    cotangent_came = [send(piece, "tp", n % (tp - 1) + 1) for n, piece in enumerate(outgoing(cotangent))]
    branch_a = sum(dot_nt(attended[t], full_out[t]) for t in halves)
    residual = x + norm_forward(branch_a, norm_gains[1], norm_biases[1])

    normed_f = norm_forward(residual, norm_gains[2], norm_biases[2]).astype(bf16)
    hidden = []
    slope = []
    for t in halves:
        values, bent = gelu_and_slope(dot_nn(normed_f, full_up[t]))
        values, bent = lax.optimization_barrier((values.astype(bf16), bent.astype(bf16)))
        hidden.append(values)
        slope.append(bent)
    branch_f = sum(dot_nt(hidden[t], full_down[t]) for t in halves)
    out = (residual + norm_forward(branch_f, norm_gains[3], norm_biases[3])).astype(bf16)
    out_rows = rows_back(out)

    grad_out = whole_trees(cotangent, cotangent_came) + [cotangent[m] for m in shared]
    grad_out = lax.optimization_barrier(jnp.concatenate(grad_out, axis=0)).astype(f32)
    grad_branch_f, sums_3 = norm_backward(branch_f, norm_gains[3], grad_out)
    grad_branch_f = grad_branch_f.astype(bf16)
    core_down = [scatter_core(dot_tn(grad_branch_f, hidden[t]).astype(bf16)) for t in halves]
    grad_up = [
        (dot_nn(grad_branch_f, full_down[t]) * slope[t].astype(f32)).astype(bf16) for t in halves
    ]
    grad_up = [after(values, *core_down) for values in grad_up]
    straight_down, across_down = scatter_plane(core_down)
    dw_up = [dot_tn(normed_f, grad_up[t]).astype(bf16) for t in halves]
    core_up = [scatter_core(part) for part in dw_up]
    ready = [*dw_up, *straight_down]
    grad_normed_f = sum(dot_nt(after(grad_up[t], *ready), full_up[t]) for t in halves)
    grad_part, sums_2 = norm_backward(residual, norm_gains[2], grad_normed_f)
    grad_residual = grad_out + grad_part

    grad_branch_a, sums_1 = norm_backward(branch_a, norm_gains[1], grad_residual)
    grad_branch_a = after(grad_branch_a.astype(bf16), *core_up, *across_down)
    z_down = scatter_z(total(straight_down + across_down))
    straight_up, across_up = scatter_plane(core_up)
    share_grad = [dot_nn(grad_branch_a[split:], w).astype(bf16) for w in full_out]
    whole_grad = [dot_nn(grad_branch_a[:split], w).astype(bf16) for w in full_out] if whole else []
    share_do = []
    for n in range(share_count):
        cut = slice(n * own_rows, (n + 1) * own_rows)
        share_do.append(in_place_order(exchange_tp([part[cut] for part in share_grad])))
    core_out = [scatter_core(dot_tn(grad_branch_a, part).astype(bf16)) for part in attended]
    grad_qkv = [[] for _ in halves]

    def whole_backward(t, *others):
        for n in range(whole):
            qkv, att, lse = saved[n, t]
            do = whole_grad[t][n * tree_len : (n + 1) * tree_len]
            made = attention_backward(qkv, after(do, *others), att, lse, *whole_tables[n])
            grad_qkv[t].append(made)
        return grad_qkv[t]

    made = []
    dw_qkv = [None] * tp
    for t in range(1, tp):
        made += whole_backward(t)
        if whole:
            dw_qkv[t] = dot_tn(normed_whole, jnp.concatenate(grad_qkv[t], axis=0)).astype(bf16)
        else:
            dw_qkv[t] = jnp.zeros(full_qkv[t].shape, bf16)
    core_qkv = [None] + [scatter_core(part) for part in dw_qkv[1:]]
    grad_shared = []
    own_part = []
    for n in range(share_count):
        qkv, att, lse = saved[n]
        do = after(share_do[n], *made)
        dx = attention_backward(qkv, do, att, lse, *share_tables[n])
        made = [dx]
        grad_shared.append(dx)
    whole_backward(0, *core_out, *straight_up, *core_qkv[1:], *made)
    for n in range(share_count):
        part = dot_nt(grad_shared[n], full_qkv[0])
        pieces = exchange_tp([share_rows(part, 0)] + [share_rows(part, k).astype(bf16) for k in halves[1:]])
        own_part.append(sum([piece.astype(f32) for piece in pieces[1:]], pieces[0]))
    straight_out, across_out = scatter_plane(core_out)
    ready = [*across_up, *straight_out, *across_out, z_down]
    owned = after(jnp.concatenate(grad_qkv[0] + grad_shared, axis=0), *ready)
    z_up = scatter_z(total(straight_up + across_up))
    z_out = scatter_z(total(straight_out + across_out))
    dw_qkv[0] = dot_tn(normed, owned).astype(bf16)
    core_qkv[0] = scatter_core(dw_qkv[0])
    straight_qkv, across_qkv = scatter_plane(core_qkv)
    z_qkv = scatter_z(total(straight_qkv + across_qkv))
    ready = [dw_qkv[0], *across_qkv]
    grad_normed = list(own_part)
    if whole:
        trees = [after(jnp.concatenate(grad_qkv[t], axis=0), *ready) for t in halves]
        trees[1:] = [after(rows, core_qkv[0]) for rows in trees[1:]]
        grad_normed = [sum(dot_nt(trees[t], full_qkv[t]) for t in halves)] + grad_normed
    grad_normed = jnp.concatenate(grad_normed, axis=0)
    grad_part, sums_0 = norm_backward(x, norm_gains[0], grad_normed)
    input_rows = rows_back(grad_residual + grad_part)
    sums = jnp.concatenate([sums_0, sums_1, sums_2, sums_3])
    sums = sum_everywhere(sums).reshape(4, 2, width)
    return (
        out_rows,
        input_rows,
        z_qkv.reshape(w_qkv.shape),
        z_out.T,
        z_up,
        z_down.T,
        sums[:, 0],
        sums[:, 1],
    )


def solution(mesh):
    groups, tp = mesh.devices.shape
    fine = jax.sharding.Mesh(mesh.devices.reshape(groups // 4, 2, 2, tp), ("z", "y", "core", "tp"))
    fsdp = ("z", "y", "core")
    in_specs = (
        P(None, fsdp, "tp", None),
        P(None, fsdp, "tp"),
        P(None, fsdp, None),
        P(),
        P(),
        P(fsdp, None, "tp"),
        P("tp", fsdp),
        P(fsdp, "tp"),
        P("tp", fsdp),
        P(None, fsdp, "tp", None),
    )
    out_specs = (
        P(None, fsdp, "tp", None),
        P(None, fsdp, "tp", None),
        P(fsdp, None, "tp"),
        P("tp", fsdp),
        P(fsdp, "tp"),
        P("tp", fsdp),
        P(),
        P(),
    )
    return jax.shard_map(
        on_device, mesh=fine, in_specs=in_specs, out_specs=out_specs, check_vma=False
    )
```

```python
import functools
import math

import jax
import jax.numpy as jnp
from jax import lax
from jax.experimental import pallas as pl
from jax.experimental.pallas import tpu as pltpu
from jax.sharding import PartitionSpec as P

HEAD_DIM = 64
norm_eps = 1e-05
masked_value = -1e30
f32 = jnp.float32
bf16 = jnp.bfloat16
exp2_scale = math.log2(math.e) / math.sqrt(HEAD_DIM)
grad_scale = 1.0 / math.sqrt(HEAD_DIM)
gelu_scale = math.sqrt(2.0 / math.pi)
gelu_cubic = 0.044715


def dot_nn(a, b):
    return lax.dot_general(a, b, (((1,), (0,)), ((), ())), preferred_element_type=f32)


def dot_nt(a, b):
    return lax.dot_general(a, b, (((1,), (1,)), ((), ())), preferred_element_type=f32)


def dot_tn(a, b):
    return lax.dot_general(a, b, (((0,), (0,)), ((), ())), preferred_element_type=f32)


def split_heads(x):
    lane = lax.broadcasted_iota(jnp.int32, x.shape, 1)
    zero = jnp.zeros_like(x)
    return jnp.where(lane < HEAD_DIM, x, zero), jnp.where(lane >= HEAD_DIM, x, zero)


def block_rows(tree_len):
    return 256 if tree_len % 256 == 0 else 128


def attention_forward_kernel(q_ref, k_ref, v_ref, col_ref, row_ref, o_ref, lse_ref, bias):
    tree_len = q_ref.shape[0]
    rows = block_rows(tree_len)

    @pl.when(pl.program_id(0) == 0)
    def _():
        for start in range(0, tree_len, rows):
            stop = start + rows
            key_seg = row_ref[0:1, :stop]
            ok = col_ref[start:stop, 0:1] == key_seg
            ok = ok | (col_ref[start:stop, 1:2] == key_seg)
            ok = ok | (col_ref[start:stop, 2:3] == key_seg)
            i = lax.broadcasted_iota(jnp.int32, (rows, stop), 0) + start
            j = lax.broadcasted_iota(jnp.int32, (rows, stop), 1)
            bias[start:stop, :stop] = jnp.where(ok & (j <= i), 0.0, masked_value).astype(f32)

    for start in range(0, tree_len, rows):
        stop = start + rows
        queries = split_heads(q_ref[start:stop, :])
        outs = []
        for h in range(2):
            scores = dot_nt(queries[h], k_ref[:stop, :]) + bias[start:stop, :stop]
            top = jnp.max(scores, axis=1, keepdims=True)
            weights = jnp.exp2((scores - top) * exp2_scale)
            total = jnp.sum(weights, axis=1, keepdims=True)
            outs.append(dot_nn(weights.astype(bf16), v_ref[:stop, :]) / total)
            lse = jnp.broadcast_to(top * exp2_scale + jnp.log2(total), (rows, 128))
            lse_ref[0, h : h + 1, start:stop] = jnp.transpose(lse)[0:1, :]
        lane = lax.broadcasted_iota(jnp.int32, (rows, 128), 1)
        o_ref[start:stop, :] = jnp.where(lane < HEAD_DIM, outs[0], outs[1]).astype(bf16)


def attention_forward(qkv, cols, rows):
    tree_len, width = qkv.shape
    pairs = width // 384
    tile = (tree_len, 128)
    return pl.pallas_call(
        attention_forward_kernel,
        name="attention_forward",
        out_shape=(
            jax.ShapeDtypeStruct((tree_len, width // 3), bf16),
            jax.ShapeDtypeStruct((pairs, 8, tree_len), f32),
        ),
        grid=(pairs,),
        in_specs=[
            pl.BlockSpec(tile, lambda p: (0, p)),
            pl.BlockSpec(tile, lambda p: (0, pairs + p)),
            pl.BlockSpec(tile, lambda p: (0, 2 * pairs + p)),
            pl.BlockSpec(cols.shape, lambda p: (0, 0)),
            pl.BlockSpec(rows.shape, lambda p: (0, 0)),
        ],
        out_specs=(
            pl.BlockSpec(tile, lambda p: (0, p)),
            pl.BlockSpec((1, 8, tree_len), lambda p: (p, 0, 0)),
        ),
        scratch_shapes=[pltpu.VMEM((tree_len, tree_len), f32)],
        compiler_params=pltpu.CompilerParams(vmem_limit_bytes=40 << 20),
        cost_estimate=pl.CostEstimate(
            flops=int(0.6 * 2 * pairs * 4 * tree_len * tree_len * 256),
            bytes_accessed=tree_len * width * 3,
            transcendentals=pairs * tree_len * tree_len,
        ),
    )(qkv, qkv, qkv, cols, rows)


def attention_backward_kernel(
    q_ref, k_ref, v_ref, do_ref, o_ref, lse_ref, col_ref, row_ref, dx_ref, bias, split_k, dk, dv
):
    tree_len = q_ref.shape[0]
    rows = block_rows(tree_len)
    pair = pl.program_id(0)
    pairs = pl.num_programs(0)

    @pl.when(pair == 0)
    def _():
        for start in range(0, tree_len, rows):
            stop = start + rows
            key_seg = col_ref[:stop, 0:1]
            ok = row_ref[0:1, start:stop] == key_seg
            ok = ok | (row_ref[1:2, start:stop] == key_seg)
            ok = ok | (row_ref[2:3, start:stop] == key_seg)
            j = lax.broadcasted_iota(jnp.int32, (stop, rows), 0)
            i = lax.broadcasted_iota(jnp.int32, (stop, rows), 1) + start
            bias[:stop, start:stop] = jnp.where(ok & (j <= i), 0.0, masked_value).astype(f32)

    split_k[0], split_k[1] = split_heads(k_ref[...])
    dk[...] = jnp.zeros_like(dk)
    dv[...] = jnp.zeros_like(dv)
    sub = lax.broadcasted_iota(jnp.int32, (8, 128), 0)
    lane = lax.broadcasted_iota(jnp.int32, (8, 128), 1)
    own = jnp.where(lane // HEAD_DIM == sub, 1.0, 0.0).astype(f32)
    for start in range(0, tree_len, rows):
        stop = start + rows
        queries = split_heads(q_ref[start:stop, :])
        grads = split_heads(do_ref[start:stop, :])
        product = do_ref[start:stop, :].astype(f32) * o_ref[start:stop, :].astype(f32)
        row_dot = lax.dot_general(
            own,
            product,
            (((1,), (1,)), ((), ())),
            precision=lax.Precision.HIGHEST,
            preferred_element_type=f32,
        )
        probs_low = []
        grad_scores = []
        for h in range(2):
            shift = bias[:stop, start:stop] - lse_ref[0, h : h + 1, start:stop]
            probs = jnp.exp2(dot_nt(k_ref[:stop, :], queries[h]) * exp2_scale + shift)
            grad_probs = dot_nt(v_ref[:stop, :], grads[h])
            probs_low.append(probs.astype(bf16))
            grad_scores.append((probs * (grad_probs - row_dot[h : h + 1, :])).astype(bf16))
        dv[:stop, :] += dot_nn(jnp.concatenate(probs_low, 1), jnp.concatenate(grads, 0))
        dk[:stop, :] += dot_nn(jnp.concatenate(grad_scores, 1), jnp.concatenate(queries, 0))
        dq = dot_tn(grad_scores[0], split_k[0, :stop, :])
        dq = dq + dot_tn(grad_scores[1], split_k[1, :stop, :])
        dq = (dq.astype(bf16).astype(f32) * grad_scale).astype(bf16)
        dx_ref[start:stop, pl.ds(pl.multiple_of(pair * 128, 128), 128)] = dq
    dx_ref[:, pl.ds(pl.multiple_of((pairs + pair) * 128, 128), 128)] = (
        dk[...] * grad_scale
    ).astype(bf16)
    dx_ref[:, pl.ds(pl.multiple_of((2 * pairs + pair) * 128, 128), 128)] = dv[...].astype(bf16)


def attention_backward(qkv, grad, out, lse, cols, rows):
    tree_len, width = qkv.shape
    pairs = width // 384
    tile = (tree_len, 128)
    return pl.pallas_call(
        attention_backward_kernel,
        name="attention_backward",
        out_shape=jax.ShapeDtypeStruct((tree_len, width), bf16),
        grid=(pairs,),
        in_specs=[
            pl.BlockSpec(tile, lambda p: (0, p)),
            pl.BlockSpec(tile, lambda p: (0, pairs + p)),
            pl.BlockSpec(tile, lambda p: (0, 2 * pairs + p)),
            pl.BlockSpec(tile, lambda p: (0, p)),
            pl.BlockSpec(tile, lambda p: (0, p)),
            pl.BlockSpec((1, 8, tree_len), lambda p: (p, 0, 0)),
            pl.BlockSpec(cols.shape, lambda p: (0, 0)),
            pl.BlockSpec(rows.shape, lambda p: (0, 0)),
        ],
        out_specs=pl.BlockSpec((tree_len, width), lambda p: (0, 0)),
        scratch_shapes=[
            pltpu.VMEM((tree_len, tree_len), f32),
            pltpu.VMEM((2, tree_len, 128), bf16),
            pltpu.VMEM(tile, f32),
            pltpu.VMEM(tile, f32),
        ],
        compiler_params=pltpu.CompilerParams(vmem_limit_bytes=40 << 20),
        cost_estimate=pl.CostEstimate(
            flops=int(0.6 * 5 * pairs * 4 * tree_len * tree_len * 256),
            bytes_accessed=tree_len * width * 6,
            transcendentals=pairs * tree_len * tree_len,
        ),
    )(qkv, qkv, qkv, grad, out, lse, cols, rows)


def norm_parts(values):
    centered = values - jnp.mean(values, axis=-1, keepdims=True)
    scale = lax.rsqrt(jnp.mean(centered * centered, axis=-1, keepdims=True) + norm_eps)
    return centered * scale, scale


def norm_forward(values, gain, shift):
    return norm_parts(values)[0] * gain + shift


def norm_backward(values, gain, grad):
    xhat, scale = norm_parts(values)
    h = grad * gain
    inner = h - jnp.mean(h, axis=-1, keepdims=True)
    inner = inner - xhat * jnp.mean(h * xhat, axis=-1, keepdims=True)
    return scale * inner, jnp.stack([jnp.sum(grad * xhat, axis=0), jnp.sum(grad, axis=0)])


def gelu_and_slope(values):
    square = values * values
    bent = jnp.tanh(gelu_scale * values * (1.0 + gelu_cubic * square))
    half = 0.5 + 0.5 * bent
    slope = half + 2.0 * gelu_scale * values * half * (1.0 - half) * (1.0 + 3.0 * gelu_cubic * square)
    return values * half, slope


def apart(position, distance):
    bit = 1
    while bit <= distance:
        if distance & bit:
            position = position + bit - 2 * bit * (position // bit % 2)
        bit *= 2
    return position


def gather_kernel(chunks, weights, moved, *refs):
    shards, refs = refs[:weights], refs[weights:]
    tokens, segments, refs = refs[0], refs[1], refs[2:]
    tp = lax.axis_size("tp")
    depth = lax.axis_size("z")
    outs, refs = refs[: weights * tp], refs[weights * tp :]
    segments_out, refs = refs[0], refs[1:]
    tokens_out, refs = (refs[0], refs[1:]) if moved else (None, refs)
    send_sems, recv_sems, local_sems = refs
    z, y, core, x = (lax.axis_index(name) for name in ("z", "y", "core", "tp"))

    barrier = pltpu.get_barrier_semaphore()
    partners = [{"z": apart(z, k)} for k in range(1, depth)]
    partners += [{"tp": apart(x, k)} for k in range(1, tp)]
    partners += [{"y": 1 - y}, {"core": 1 - core}]
    for partner in partners:
        pl.semaphore_signal(barrier, inc=1, device_id=partner, device_id_type=pl.DeviceIdType.MESH)
    pl.semaphore_wait(barrier, len(partners))

    half = depth // 2
    first = pl.ds(z // half * half, half)
    second = pl.ds(half - z // half * half, half)
    started = []

    def copy(source, target, partner):
        slot = len(started)
        made = pltpu.make_async_remote_copy(
            src_ref=source,
            dst_ref=target,
            send_sem=send_sems.at[slot],
            recv_sem=recv_sems.at[slot],
            device_id=partner,
            device_id_type=pl.DeviceIdType.MESH,
        )
        made.start()
        started.append(made)
        return made

    crossed = []
    for k in range(1, tp):
        partner = {"tp": apart(x, k)}
        crossed.append(copy(segments, segments_out.at[k - 1], partner))
        for n in range(moved):
            target = tokens_out.at[n * (tp - 1) + k - 1]
            crossed.append(copy(tokens.at[n * tp + apart(x, k)], target, partner))

    def part(number, t, at_y, span):
        weight, low, rows = chunks[number]
        return outs[weight * tp + t].at[span, at_y, core, pl.ds(low, rows)]

    def along_z(number):
        weight, low, rows = chunks[number]
        own = shards[weight].at[pl.ds(low, rows)]
        target = outs[weight * tp].at[z, y, core, pl.ds(low, rows)]
        keep = pltpu.make_async_copy(own, target, local_sems.at[number])
        keep.start()
        return keep, [copy(own, target, {"z": apart(z, k)}) for k in range(1, depth)]

    def over(number, t, target_t, at_y, span, partner):
        return copy(part(number, t, at_y, span), part(number, target_t, at_y, span), partner)

    def to_core(number, t, at_y, span):
        crossed.append(over(number, t, t, at_y, span, {"core": 1 - core}))

    def plane_start(number, keep, sent):
        keep.wait()
        for k in range(1, half):
            sent[k - 1].wait_recv()
        over_x = [over(number, 0, k, y, first, {"tp": apart(x, k)}) for k in range(1, tp)]
        for k in range(half, depth):
            sent[k - 1].wait_recv()
        over_y = over(number, 0, 0, y, second, {"y": 1 - y})
        last = [(over(number, 0, 0, y, first, {"y": 1 - y}), 0, 1 - y, first)]
        for k in range(1, tp):
            made = over(number, 0, k, y, second, {"tp": apart(x, k)})
            last.append((made, k, y, second))
        to_core(number, 0, y, first)
        to_core(number, 0, y, second)
        return over_x, over_y, last

    def plane_turn(number, over_x, over_y, last):
        for k in range(1, tp):
            over_x[k - 1].wait_recv()
            made = over(number, k, k, y, first, {"y": 1 - y})
            last.append((made, k, 1 - y, first))
            to_core(number, k, y, first)
        over_y.wait_recv()
        for k in range(1, tp):
            made = over(number, 0, k, 1 - y, second, {"tp": apart(x, k)})
            last.append((made, k, 1 - y, second))
        to_core(number, 0, 1 - y, second)
        return last

    def plane_end(number, last):
        for made, t, at_y, span in last:
            made.wait_recv()
            to_core(number, t, at_y, span)

    count = len(chunks)
    state = {0: along_z(0)}
    for step in range(count + 2):
        if step < count:
            state[step] = plane_start(step, *state[step])
            if step + 1 < count:
                state[step + 1] = along_z(step + 1)
        if 0 <= step - 1 < count:
            state[step - 1] = plane_turn(step - 1, *state[step - 1])
        if 0 <= step - 2 < count:
            plane_end(step - 2, state[step - 2])
    for made in crossed:
        made.wait_recv()
    for made in started:
        made.wait_send()


def gather_weights(shards, pieces, tokens, segments):
    tp = lax.axis_size("tp")
    depth = lax.axis_size("z")
    moved = tokens.shape[0] // tp
    chunks = []
    for number, (shard, split) in enumerate(zip(shards, pieces)):
        rows = shard.shape[0] // split
        chunks += [(number, piece * rows, rows) for piece in range(split)]
    copies = len(chunks) * (depth + 1 + 4 * (tp - 1) + 4 * tp)
    copies += (moved + 1) * (tp - 1)
    shapes = [
        jax.ShapeDtypeStruct((depth, 2, 2) + shard.shape, shard.dtype)
        for shard in shards
        for _ in range(tp)
    ]
    sent = sum(shape.size for shape in shapes) * 2
    shapes += [jax.ShapeDtypeStruct((tp - 1,) + segments.shape, segments.dtype)]
    if moved:
        shapes += [jax.ShapeDtypeStruct((moved * (tp - 1),) + tokens.shape[1:], tokens.dtype)]
    inside = pl.BlockSpec(memory_space=pltpu.VMEM)
    outside = pl.BlockSpec(memory_space=pl.ANY)
    made = pl.pallas_call(
        functools.partial(gather_kernel, chunks, len(shards), moved),
        name="gather_weights",
        out_shape=shapes,
        in_specs=[inside] * len(shards) + [outside, inside],
        out_specs=[outside] * len(shapes),
        scratch_shapes=[
            pltpu.SemaphoreType.DMA((copies,)),
            pltpu.SemaphoreType.DMA((copies,)),
            pltpu.SemaphoreType.DMA((len(chunks),)),
        ],
        compiler_params=pltpu.CompilerParams(collective_id=0, has_side_effects=True),
        cost_estimate=pl.CostEstimate(flops=0, bytes_accessed=2 * sent, transcendentals=0),
    )(*shards, tokens, segments)
    count = len(shards) * tp
    full = [array.reshape(-1, array.shape[-1]) for array in made[:count]]
    full = [full[number * tp : (number + 1) * tp] for number in range(len(shards))]
    crossed = made[count:]
    came = [crossed[1][number] for number in range(moved * (tp - 1))] if moved else []
    return full, [crossed[0][k] for k in range(tp - 1)], came


def send(values, axes, distance):
    count = 1
    for axis in (axes,) if isinstance(axes, str) else axes:
        count *= lax.axis_size(axis)
    return lax.ppermute(values, axes, [(s, s ^ distance) for s in range(count)])


def after(values, *others):
    return lax.optimization_barrier((values,) + others)[0]


def pick(pieces, position):
    chosen = pieces[0]
    for number in range(1, len(pieces)):
        chosen = jnp.where(position == number, pieces[number], chosen)
    return chosen


def exchange_tp(pieces):
    return pieces[:1] + [send(pieces[k], "tp", k) for k in range(1, len(pieces))]


def in_place_order(pieces):
    here = lax.axis_index("tp")
    return jnp.concatenate([pick(pieces, here ^ s) for s in range(len(pieces))], axis=0)


def sum_everywhere(values):
    for axes in (("y", "tp"), ("z",), ("core",)):
        count = 1
        for axis in axes:
            count *= lax.axis_size(axis)
        values = sum([send(values, axes, k) for k in range(1, count)], values)
    return values


def block_at(values, axis, index):
    return lax.dynamic_index_in_dim(values, index, axis, keepdims=False)


def scatter_core(part):
    depth, core = lax.axis_size("z"), lax.axis_index("core")
    blocks = part.reshape(depth, 2, 2, -1, part.shape[1])
    came = send(block_at(blocks, 2, 1 - core), "core", 1)
    return (block_at(blocks, 2, core).astype(f32) + came.astype(f32)).astype(bf16)


def scatter_plane(parts):
    y = lax.axis_index("y")
    straight, across = [block_at(parts[0], 1, y)], []
    for t in range(len(parts)):
        for j in range(2):
            if t or j:
                came = send(block_at(parts[t], 1, y ^ j), ("y", "tp"), j * len(parts) + t)
                (across if t and j else straight).append(came)
    return straight, across


def total(pieces):
    return sum([piece.astype(f32) for piece in pieces[1:]], pieces[0].astype(f32)).astype(bf16)


def scatter_z(part):
    z = lax.axis_index("z")
    made = block_at(part, 0, z).astype(f32)
    for k in range(1, part.shape[0]):
        made = made + send(block_at(part, 0, z ^ k), "z", k).astype(f32)
    return made


def segment_tables(segments, parents):
    labels = jnp.arange(parents.shape[0], dtype=jnp.int32)
    up = lambda seg: jnp.sum(jnp.where(seg[:, None] == labels, parents, 0), axis=1)
    parent = up(segments)
    table = jnp.stack([segments, parent, up(parent)])
    return jnp.pad(table.T, ((0, 0), (0, 5))), jnp.pad(table, ((0, 5), (0, 0)))


def on_device(
    tokens, segments, parents, norm_gains, norm_biases, w_qkv, w_out, w_up, w_down, cotangent
):
    tp = lax.axis_size("tp")
    here = lax.axis_index("tp")
    micro = tokens.shape[0]
    own_rows = tokens.shape[2]
    width = tokens.shape[3]
    head_width = w_out.shape[0]
    tree_len = own_rows * tp
    whole = micro // tp
    shared = list(range(whole * tp, micro))
    share_count = len(shared)
    halves = range(tp)
    split = whole * tree_len

    def outgoing(values):
        return [block_at(values, 0, n * tp + (here ^ k)) for n in range(whole) for k in range(1, tp)]

    def whole_trees(values, came):
        rows = []
        for n in range(whole):
            near = [block_at(values, 0, n * tp + here)]
            rows.append(in_place_order(near + came[n * (tp - 1) : (n + 1) * (tp - 1)]))
        return rows

    def rows_back(values):
        trees = values.reshape(micro, own_rows, width)
        back = []
        for n in range(whole):
            pieces = [block_at(trees, 0, n * tp + here)]
            for k in range(1, tp):
                low = block_at(trees, 0, n * tp + (here ^ k)).astype(bf16)
                pieces.append(send(low, "tp", k).astype(values.dtype))
            back += [pick(pieces, here ^ s) for s in halves]
        return jnp.stack(back + [trees[m] for m in shared])[:, None]

    def share_rows(values, k):
        return lax.dynamic_slice_in_dim(values, (here ^ k) * own_rows, own_rows)

    shard_qkv = w_qkv.reshape(w_qkv.shape[0], -1)
    (full_qkv, full_out, full_up), seg_came, tokens_came = gather_weights(
        [shard_qkv, w_out.T, w_up], [4, 1, 4], tokens[:, 0], segments[:, 0]
    )
    down = lax.all_gather(
        after(w_down.T, full_qkv[0]), ("tp", "z", "y", "core"), axis=0, tiled=True
    ).reshape(tp, width, -1)
    full_down = [pick([down[s] for s in halves], here ^ t) for t in halves]
    seg_came = [segments[:, 0]] + seg_came
    seg_all = jnp.concatenate([pick(seg_came, here ^ s) for s in halves], axis=1)
    rows = whole_trees(tokens[:, 0], tokens_came) + [tokens[m, 0] for m in shared]
    x = lax.optimization_barrier(jnp.concatenate(rows, axis=0)).astype(f32)
    whole_tables = []
    for n in range(whole):
        seg = pick([seg_all[n * tp + s] for s in halves], here)
        par = pick([parents[n * tp + s, 0] for s in halves], here)
        whole_tables.append(segment_tables(seg, par))
    share_tables = [segment_tables(seg_all[m], parents[m, 0]) for m in shared]

    normed = norm_forward(x, norm_gains[0], norm_biases[0]).astype(bf16)
    normed_whole = normed[:split]
    share_qkv = [dot_nn(normed[split:], w).astype(bf16) for w in full_qkv]
    whole_qkv = [dot_nn(normed_whole, w).astype(bf16) for w in full_qkv] if whole else []
    share_calls = []
    for n in range(share_count):
        cut = slice(n * own_rows, (n + 1) * own_rows)
        share_calls.append(in_place_order(exchange_tp([part[cut] for part in share_qkv])))
    whole_out = [[] for _ in halves]
    share_out = [[] for _ in halves]
    saved = {}
    for n in range(whole):
        for t in halves:
            qkv = whole_qkv[t][n * tree_len : (n + 1) * tree_len]
            out, lse = attention_forward(qkv, *whole_tables[n])
            saved[n, t] = (qkv, out, lse)
            whole_out[t].append(out)
    share_calls = [after(call, *whole_out[0]) for call in share_calls]
    for n in range(share_count):
        out, lse = attention_forward(share_calls[n], *share_tables[n])
        saved[n] = (share_calls[n], out, lse)
        parts = exchange_tp([share_rows(out, k) for k in halves])
        for t in halves:
            share_out[t].append(parts[t])
    attended = [jnp.concatenate(whole_out[t] + share_out[t], axis=0) for t in halves]
    cotangent = after(cotangent[:, 0], *attended)
    cotangent_came = [send(piece, "tp", n % (tp - 1) + 1) for n, piece in enumerate(outgoing(cotangent))]
    branch_a = sum(dot_nt(attended[t], full_out[t]) for t in halves)
    residual = x + norm_forward(branch_a, norm_gains[1], norm_biases[1])

    normed_f = norm_forward(residual, norm_gains[2], norm_biases[2]).astype(bf16)
    hidden = []
    slope = []
    for t in halves:
        values, bent = gelu_and_slope(dot_nn(normed_f, full_up[t]))
        values, bent = lax.optimization_barrier((values.astype(bf16), bent.astype(bf16)))
        hidden.append(values)
        slope.append(bent)
    normed_shared = []
    for n in range(share_count):
        start = split + n * own_rows
        near = after(normed[start : start + own_rows], hidden[0])
        normed_shared.append(in_place_order(exchange_tp([near] * tp)))
    branch_f = sum(dot_nt(hidden[t], full_down[t]) for t in halves)
    out = (residual + norm_forward(branch_f, norm_gains[3], norm_biases[3])).astype(bf16)
    out_rows = rows_back(out)

    grad_out = whole_trees(cotangent, cotangent_came) + [cotangent[m] for m in shared]
    grad_out = lax.optimization_barrier(jnp.concatenate(grad_out, axis=0)).astype(f32)
    grad_branch_f, sums_3 = norm_backward(branch_f, norm_gains[3], grad_out)
    grad_branch_f = grad_branch_f.astype(bf16)
    core_down = [scatter_core(dot_tn(grad_branch_f, hidden[t]).astype(bf16)) for t in halves]
    grad_up = [
        (dot_nn(grad_branch_f, full_down[t]) * slope[t].astype(f32)).astype(bf16) for t in halves
    ]
    grad_up = [after(values, *core_down) for values in grad_up]
    straight_down, across_down = scatter_plane(core_down)
    dw_up = [dot_tn(normed_f, grad_up[t]).astype(bf16) for t in halves]
    core_up = [scatter_core(part) for part in dw_up]
    grad_up = [after(values, *dw_up) for values in grad_up]
    grad_up[1:] = [after(values, *straight_down) for values in grad_up[1:]]
    grad_normed_f = sum(dot_nt(grad_up[t], full_up[t]) for t in halves)
    grad_part, sums_2 = norm_backward(residual, norm_gains[2], grad_normed_f)
    grad_residual = grad_out + grad_part

    grad_branch_a, sums_1 = norm_backward(branch_a, norm_gains[1], grad_residual)
    grad_branch_a = after(grad_branch_a.astype(bf16), *core_up, *across_down)
    z_down = scatter_z(total(straight_down + across_down))
    straight_up, across_up = scatter_plane(core_up)
    share_grad = [dot_nn(grad_branch_a[split:], w).astype(bf16) for w in full_out]
    whole_grad = [dot_nn(grad_branch_a[:split], w).astype(bf16) for w in full_out] if whole else []
    share_do = []
    for n in range(share_count):
        cut = slice(n * own_rows, (n + 1) * own_rows)
        share_do.append(in_place_order(exchange_tp([part[cut] for part in share_grad])))
    core_out = [scatter_core(dot_tn(grad_branch_a, part).astype(bf16)) for part in attended]
    grad_qkv = [[] for _ in halves]

    def whole_backward(t, *others):
        for n in range(whole):
            qkv, att, lse = saved[n, t]
            do = after(whole_grad[t][n * tree_len : (n + 1) * tree_len], *share_grad)
            made = attention_backward(qkv, after(do, *others), att, lse, *whole_tables[n])
            grad_qkv[t].append(made)
        return grad_qkv[t]

    made = []
    dw_qkv = [None] * tp
    for t in range(1, tp):
        made += whole_backward(t)
        if whole:
            dw_qkv[t] = dot_tn(normed_whole, jnp.concatenate(grad_qkv[t], axis=0)).astype(bf16)
        else:
            dw_qkv[t] = jnp.zeros(full_qkv[t].shape, bf16)
    core_qkv = [None] + [scatter_core(part) for part in dw_qkv[1:]]
    grad_shared = []
    own_part = []
    for n in range(share_count):
        qkv, att, lse = saved[n]
        do = after(share_do[n], *made)
        dx = attention_backward(qkv, do, att, lse, *share_tables[n])
        made = [dx]
        grad_shared.append(dx)
    whole_backward(0, *core_out, *straight_up, *core_qkv[1:], *made)
    for n in range(share_count):
        part = dot_nt(grad_shared[n], full_qkv[0])
        pieces = exchange_tp([share_rows(part, 0)] + [share_rows(part, k).astype(bf16) for k in halves[1:]])
        own_part.append(sum([piece.astype(f32) for piece in pieces[1:]], pieces[0]))
    straight_out, across_out = scatter_plane(core_out)
    ready = [*across_up, z_down]
    owned = [after(rows, *ready) for rows in grad_shared]
    z_up = scatter_z(total(straight_up + across_up))
    z_out = scatter_z(total(straight_out + across_out))
    owned = [dot_tn(rows, grad) for rows, grad in zip(normed_shared, owned)]
    if whole:
        owned.append(dot_tn(normed_whole, jnp.concatenate(grad_qkv[0], axis=0)))
    dw_qkv[0] = sum(owned).astype(bf16)
    core_qkv[0] = scatter_core(dw_qkv[0])
    straight_qkv, across_qkv = scatter_plane(core_qkv)
    z_qkv = scatter_z(total(straight_qkv + across_qkv))
    ready = [dw_qkv[0], *across_qkv, *straight_out, *across_out]
    grad_normed = list(own_part)
    if whole:
        trees = [after(jnp.concatenate(grad_qkv[t], axis=0), *ready) for t in halves]
        trees[1:] = [after(rows, core_qkv[0]) for rows in trees[1:]]
        grad_normed = [sum(dot_nt(trees[t], full_qkv[t]) for t in halves)] + grad_normed
    grad_normed = jnp.concatenate(grad_normed, axis=0)
    grad_part, sums_0 = norm_backward(x, norm_gains[0], grad_normed)
    input_rows = rows_back(grad_residual + grad_part)
    sums = jnp.concatenate([sums_0, sums_1, sums_2, sums_3])
    sums = sum_everywhere(sums).reshape(4, 2, width)
    return (
        out_rows,
        input_rows,
        z_qkv.reshape(w_qkv.shape),
        z_out.T,
        z_up,
        z_down.T,
        sums[:, 0],
        sums[:, 1],
    )


def solution(mesh):
    groups, tp = mesh.devices.shape
    fine = jax.sharding.Mesh(mesh.devices.reshape(groups // 4, 2, 2, tp), ("z", "y", "core", "tp"))
    fsdp = ("z", "y", "core")
    in_specs = (
        P(None, fsdp, "tp", None),
        P(None, fsdp, "tp"),
        P(None, fsdp, None),
        P(),
        P(),
        P(fsdp, None, "tp"),
        P("tp", fsdp),
        P(fsdp, "tp"),
        P("tp", fsdp),
        P(None, fsdp, "tp", None),
    )
    out_specs = (
        P(None, fsdp, "tp", None),
        P(None, fsdp, "tp", None),
        P(fsdp, None, "tp"),
        P("tp", fsdp),
        P(fsdp, "tp"),
        P("tp", fsdp),
        P(),
        P(),
    )
    return jax.shard_map(
        on_device, mesh=fine, in_specs=in_specs, out_specs=out_specs, check_vma=False
    )
```

```python
import functools
import math

import jax
import jax.numpy as jnp
from jax import lax
from jax.experimental import pallas as pl
from jax.experimental.pallas import tpu as pltpu
from jax.sharding import PartitionSpec as P

HEAD_DIM = 64
norm_eps = 1e-05
masked_value = -1e30
f32 = jnp.float32
bf16 = jnp.bfloat16
exp2_scale = math.log2(math.e) / math.sqrt(HEAD_DIM)
grad_scale = 1.0 / math.sqrt(HEAD_DIM)
gelu_scale = math.sqrt(2.0 / math.pi)
gelu_cubic = 0.044715


def dot_nn(a, b):
    return lax.dot_general(a, b, (((1,), (0,)), ((), ())), preferred_element_type=f32)


def dot_nt(a, b):
    return lax.dot_general(a, b, (((1,), (1,)), ((), ())), preferred_element_type=f32)


def dot_tn(a, b):
    return lax.dot_general(a, b, (((0,), (0,)), ((), ())), preferred_element_type=f32)


def split_heads(x):
    lane = lax.broadcasted_iota(jnp.int32, x.shape, 1)
    zero = jnp.zeros_like(x)
    return jnp.where(lane < HEAD_DIM, x, zero), jnp.where(lane >= HEAD_DIM, x, zero)


def block_rows(tree_len):
    return 256 if tree_len % 256 == 0 else 128


def attention_forward_kernel(q_ref, k_ref, v_ref, col_ref, row_ref, o_ref, lse_ref, bias):
    tree_len = q_ref.shape[0]
    rows = block_rows(tree_len)

    @pl.when(pl.program_id(0) == 0)
    def _():
        for start in range(0, tree_len, rows):
            stop = start + rows
            key_seg = row_ref[0:1, :stop]
            ok = col_ref[start:stop, 0:1] == key_seg
            ok = ok | (col_ref[start:stop, 1:2] == key_seg)
            ok = ok | (col_ref[start:stop, 2:3] == key_seg)
            i = lax.broadcasted_iota(jnp.int32, (rows, stop), 0) + start
            j = lax.broadcasted_iota(jnp.int32, (rows, stop), 1)
            bias[start:stop, :stop] = jnp.where(ok & (j <= i), 0.0, masked_value).astype(f32)

    for start in range(0, tree_len, rows):
        stop = start + rows
        queries = split_heads(q_ref[start:stop, :])
        outs = []
        for h in range(2):
            scores = dot_nt(queries[h], k_ref[:stop, :]) + bias[start:stop, :stop]
            top = jnp.max(scores, axis=1, keepdims=True)
            weights = jnp.exp2((scores - top) * exp2_scale)
            total = jnp.sum(weights, axis=1, keepdims=True)
            outs.append(dot_nn(weights.astype(bf16), v_ref[:stop, :]) / total)
            lse = jnp.broadcast_to(top * exp2_scale + jnp.log2(total), (rows, 128))
            lse_ref[0, h : h + 1, start:stop] = jnp.transpose(lse)[0:1, :]
        lane = lax.broadcasted_iota(jnp.int32, (rows, 128), 1)
        o_ref[start:stop, :] = jnp.where(lane < HEAD_DIM, outs[0], outs[1]).astype(bf16)


def attention_forward(qkv, cols, rows):
    tree_len, width = qkv.shape
    pairs = width // 384
    tile = (tree_len, 128)
    return pl.pallas_call(
        attention_forward_kernel,
        name="attention_forward",
        out_shape=(
            jax.ShapeDtypeStruct((tree_len, width // 3), bf16),
            jax.ShapeDtypeStruct((pairs, 8, tree_len), f32),
        ),
        grid=(pairs,),
        in_specs=[
            pl.BlockSpec(tile, lambda p: (0, p)),
            pl.BlockSpec(tile, lambda p: (0, pairs + p)),
            pl.BlockSpec(tile, lambda p: (0, 2 * pairs + p)),
            pl.BlockSpec(cols.shape, lambda p: (0, 0)),
            pl.BlockSpec(rows.shape, lambda p: (0, 0)),
        ],
        out_specs=(
            pl.BlockSpec(tile, lambda p: (0, p)),
            pl.BlockSpec((1, 8, tree_len), lambda p: (p, 0, 0)),
        ),
        scratch_shapes=[pltpu.VMEM((tree_len, tree_len), f32)],
        compiler_params=pltpu.CompilerParams(vmem_limit_bytes=40 << 20),
        cost_estimate=pl.CostEstimate(
            flops=int(0.6 * 2 * pairs * 4 * tree_len * tree_len * 256),
            bytes_accessed=tree_len * width * 3,
            transcendentals=pairs * tree_len * tree_len,
        ),
    )(qkv, qkv, qkv, cols, rows)


def attention_backward_kernel(
    q_ref, k_ref, v_ref, do_ref, o_ref, lse_ref, col_ref, row_ref, dx_ref, bias, split_k, dk, dv
):
    tree_len = q_ref.shape[0]
    rows = block_rows(tree_len)
    pair = pl.program_id(0)
    pairs = pl.num_programs(0)

    @pl.when(pair == 0)
    def _():
        for start in range(0, tree_len, rows):
            stop = start + rows
            key_seg = col_ref[:stop, 0:1]
            ok = row_ref[0:1, start:stop] == key_seg
            ok = ok | (row_ref[1:2, start:stop] == key_seg)
            ok = ok | (row_ref[2:3, start:stop] == key_seg)
            j = lax.broadcasted_iota(jnp.int32, (stop, rows), 0)
            i = lax.broadcasted_iota(jnp.int32, (stop, rows), 1) + start
            bias[:stop, start:stop] = jnp.where(ok & (j <= i), 0.0, masked_value).astype(f32)

    split_k[0], split_k[1] = split_heads(k_ref[...])
    dk[...] = jnp.zeros_like(dk)
    dv[...] = jnp.zeros_like(dv)
    sub = lax.broadcasted_iota(jnp.int32, (8, 128), 0)
    lane = lax.broadcasted_iota(jnp.int32, (8, 128), 1)
    own = jnp.where(lane // HEAD_DIM == sub, 1.0, 0.0).astype(f32)
    for start in range(0, tree_len, rows):
        stop = start + rows
        queries = split_heads(q_ref[start:stop, :])
        grads = split_heads(do_ref[start:stop, :])
        product = do_ref[start:stop, :].astype(f32) * o_ref[start:stop, :].astype(f32)
        row_dot = lax.dot_general(
            own,
            product,
            (((1,), (1,)), ((), ())),
            precision=lax.Precision.HIGHEST,
            preferred_element_type=f32,
        )
        probs_low = []
        grad_scores = []
        for h in range(2):
            shift = bias[:stop, start:stop] - lse_ref[0, h : h + 1, start:stop]
            probs = jnp.exp2(dot_nt(k_ref[:stop, :], queries[h]) * exp2_scale + shift)
            grad_probs = dot_nt(v_ref[:stop, :], grads[h])
            probs_low.append(probs.astype(bf16))
            grad_scores.append((probs * (grad_probs - row_dot[h : h + 1, :])).astype(bf16))
        dv[:stop, :] += dot_nn(jnp.concatenate(probs_low, 1), jnp.concatenate(grads, 0))
        dk[:stop, :] += dot_nn(jnp.concatenate(grad_scores, 1), jnp.concatenate(queries, 0))
        dq = dot_tn(grad_scores[0], split_k[0, :stop, :])
        dq = dq + dot_tn(grad_scores[1], split_k[1, :stop, :])
        dq = (dq.astype(bf16).astype(f32) * grad_scale).astype(bf16)
        dx_ref[start:stop, pl.ds(pl.multiple_of(pair * 128, 128), 128)] = dq
    dx_ref[:, pl.ds(pl.multiple_of((pairs + pair) * 128, 128), 128)] = (
        dk[...] * grad_scale
    ).astype(bf16)
    dx_ref[:, pl.ds(pl.multiple_of((2 * pairs + pair) * 128, 128), 128)] = dv[...].astype(bf16)


def attention_backward(qkv, grad, out, lse, cols, rows):
    tree_len, width = qkv.shape
    pairs = width // 384
    tile = (tree_len, 128)
    return pl.pallas_call(
        attention_backward_kernel,
        name="attention_backward",
        out_shape=jax.ShapeDtypeStruct((tree_len, width), bf16),
        grid=(pairs,),
        in_specs=[
            pl.BlockSpec(tile, lambda p: (0, p)),
            pl.BlockSpec(tile, lambda p: (0, pairs + p)),
            pl.BlockSpec(tile, lambda p: (0, 2 * pairs + p)),
            pl.BlockSpec(tile, lambda p: (0, p)),
            pl.BlockSpec(tile, lambda p: (0, p)),
            pl.BlockSpec((1, 8, tree_len), lambda p: (p, 0, 0)),
            pl.BlockSpec(cols.shape, lambda p: (0, 0)),
            pl.BlockSpec(rows.shape, lambda p: (0, 0)),
        ],
        out_specs=pl.BlockSpec((tree_len, width), lambda p: (0, 0)),
        scratch_shapes=[
            pltpu.VMEM((tree_len, tree_len), f32),
            pltpu.VMEM((2, tree_len, 128), bf16),
            pltpu.VMEM(tile, f32),
            pltpu.VMEM(tile, f32),
        ],
        compiler_params=pltpu.CompilerParams(vmem_limit_bytes=40 << 20),
        cost_estimate=pl.CostEstimate(
            flops=int(0.6 * 5 * pairs * 4 * tree_len * tree_len * 256),
            bytes_accessed=tree_len * width * 6,
            transcendentals=pairs * tree_len * tree_len,
        ),
    )(qkv, qkv, qkv, grad, out, lse, cols, rows)


def norm_parts(values):
    centered = values - jnp.mean(values, axis=-1, keepdims=True)
    scale = lax.rsqrt(jnp.mean(centered * centered, axis=-1, keepdims=True) + norm_eps)
    return centered * scale, scale


def norm_forward(values, gain, shift):
    return norm_parts(values)[0] * gain + shift


def norm_backward(values, gain, grad):
    xhat, scale = norm_parts(values)
    h = grad * gain
    inner = h - jnp.mean(h, axis=-1, keepdims=True)
    inner = inner - xhat * jnp.mean(h * xhat, axis=-1, keepdims=True)
    return scale * inner, jnp.stack([jnp.sum(grad * xhat, axis=0), jnp.sum(grad, axis=0)])


def gelu_and_slope(values):
    square = values * values
    bent = jnp.tanh(values * (gelu_scale + gelu_scale * gelu_cubic * square))
    half = 0.5 + 0.5 * bent
    made = values * half
    slope = half + made * (1.0 - half) * (2.0 * gelu_scale + 6.0 * gelu_scale * gelu_cubic * square)
    return made, slope


def apart(position, distance):
    bit = 1
    while bit <= distance:
        if distance & bit:
            position = position + bit - 2 * bit * (position // bit % 2)
        bit *= 2
    return position


def gather_kernel(chunks, weights, moved, *refs):
    shards, refs = refs[:weights], refs[weights:]
    tokens, segments, refs = refs[0], refs[1], refs[2:]
    tp = lax.axis_size("tp")
    depth = lax.axis_size("z")
    outs, refs = refs[: weights * tp], refs[weights * tp :]
    segments_out, refs = refs[0], refs[1:]
    tokens_out, refs = (refs[0], refs[1:]) if moved else (None, refs)
    send_sems, recv_sems, local_sems = refs
    z, y, core, x = (lax.axis_index(name) for name in ("z", "y", "core", "tp"))

    barrier = pltpu.get_barrier_semaphore()
    partners = [{"z": apart(z, k)} for k in range(1, depth)]
    partners += [{"tp": apart(x, k)} for k in range(1, tp)]
    partners += [{"y": 1 - y}, {"core": 1 - core}]
    for partner in partners:
        pl.semaphore_signal(barrier, inc=1, device_id=partner, device_id_type=pl.DeviceIdType.MESH)
    pl.semaphore_wait(barrier, len(partners))

    half = depth // 2
    everything = pl.ds(0, depth)
    started = []

    def spans(number):
        if number % 3:
            return everything, None
        return pl.ds(z // half * half, half), pl.ds(half - z // half * half, half)

    def copy(source, target, partner):
        slot = len(started)
        made = pltpu.make_async_remote_copy(
            src_ref=source,
            dst_ref=target,
            send_sem=send_sems.at[slot],
            recv_sem=recv_sems.at[slot],
            device_id=partner,
            device_id_type=pl.DeviceIdType.MESH,
        )
        made.start()
        started.append(made)
        return made

    crossed = []
    for k in range(1, tp):
        partner = {"tp": apart(x, k)}
        crossed.append(copy(segments, segments_out.at[k - 1], partner))
        for n in range(moved):
            target = tokens_out.at[n * (tp - 1) + k - 1]
            crossed.append(copy(tokens.at[n * tp + apart(x, k)], target, partner))

    def part(number, t, at_y, span):
        weight, low, rows = chunks[number]
        return outs[weight * tp + t].at[span, at_y, core, pl.ds(low, rows)]

    def along_z(number):
        weight, low, rows = chunks[number]
        own = shards[weight].at[pl.ds(low, rows)]
        target = outs[weight * tp].at[z, y, core, pl.ds(low, rows)]
        keep = pltpu.make_async_copy(own, target, local_sems.at[number])
        keep.start()
        return keep, [copy(own, target, {"z": apart(z, k)}) for k in range(1, depth)]

    def over(number, t, target_t, at_y, span, partner):
        return copy(part(number, t, at_y, span), part(number, target_t, at_y, span), partner)

    def to_core(number, t, at_y, span):
        crossed.append(over(number, t, t, at_y, span, {"core": 1 - core}))

    def plane_start(number, keep, sent):
        first, second = spans(number)
        keep.wait()
        for k in range(1, half if second is not None else depth):
            sent[k - 1].wait_recv()
        over_x = [over(number, 0, k, y, first, {"tp": apart(x, k)}) for k in range(1, tp)]
        last = [(over(number, 0, 0, y, first, {"y": 1 - y}), 0, 1 - y, first)]
        to_core(number, 0, y, first)
        if second is None:
            return over_x, None, last
        for k in range(half, depth):
            sent[k - 1].wait_recv()
        over_y = over(number, 0, 0, y, second, {"y": 1 - y})
        for k in range(1, tp):
            made = over(number, 0, k, y, second, {"tp": apart(x, k)})
            last.append((made, k, y, second))
        to_core(number, 0, y, second)
        return over_x, over_y, last

    def plane_turn(number, over_x, over_y, last):
        first, second = spans(number)
        for k in range(1, tp):
            over_x[k - 1].wait_recv()
            made = over(number, k, k, y, first, {"y": 1 - y})
            last.append((made, k, 1 - y, first))
            to_core(number, k, y, first)
        if second is None:
            return last
        over_y.wait_recv()
        for k in range(1, tp):
            made = over(number, 0, k, 1 - y, second, {"tp": apart(x, k)})
            last.append((made, k, 1 - y, second))
        to_core(number, 0, 1 - y, second)
        return last

    def plane_end(number, last):
        for made, t, at_y, span in last:
            made.wait_recv()
            to_core(number, t, at_y, span)

    count = len(chunks)
    state = {0: along_z(0)}
    for step in range(count + 2):
        if step < count:
            state[step] = plane_start(step, *state[step])
            if step + 1 < count:
                state[step + 1] = along_z(step + 1)
        if 0 <= step - 1 < count:
            state[step - 1] = plane_turn(step - 1, *state[step - 1])
        if 0 <= step - 2 < count:
            plane_end(step - 2, state[step - 2])
    for made in crossed:
        made.wait_recv()
    for made in started:
        made.wait_send()


def gather_weights(shards, pieces, tokens, segments):
    tp = lax.axis_size("tp")
    depth = lax.axis_size("z")
    moved = tokens.shape[0] // tp
    chunks = []
    for number, (shard, split) in enumerate(zip(shards, pieces)):
        rows = shard.shape[0] // split
        chunks += [(number, piece * rows, rows) for piece in range(split)]
    copies = len(chunks) * (depth + 1 + 4 * (tp - 1) + 4 * tp)
    copies += (moved + 1) * (tp - 1)
    shapes = [
        jax.ShapeDtypeStruct((depth, 2, 2) + shard.shape, shard.dtype)
        for shard in shards
        for _ in range(tp)
    ]
    sent = sum(shape.size for shape in shapes) * 2
    shapes += [jax.ShapeDtypeStruct((tp - 1,) + segments.shape, segments.dtype)]
    if moved:
        shapes += [jax.ShapeDtypeStruct((moved * (tp - 1),) + tokens.shape[1:], tokens.dtype)]
    inside = pl.BlockSpec(memory_space=pltpu.VMEM)
    outside = pl.BlockSpec(memory_space=pl.ANY)
    made = pl.pallas_call(
        functools.partial(gather_kernel, chunks, len(shards), moved),
        name="gather_weights",
        out_shape=shapes,
        in_specs=[inside] * len(shards) + [outside, inside],
        out_specs=[outside] * len(shapes),
        scratch_shapes=[
            pltpu.SemaphoreType.DMA((copies,)),
            pltpu.SemaphoreType.DMA((copies,)),
            pltpu.SemaphoreType.DMA((len(chunks),)),
        ],
        compiler_params=pltpu.CompilerParams(collective_id=0, has_side_effects=True),
        cost_estimate=pl.CostEstimate(flops=0, bytes_accessed=2 * sent, transcendentals=0),
    )(*shards, tokens, segments)
    count = len(shards) * tp
    full = [array.reshape(-1, array.shape[-1]) for array in made[:count]]
    full = [full[number * tp : (number + 1) * tp] for number in range(len(shards))]
    crossed = made[count:]
    came = [crossed[1][number] for number in range(moved * (tp - 1))] if moved else []
    return full, [crossed[0][k] for k in range(tp - 1)], came


def send(values, axes, distance):
    count = 1
    for axis in (axes,) if isinstance(axes, str) else axes:
        count *= lax.axis_size(axis)
    return lax.ppermute(values, axes, [(s, s ^ distance) for s in range(count)])


def after(values, *others):
    return lax.optimization_barrier((values,) + others)[0]


def pick(pieces, position):
    chosen = pieces[0]
    for number in range(1, len(pieces)):
        chosen = jnp.where(position == number, pieces[number], chosen)
    return chosen


def exchange_tp(pieces):
    return pieces[:1] + [send(pieces[k], "tp", k) for k in range(1, len(pieces))]


def in_place_order(pieces):
    here = lax.axis_index("tp")
    return jnp.concatenate([pick(pieces, here ^ s) for s in range(len(pieces))], axis=0)


def sum_everywhere(values):
    for axes in (("y", "tp"), ("z",), ("core",)):
        count = 1
        for axis in axes:
            count *= lax.axis_size(axis)
        values = sum([send(values, axes, k) for k in range(1, count)], values)
    return values


def block_at(values, axis, index):
    return lax.dynamic_index_in_dim(values, index, axis, keepdims=False)


def scatter_core(part):
    depth, core = lax.axis_size("z"), lax.axis_index("core")
    blocks = part.reshape(depth, 2, 2, -1, part.shape[1])
    came = send(block_at(blocks, 2, 1 - core), "core", 1)
    return (block_at(blocks, 2, core).astype(f32) + came.astype(f32)).astype(bf16)


def scatter_plane(parts, pieces=1):
    y = lax.axis_index("y")
    straight, across = [[] for _ in range(pieces)], [[] for _ in range(pieces)]
    size = parts[0].shape[0] // pieces
    for piece in range(pieces):
        rows = [part[piece * size : (piece + 1) * size] for part in parts]
        straight[piece].append(block_at(rows[0], 1, y))
        for t in range(len(parts)):
            for j in range(2):
                if t or j:
                    came = send(block_at(rows[t], 1, y ^ j), ("y", "tp"), j * len(parts) + t)
                    (across if t and j else straight)[piece].append(came)
    return straight, across


def flat(pieces):
    return [value for piece in pieces for value in piece]


def total(straight, across):
    sums = []
    for near, far in zip(straight, across):
        pieces = near + far
        made = sum([piece.astype(f32) for piece in pieces[1:]], pieces[0].astype(f32))
        sums.append(made.astype(bf16))
    return jnp.concatenate(sums, axis=0)


def scatter_z(part):
    z = lax.axis_index("z")
    made = block_at(part, 0, z).astype(f32)
    for k in range(1, part.shape[0]):
        made = made + send(block_at(part, 0, z ^ k), "z", k).astype(f32)
    return made


def segment_tables(segments, parents):
    labels = jnp.arange(parents.shape[0], dtype=jnp.int32)
    up = lambda seg: jnp.sum(jnp.where(seg[:, None] == labels, parents, 0), axis=1)
    parent = up(segments)
    table = jnp.stack([segments, parent, up(parent)])
    return jnp.pad(table.T, ((0, 0), (0, 5))), jnp.pad(table, ((0, 5), (0, 0)))


def on_device(
    tokens, segments, parents, norm_gains, norm_biases, w_qkv, w_out, w_up, w_down, cotangent
):
    tp = lax.axis_size("tp")
    here = lax.axis_index("tp")
    micro = tokens.shape[0]
    own_rows = tokens.shape[2]
    width = tokens.shape[3]
    head_width = w_out.shape[0]
    tree_len = own_rows * tp
    whole = micro // tp
    shared = list(range(whole * tp, micro))
    share_count = len(shared)
    halves = range(tp)
    split = whole * tree_len

    def outgoing(values):
        return [block_at(values, 0, n * tp + (here ^ k)) for n in range(whole) for k in range(1, tp)]

    def whole_trees(values, came):
        rows = []
        for n in range(whole):
            near = [block_at(values, 0, n * tp + here)]
            rows.append(in_place_order(near + came[n * (tp - 1) : (n + 1) * (tp - 1)]))
        return rows

    def rows_back(values):
        trees = values.reshape(micro, own_rows, width)
        back = []
        for n in range(whole):
            pieces = [block_at(trees, 0, n * tp + here)]
            for k in range(1, tp):
                low = block_at(trees, 0, n * tp + (here ^ k)).astype(bf16)
                pieces.append(send(low, "tp", k).astype(values.dtype))
            back += [pick(pieces, here ^ s) for s in halves]
        return jnp.stack(back + [trees[m] for m in shared])[:, None]

    def share_rows(values, k):
        return lax.dynamic_slice_in_dim(values, (here ^ k) * own_rows, own_rows)

    shard_qkv = w_qkv.reshape(w_qkv.shape[0], -1)
    (full_qkv, full_out, full_up), seg_came, tokens_came = gather_weights(
        [shard_qkv, w_out.T, w_up], [4, 1, 4], tokens[:, 0], segments[:, 0]
    )
    down = lax.all_gather(
        after(w_down.T, full_qkv[0]), ("tp", "z", "y", "core"), axis=0, tiled=True
    ).reshape(tp, width, -1)
    full_down = [pick([down[s] for s in halves], here ^ t) for t in halves]
    seg_came = [segments[:, 0]] + seg_came
    seg_all = jnp.concatenate([pick(seg_came, here ^ s) for s in halves], axis=1)
    rows = whole_trees(tokens[:, 0], tokens_came) + [tokens[m, 0] for m in shared]
    x = lax.optimization_barrier(jnp.concatenate(rows, axis=0)).astype(f32)
    whole_tables = []
    for n in range(whole):
        seg = pick([seg_all[n * tp + s] for s in halves], here)
        par = pick([parents[n * tp + s, 0] for s in halves], here)
        whole_tables.append(segment_tables(seg, par))
    share_tables = [segment_tables(seg_all[m], parents[m, 0]) for m in shared]

    normed = norm_forward(x, norm_gains[0], norm_biases[0]).astype(bf16)
    normed_whole = normed[:split]
    share_qkv = [dot_nn(normed[split:], w).astype(bf16) for w in full_qkv]
    whole_qkv = [dot_nn(normed_whole, w).astype(bf16) for w in full_qkv] if whole else []
    share_calls = []
    for n in range(share_count):
        cut = slice(n * own_rows, (n + 1) * own_rows)
        share_calls.append(in_place_order(exchange_tp([part[cut] for part in share_qkv])))
    whole_out = [[] for _ in halves]
    share_out = [[] for _ in halves]
    saved = {}
    def whole_forward(t, *others):
        for n in range(whole):
            qkv = after(whole_qkv[t][n * tree_len : (n + 1) * tree_len], *others)
            out, lse = attention_forward(qkv, *whole_tables[n])
            saved[n, t] = (qkv, out, lse)
            whole_out[t].append(out)

    whole_forward(0)
    share_calls = [after(call, *whole_out[0]) for call in share_calls]
    made = []
    for n in range(share_count):
        out, lse = attention_forward(share_calls[n], *share_tables[n])
        saved[n] = (share_calls[n], out, lse)
        made.append(out)
        parts = exchange_tp([share_rows(out, k) for k in halves])
        for t in halves:
            share_out[t].append(parts[t])
    for t in range(1, tp):
        whole_forward(t, *made)
    attended = [jnp.concatenate(whole_out[t] + share_out[t], axis=0) for t in halves]
    cotangent = after(cotangent[:, 0], *attended)
    cotangent_came = [send(piece, "tp", n % (tp - 1) + 1) for n, piece in enumerate(outgoing(cotangent))]
    branch_a = sum(dot_nt(attended[t], full_out[t]) for t in halves)
    residual = x + norm_forward(branch_a, norm_gains[1], norm_biases[1])

    normed_f = norm_forward(residual, norm_gains[2], norm_biases[2]).astype(bf16)
    hidden = []
    slope = []
    for t in halves:
        values, bent = gelu_and_slope(dot_nn(normed_f, full_up[t]))
        values, bent = lax.optimization_barrier((values.astype(bf16), bent.astype(bf16)))
        hidden.append(values)
        slope.append(bent)
    branch_f = sum(dot_nt(hidden[t], full_down[t]) for t in halves)
    normed_shared = []
    for n in range(share_count):
        start = split + n * own_rows
        near = after(normed[start : start + own_rows], branch_f)
        normed_shared.append(in_place_order(exchange_tp([near] * tp)))
    out = (residual + norm_forward(branch_f, norm_gains[3], norm_biases[3])).astype(bf16)
    out_rows = rows_back(out)

    grad_out = whole_trees(cotangent, cotangent_came) + [cotangent[m] for m in shared]
    grad_out = lax.optimization_barrier(jnp.concatenate(grad_out, axis=0)).astype(f32)
    grad_branch_f, sums_3 = norm_backward(branch_f, norm_gains[3], grad_out)
    grad_branch_f = grad_branch_f.astype(bf16)
    core_down = [scatter_core(dot_tn(grad_branch_f, hidden[t]).astype(bf16)) for t in halves]
    grad_up = [
        (dot_nn(grad_branch_f, full_down[t]) * slope[t].astype(f32)).astype(bf16) for t in halves
    ]
    grad_up = [after(values, *core_down) for values in grad_up]
    straight_down, across_down = scatter_plane(core_down, 2)
    dw_up = [dot_tn(normed_f, grad_up[0]).astype(bf16)]
    ready = [*dw_up, *straight_down[0]]
    dw_up += [dot_tn(after(normed_f, *ready), grad_up[t]).astype(bf16) for t in halves[1:]]
    core_up = [scatter_core(part) for part in dw_up]
    grad_up = [after(values, *dw_up, *straight_down[1]) for values in grad_up]
    grad_up[1:] = [after(values, *across_down[0]) for values in grad_up[1:]]
    grad_normed_f = sum(dot_nt(grad_up[t], full_up[t]) for t in halves)
    grad_part, sums_2 = norm_backward(residual, norm_gains[2], grad_normed_f)
    grad_residual = grad_out + grad_part

    grad_branch_a, sums_1 = norm_backward(branch_a, norm_gains[1], grad_residual)
    grad_branch_a = after(grad_branch_a.astype(bf16), *core_up, *across_down[1])
    z_down = scatter_z(after(total(straight_down, across_down), grad_branch_a))
    straight_up, across_up = scatter_plane(core_up)
    share_grad = [dot_nn(grad_branch_a[split:], w).astype(bf16) for w in full_out]
    whole_grad = [dot_nn(grad_branch_a[:split], w).astype(bf16) for w in full_out] if whole else []
    share_do = []
    for n in range(share_count):
        cut = slice(n * own_rows, (n + 1) * own_rows)
        share_do.append(in_place_order(exchange_tp([part[cut] for part in share_grad])))
    core_out = [scatter_core(dot_tn(grad_branch_a, part).astype(bf16)) for part in attended]
    grad_qkv = [[] for _ in halves]

    def whole_backward(t, *others):
        for n in range(whole):
            qkv, att, lse = saved[n, t]
            do = after(whole_grad[t][n * tree_len : (n + 1) * tree_len], *share_grad)
            made = attention_backward(qkv, after(do, *others), att, lse, *whole_tables[n])
            grad_qkv[t].append(made)
        return grad_qkv[t]

    made = []
    dw_qkv = [None] * tp
    for t in range(1, tp):
        made += whole_backward(t, z_down)
        if whole:
            dw_qkv[t] = dot_tn(normed_whole, jnp.concatenate(grad_qkv[t], axis=0)).astype(bf16)
        else:
            dw_qkv[t] = jnp.zeros(full_qkv[t].shape, bf16)
    core_qkv = [None] + [scatter_core(part) for part in dw_qkv[1:]]
    grad_shared = []
    own_part = []
    for n in range(share_count):
        qkv, att, lse = saved[n]
        do = after(share_do[n], *made)
        dx = attention_backward(qkv, do, att, lse, *share_tables[n])
        made = [dx]
        grad_shared.append(dx)
    whole_backward(0, *core_out, *flat(straight_up), *core_qkv[1:], *made)
    for n in range(share_count):
        part = dot_nt(grad_shared[n], full_qkv[0])
        pieces = exchange_tp([share_rows(part, 0)] + [share_rows(part, k).astype(bf16) for k in halves[1:]])
        own_part.append(sum([piece.astype(f32) for piece in pieces[1:]], pieces[0]))
    straight_out, across_out = scatter_plane(core_out)
    ready = flat(across_up)
    owned = [after(rows, *ready) for rows in grad_shared]
    z_out = scatter_z(total(straight_out, across_out))
    owned = [dot_tn(rows, grad) for rows, grad in zip(normed_shared, owned)]
    if whole:
        owned.append(dot_tn(normed_whole, jnp.concatenate(grad_qkv[0], axis=0)))
    dw_qkv[0] = sum(owned).astype(bf16)
    core_qkv[0] = scatter_core(dw_qkv[0])
    z_up = scatter_z(after(total(straight_up, across_up), dw_qkv[0]))
    straight_qkv, across_qkv = scatter_plane(core_qkv)
    z_qkv = scatter_z(total(straight_qkv, across_qkv))
    ready = [dw_qkv[0], *flat(across_qkv), *flat(straight_out), *flat(across_out)]
    grad_normed = list(own_part)
    if whole:
        trees = [after(jnp.concatenate(grad_qkv[t], axis=0), *ready) for t in halves]
        trees[1:] = [after(rows, core_qkv[0]) for rows in trees[1:]]
        grad_normed = [sum(dot_nt(trees[t], full_qkv[t]) for t in halves)] + grad_normed
    grad_normed = jnp.concatenate(grad_normed, axis=0)
    grad_part, sums_0 = norm_backward(x, norm_gains[0], grad_normed)
    grad_x = grad_residual + grad_part
    input_rows = rows_back(grad_x)
    sums = after(jnp.concatenate([sums_0, sums_1, sums_2, sums_3]), grad_x)
    sums = sum_everywhere(sums).reshape(4, 2, width)
    return (
        out_rows,
        input_rows,
        z_qkv.reshape(w_qkv.shape),
        z_out.T,
        z_up,
        z_down.T,
        sums[:, 0],
        sums[:, 1],
    )


def solution(mesh):
    groups, tp = mesh.devices.shape
    fine = jax.sharding.Mesh(mesh.devices.reshape(groups // 4, 2, 2, tp), ("z", "y", "core", "tp"))
    fsdp = ("z", "y", "core")
    in_specs = (
        P(None, fsdp, "tp", None),
        P(None, fsdp, "tp"),
        P(None, fsdp, None),
        P(),
        P(),
        P(fsdp, None, "tp"),
        P("tp", fsdp),
        P(fsdp, "tp"),
        P("tp", fsdp),
        P(None, fsdp, "tp", None),
    )
    out_specs = (
        P(None, fsdp, "tp", None),
        P(None, fsdp, "tp", None),
        P(fsdp, None, "tp"),
        P("tp", fsdp),
        P(fsdp, "tp"),
        P("tp", fsdp),
        P(),
        P(),
    )
    return jax.shard_map(
        on_device, mesh=fine, in_specs=in_specs, out_specs=out_specs, check_vma=False
    )
```

```python
import functools
import math

import jax
import jax.numpy as jnp
from jax import lax
from jax.experimental import pallas as pl
from jax.experimental.pallas import tpu as pltpu
from jax.sharding import PartitionSpec as P

HEAD_DIM = 64
norm_eps = 1e-05
masked_value = -1e30
f32 = jnp.float32
bf16 = jnp.bfloat16
exp2_scale = math.log2(math.e) / math.sqrt(HEAD_DIM)
grad_scale = 1.0 / math.sqrt(HEAD_DIM)
gelu_scale = math.sqrt(2.0 / math.pi)
gelu_cubic = 0.044715


def dot_nn(a, b):
    return lax.dot_general(a, b, (((1,), (0,)), ((), ())), preferred_element_type=f32)


def dot_nt(a, b):
    return lax.dot_general(a, b, (((1,), (1,)), ((), ())), preferred_element_type=f32)


def dot_tn(a, b):
    return lax.dot_general(a, b, (((0,), (0,)), ((), ())), preferred_element_type=f32)


def split_heads(x):
    lane = lax.broadcasted_iota(jnp.int32, x.shape, 1)
    zero = jnp.zeros_like(x)
    return jnp.where(lane < HEAD_DIM, x, zero), jnp.where(lane >= HEAD_DIM, x, zero)


def block_rows(tree_len):
    return 256 if tree_len % 256 == 0 else 128


def attention_forward_kernel(q_ref, k_ref, v_ref, col_ref, row_ref, o_ref, lse_ref, bias):
    tree_len = q_ref.shape[0]
    rows = block_rows(tree_len)

    @pl.when(pl.program_id(0) == 0)
    def _():
        for start in range(0, tree_len, rows):
            stop = start + rows
            key_seg = row_ref[0:1, :stop]
            ok = col_ref[start:stop, 0:1] == key_seg
            ok = ok | (col_ref[start:stop, 1:2] == key_seg)
            ok = ok | (col_ref[start:stop, 2:3] == key_seg)
            i = lax.broadcasted_iota(jnp.int32, (rows, stop), 0) + start
            j = lax.broadcasted_iota(jnp.int32, (rows, stop), 1)
            bias[start:stop, :stop] = jnp.where(ok & (j <= i), 0.0, masked_value).astype(f32)

    for start in range(0, tree_len, rows):
        stop = start + rows
        queries = split_heads(q_ref[start:stop, :])
        outs = []
        for h in range(2):
            scores = dot_nt(queries[h], k_ref[:stop, :]) + bias[start:stop, :stop]
            top = jnp.max(scores, axis=1, keepdims=True)
            weights = jnp.exp2((scores - top) * exp2_scale)
            total = jnp.sum(weights, axis=1, keepdims=True)
            outs.append(dot_nn(weights.astype(bf16), v_ref[:stop, :]) / total)
            lse = jnp.broadcast_to(top * exp2_scale + jnp.log2(total), (rows, 128))
            lse_ref[0, h : h + 1, start:stop] = jnp.transpose(lse)[0:1, :]
        lane = lax.broadcasted_iota(jnp.int32, (rows, 128), 1)
        o_ref[start:stop, :] = jnp.where(lane < HEAD_DIM, outs[0], outs[1]).astype(bf16)


def attention_forward(qkv, cols, rows):
    tree_len, width = qkv.shape
    pairs = width // 384
    tile = (tree_len, 128)
    return pl.pallas_call(
        attention_forward_kernel,
        name="attention_forward",
        out_shape=(
            jax.ShapeDtypeStruct((tree_len, width // 3), bf16),
            jax.ShapeDtypeStruct((pairs, 8, tree_len), f32),
        ),
        grid=(pairs,),
        in_specs=[
            pl.BlockSpec(tile, lambda p: (0, p)),
            pl.BlockSpec(tile, lambda p: (0, pairs + p)),
            pl.BlockSpec(tile, lambda p: (0, 2 * pairs + p)),
            pl.BlockSpec(cols.shape, lambda p: (0, 0)),
            pl.BlockSpec(rows.shape, lambda p: (0, 0)),
        ],
        out_specs=(
            pl.BlockSpec(tile, lambda p: (0, p)),
            pl.BlockSpec((1, 8, tree_len), lambda p: (p, 0, 0)),
        ),
        scratch_shapes=[pltpu.VMEM((tree_len, tree_len), f32)],
        compiler_params=pltpu.CompilerParams(vmem_limit_bytes=40 << 20),
        cost_estimate=pl.CostEstimate(
            flops=int(0.6 * 2 * pairs * 4 * tree_len * tree_len * 256),
            bytes_accessed=tree_len * width * 3,
            transcendentals=pairs * tree_len * tree_len,
        ),
    )(qkv, qkv, qkv, cols, rows)


def attention_backward_kernel(
    q_ref, k_ref, v_ref, do_ref, o_ref, lse_ref, col_ref, row_ref, dx_ref, bias, split_k, dk, dv
):
    tree_len = q_ref.shape[0]
    rows = block_rows(tree_len)
    pair = pl.program_id(0)
    pairs = pl.num_programs(0)

    @pl.when(pair == 0)
    def _():
        for start in range(0, tree_len, rows):
            stop = start + rows
            key_seg = col_ref[:stop, 0:1]
            ok = row_ref[0:1, start:stop] == key_seg
            ok = ok | (row_ref[1:2, start:stop] == key_seg)
            ok = ok | (row_ref[2:3, start:stop] == key_seg)
            j = lax.broadcasted_iota(jnp.int32, (stop, rows), 0)
            i = lax.broadcasted_iota(jnp.int32, (stop, rows), 1) + start
            bias[:stop, start:stop] = jnp.where(ok & (j <= i), 0.0, masked_value).astype(f32)

    split_k[0], split_k[1] = split_heads(k_ref[...])
    dk[...] = jnp.zeros_like(dk)
    dv[...] = jnp.zeros_like(dv)
    sub = lax.broadcasted_iota(jnp.int32, (8, 128), 0)
    lane = lax.broadcasted_iota(jnp.int32, (8, 128), 1)
    own = jnp.where(lane // HEAD_DIM == sub, 1.0, 0.0).astype(f32)
    for start in range(0, tree_len, rows):
        stop = start + rows
        queries = split_heads(q_ref[start:stop, :])
        grads = split_heads(do_ref[start:stop, :])
        product = do_ref[start:stop, :].astype(f32) * o_ref[start:stop, :].astype(f32)
        row_dot = lax.dot_general(
            own,
            product,
            (((1,), (1,)), ((), ())),
            precision=lax.Precision.HIGHEST,
            preferred_element_type=f32,
        )
        probs_low = []
        grad_scores = []
        for h in range(2):
            shift = bias[:stop, start:stop] - lse_ref[0, h : h + 1, start:stop]
            probs = jnp.exp2(dot_nt(k_ref[:stop, :], queries[h]) * exp2_scale + shift)
            grad_probs = dot_nt(v_ref[:stop, :], grads[h])
            probs_low.append(probs.astype(bf16))
            grad_scores.append((probs * (grad_probs - row_dot[h : h + 1, :])).astype(bf16))
        dv[:stop, :] += dot_nn(jnp.concatenate(probs_low, 1), jnp.concatenate(grads, 0))
        dk[:stop, :] += dot_nn(jnp.concatenate(grad_scores, 1), jnp.concatenate(queries, 0))
        dq = dot_tn(grad_scores[0], split_k[0, :stop, :])
        dq = dq + dot_tn(grad_scores[1], split_k[1, :stop, :])
        dq = (dq.astype(bf16).astype(f32) * grad_scale).astype(bf16)
        dx_ref[start:stop, pl.ds(pl.multiple_of(pair * 128, 128), 128)] = dq
    dx_ref[:, pl.ds(pl.multiple_of((pairs + pair) * 128, 128), 128)] = (
        dk[...] * grad_scale
    ).astype(bf16)
    dx_ref[:, pl.ds(pl.multiple_of((2 * pairs + pair) * 128, 128), 128)] = dv[...].astype(bf16)


def attention_backward(qkv, grad, out, lse, cols, rows):
    tree_len, width = qkv.shape
    pairs = width // 384
    tile = (tree_len, 128)
    return pl.pallas_call(
        attention_backward_kernel,
        name="attention_backward",
        out_shape=jax.ShapeDtypeStruct((tree_len, width), bf16),
        grid=(pairs,),
        in_specs=[
            pl.BlockSpec(tile, lambda p: (0, p)),
            pl.BlockSpec(tile, lambda p: (0, pairs + p)),
            pl.BlockSpec(tile, lambda p: (0, 2 * pairs + p)),
            pl.BlockSpec(tile, lambda p: (0, p)),
            pl.BlockSpec(tile, lambda p: (0, p)),
            pl.BlockSpec((1, 8, tree_len), lambda p: (p, 0, 0)),
            pl.BlockSpec(cols.shape, lambda p: (0, 0)),
            pl.BlockSpec(rows.shape, lambda p: (0, 0)),
        ],
        out_specs=pl.BlockSpec((tree_len, width), lambda p: (0, 0)),
        scratch_shapes=[
            pltpu.VMEM((tree_len, tree_len), f32),
            pltpu.VMEM((2, tree_len, 128), bf16),
            pltpu.VMEM(tile, f32),
            pltpu.VMEM(tile, f32),
        ],
        compiler_params=pltpu.CompilerParams(vmem_limit_bytes=40 << 20),
        cost_estimate=pl.CostEstimate(
            flops=int(0.6 * 5 * pairs * 4 * tree_len * tree_len * 256),
            bytes_accessed=tree_len * width * 6,
            transcendentals=pairs * tree_len * tree_len,
        ),
    )(qkv, qkv, qkv, grad, out, lse, cols, rows)


def norm_parts(values):
    centered = values - jnp.mean(values, axis=-1, keepdims=True)
    scale = lax.rsqrt(jnp.mean(centered * centered, axis=-1, keepdims=True) + norm_eps)
    return centered * scale, scale


def norm_forward(values, gain, shift):
    return norm_parts(values)[0] * gain + shift


def norm_backward(values, gain, grad):
    xhat, scale = norm_parts(values)
    h = grad * gain
    inner = h - jnp.mean(h, axis=-1, keepdims=True)
    inner = inner - xhat * jnp.mean(h * xhat, axis=-1, keepdims=True)
    return scale * inner, jnp.stack([jnp.sum(grad * xhat, axis=0), jnp.sum(grad, axis=0)])


def gelu_and_slope(values):
    square = values * values
    bent = jnp.tanh(values * (gelu_scale + gelu_scale * gelu_cubic * square))
    half = 0.5 + 0.5 * bent
    made = values * half
    slope = half + made * (1.0 - half) * (2.0 * gelu_scale + 6.0 * gelu_scale * gelu_cubic * square)
    return made, slope


def apart(position, distance):
    bit = 1
    while bit <= distance:
        if distance & bit:
            position = position + bit - 2 * bit * (position // bit % 2)
        bit *= 2
    return position


def gather_kernel(chunks, weights, moved, *refs):
    shards, refs = refs[:weights], refs[weights:]
    tokens, segments, refs = refs[0], refs[1], refs[2:]
    tp = lax.axis_size("tp")
    depth = lax.axis_size("z")
    outs, refs = refs[: weights * tp], refs[weights * tp :]
    segments_out, refs = refs[0], refs[1:]
    tokens_out, refs = (refs[0], refs[1:]) if moved else (None, refs)
    send_sems, recv_sems, local_sems = refs
    z, y, core, x = (lax.axis_index(name) for name in ("z", "y", "core", "tp"))

    barrier = pltpu.get_barrier_semaphore()
    partners = [{"z": apart(z, k)} for k in range(1, depth)]
    partners += [{"tp": apart(x, k)} for k in range(1, tp)]
    partners += [{"y": 1 - y}, {"core": 1 - core}]
    for partner in partners:
        pl.semaphore_signal(barrier, inc=1, device_id=partner, device_id_type=pl.DeviceIdType.MESH)
    pl.semaphore_wait(barrier, len(partners))

    half = depth // 2
    first = pl.ds(z // half * half, half)
    second = pl.ds(half - z // half * half, half)
    started = []

    def copy(source, target, partner):
        slot = len(started)
        made = pltpu.make_async_remote_copy(
            src_ref=source,
            dst_ref=target,
            send_sem=send_sems.at[slot],
            recv_sem=recv_sems.at[slot],
            device_id=partner,
            device_id_type=pl.DeviceIdType.MESH,
        )
        made.start()
        started.append(made)
        return made

    crossed = []
    for k in range(1, tp):
        partner = {"tp": apart(x, k)}
        crossed.append(copy(segments, segments_out.at[k - 1], partner))
        for n in range(moved):
            target = tokens_out.at[n * (tp - 1) + k - 1]
            crossed.append(copy(tokens.at[n * tp + apart(x, k)], target, partner))

    def part(number, t, at_y, span):
        weight, low, rows = chunks[number]
        return outs[weight * tp + t].at[span, at_y, core, pl.ds(low, rows)]

    def along_z(number):
        weight, low, rows = chunks[number]
        own = shards[weight].at[pl.ds(low, rows)]
        target = outs[weight * tp].at[z, y, core, pl.ds(low, rows)]
        keep = pltpu.make_async_copy(own, target, local_sems.at[number])
        keep.start()
        return keep, [copy(own, target, {"z": apart(z, k)}) for k in range(1, depth)]

    def over(number, t, target_t, at_y, span, partner):
        return copy(part(number, t, at_y, span), part(number, target_t, at_y, span), partner)

    def to_core(number, t, at_y, span):
        crossed.append(over(number, t, t, at_y, span, {"core": 1 - core}))

    def plane_start(number, keep, sent):
        keep.wait()
        for k in range(1, half):
            sent[k - 1].wait_recv()
        over_x = [over(number, 0, k, y, first, {"tp": apart(x, k)}) for k in range(1, tp)]
        for k in range(half, depth):
            sent[k - 1].wait_recv()
        over_y = over(number, 0, 0, y, second, {"y": 1 - y})
        last = [(over(number, 0, 0, y, first, {"y": 1 - y}), 0, 1 - y, first)]
        for k in range(1, tp):
            made = over(number, 0, k, y, second, {"tp": apart(x, k)})
            last.append((made, k, y, second))
        to_core(number, 0, y, first)
        to_core(number, 0, y, second)
        return over_x, over_y, last

    def plane_turn(number, over_x, over_y, last):
        for k in range(1, tp):
            over_x[k - 1].wait_recv()
            made = over(number, k, k, y, first, {"y": 1 - y})
            last.append((made, k, 1 - y, first))
            to_core(number, k, y, first)
        over_y.wait_recv()
        for k in range(1, tp):
            made = over(number, 0, k, 1 - y, second, {"tp": apart(x, k)})
            last.append((made, k, 1 - y, second))
        to_core(number, 0, 1 - y, second)
        return last

    def plane_end(number, last):
        for made, t, at_y, span in last:
            made.wait_recv()
            to_core(number, t, at_y, span)

    count = len(chunks)
    state = {0: along_z(0)}
    for step in range(count + 2):
        if step < count:
            state[step] = plane_start(step, *state[step])
            if step + 1 < count:
                state[step + 1] = along_z(step + 1)
        if 0 <= step - 1 < count:
            state[step - 1] = plane_turn(step - 1, *state[step - 1])
        if 0 <= step - 2 < count:
            plane_end(step - 2, state[step - 2])
    for made in crossed:
        made.wait_recv()
    for made in started:
        made.wait_send()


def gather_weights(shards, pieces, tokens, segments):
    tp = lax.axis_size("tp")
    depth = lax.axis_size("z")
    moved = tokens.shape[0] // tp
    chunks = []
    for number, (shard, split) in enumerate(zip(shards, pieces)):
        rows = shard.shape[0] // split
        chunks += [(number, piece * rows, rows) for piece in range(split)]
    copies = len(chunks) * (depth + 1 + 4 * (tp - 1) + 4 * tp)
    copies += (moved + 1) * (tp - 1)
    shapes = [
        jax.ShapeDtypeStruct((depth, 2, 2) + shard.shape, shard.dtype)
        for shard in shards
        for _ in range(tp)
    ]
    sent = sum(shape.size for shape in shapes) * 2
    shapes += [jax.ShapeDtypeStruct((tp - 1,) + segments.shape, segments.dtype)]
    if moved:
        shapes += [jax.ShapeDtypeStruct((moved * (tp - 1),) + tokens.shape[1:], tokens.dtype)]
    inside = pl.BlockSpec(memory_space=pltpu.VMEM)
    outside = pl.BlockSpec(memory_space=pl.ANY)
    made = pl.pallas_call(
        functools.partial(gather_kernel, chunks, len(shards), moved),
        name="gather_weights",
        out_shape=shapes,
        in_specs=[inside] * len(shards) + [outside, inside],
        out_specs=[outside] * len(shapes),
        scratch_shapes=[
            pltpu.SemaphoreType.DMA((copies,)),
            pltpu.SemaphoreType.DMA((copies,)),
            pltpu.SemaphoreType.DMA((len(chunks),)),
        ],
        compiler_params=pltpu.CompilerParams(collective_id=0, has_side_effects=True),
        cost_estimate=pl.CostEstimate(flops=0, bytes_accessed=2 * sent, transcendentals=0),
    )(*shards, tokens, segments)
    count = len(shards) * tp
    full = [array.reshape(-1, array.shape[-1]) for array in made[:count]]
    full = [full[number * tp : (number + 1) * tp] for number in range(len(shards))]
    crossed = made[count:]
    came = [crossed[1][number] for number in range(moved * (tp - 1))] if moved else []
    return full, [crossed[0][k] for k in range(tp - 1)], came


def send(values, axes, distance):
    count = 1
    for axis in (axes,) if isinstance(axes, str) else axes:
        count *= lax.axis_size(axis)
    return lax.ppermute(values, axes, [(s, s ^ distance) for s in range(count)])


def after(values, *others):
    return lax.optimization_barrier((values,) + others)[0]


def pick(pieces, position):
    chosen = pieces[0]
    for number in range(1, len(pieces)):
        chosen = jnp.where(position == number, pieces[number], chosen)
    return chosen


def exchange_tp(pieces):
    return pieces[:1] + [send(pieces[k], "tp", k) for k in range(1, len(pieces))]


def in_place_order(pieces):
    here = lax.axis_index("tp")
    return jnp.concatenate([pick(pieces, here ^ s) for s in range(len(pieces))], axis=0)


def sum_everywhere(values):
    for axes in (("y", "tp"), ("z",), ("core",)):
        count = 1
        for axis in axes:
            count *= lax.axis_size(axis)
        values = sum([send(values, axes, k) for k in range(1, count)], values)
    return values


def block_at(values, axis, index):
    return lax.dynamic_index_in_dim(values, index, axis, keepdims=False)


def scatter_core(part):
    depth, core = lax.axis_size("z"), lax.axis_index("core")
    blocks = part.reshape(depth, 2, 2, -1, part.shape[1])
    came = send(block_at(blocks, 2, 1 - core), "core", 1)
    return (block_at(blocks, 2, core).astype(f32) + came.astype(f32)).astype(bf16)


def scatter_plane(parts, pieces=1):
    y = lax.axis_index("y")
    straight, across = [[] for _ in range(pieces)], [[] for _ in range(pieces)]
    size = parts[0].shape[0] // pieces
    for piece in range(pieces):
        rows = [part[piece * size : (piece + 1) * size] for part in parts]
        straight[piece].append(block_at(rows[0], 1, y))
        for t in range(len(parts)):
            for j in range(2):
                if t or j:
                    came = send(block_at(rows[t], 1, y ^ j), ("y", "tp"), j * len(parts) + t)
                    (across if t and j else straight)[piece].append(came)
    return straight, across


def flat(pieces):
    return [value for piece in pieces for value in piece]


def over_y(part):
    y = lax.axis_index("y")
    return block_at(part, 1, y), send(block_at(part, 1, 1 - y), "y", 1)


def over_tp(pairs):
    return [send(total([list(pair)], [[]]), "tp", t + 1) for t, pair in enumerate(pairs)]


def total(straight, across):
    sums = []
    for near, far in zip(straight, across):
        pieces = near + far
        made = sum([piece.astype(f32) for piece in pieces[1:]], pieces[0].astype(f32))
        sums.append(made.astype(bf16))
    return jnp.concatenate(sums, axis=0)


def scatter_z(part, *late):
    z = lax.axis_index("z")
    made = block_at(part, 0, z).astype(f32)
    for k in range(1, part.shape[0]):
        came = send(block_at(part, 0, z ^ k), "z", k)
        made = made + (after(came, *late) if late else came).astype(f32)
    return made


def segment_tables(segments, parents):
    labels = jnp.arange(parents.shape[0], dtype=jnp.int32)
    up = lambda seg: jnp.sum(jnp.where(seg[:, None] == labels, parents, 0), axis=1)
    parent = up(segments)
    table = jnp.stack([segments, parent, up(parent)])
    return jnp.pad(table.T, ((0, 0), (0, 5))), jnp.pad(table, ((0, 5), (0, 0)))


def on_device(
    tokens, segments, parents, norm_gains, norm_biases, w_qkv, w_out, w_up, w_down, cotangent
):
    tp = lax.axis_size("tp")
    here = lax.axis_index("tp")
    micro = tokens.shape[0]
    own_rows = tokens.shape[2]
    width = tokens.shape[3]
    head_width = w_out.shape[0]
    tree_len = own_rows * tp
    whole = micro // tp
    shared = list(range(whole * tp, micro))
    share_count = len(shared)
    halves = range(tp)
    split = whole * tree_len

    def outgoing(values):
        return [block_at(values, 0, n * tp + (here ^ k)) for n in range(whole) for k in range(1, tp)]

    def whole_trees(values, came):
        rows = []
        for n in range(whole):
            near = [block_at(values, 0, n * tp + here)]
            rows.append(in_place_order(near + came[n * (tp - 1) : (n + 1) * (tp - 1)]))
        return rows

    def rows_back(values):
        trees = values.reshape(micro, own_rows, width)
        back = []
        for n in range(whole):
            pieces = [block_at(trees, 0, n * tp + here)]
            for k in range(1, tp):
                low = block_at(trees, 0, n * tp + (here ^ k)).astype(bf16)
                pieces.append(send(low, "tp", k).astype(values.dtype))
            back += [pick(pieces, here ^ s) for s in halves]
        return jnp.stack(back + [trees[m] for m in shared])[:, None]

    def share_rows(values, k):
        return lax.dynamic_slice_in_dim(values, (here ^ k) * own_rows, own_rows)

    shard_qkv = w_qkv.reshape(w_qkv.shape[0], -1)
    (full_qkv, full_out, full_up), seg_came, tokens_came = gather_weights(
        [shard_qkv, w_out.T, w_up], [4, 1, 4], tokens[:, 0], segments[:, 0]
    )
    down = lax.all_gather(
        after(w_down.T, full_qkv[0]), ("tp", "z", "y", "core"), axis=0, tiled=True
    ).reshape(tp, width, -1)
    full_down = [pick([down[s] for s in halves], here ^ t) for t in halves]
    seg_came = [segments[:, 0]] + seg_came
    seg_all = jnp.concatenate([pick(seg_came, here ^ s) for s in halves], axis=1)
    rows = whole_trees(tokens[:, 0], tokens_came) + [tokens[m, 0] for m in shared]
    x = lax.optimization_barrier(jnp.concatenate(rows, axis=0)).astype(f32)
    whole_tables = []
    for n in range(whole):
        seg = pick([seg_all[n * tp + s] for s in halves], here)
        par = pick([parents[n * tp + s, 0] for s in halves], here)
        whole_tables.append(segment_tables(seg, par))
    share_tables = [segment_tables(seg_all[m], parents[m, 0]) for m in shared]

    normed = norm_forward(x, norm_gains[0], norm_biases[0]).astype(bf16)
    normed_whole = normed[:split]
    share_qkv = [dot_nn(normed[split:], w).astype(bf16) for w in full_qkv]
    whole_qkv = [dot_nn(normed_whole, w).astype(bf16) for w in full_qkv] if whole else []
    share_calls = []
    for n in range(share_count):
        cut = slice(n * own_rows, (n + 1) * own_rows)
        share_calls.append(in_place_order(exchange_tp([part[cut] for part in share_qkv])))
    whole_out = [[] for _ in halves]
    share_out = [[] for _ in halves]
    saved = {}
    for n in range(whole):
        for t in halves:
            qkv = whole_qkv[t][n * tree_len : (n + 1) * tree_len]
            out, lse = attention_forward(qkv, *whole_tables[n])
            saved[n, t] = (qkv, out, lse)
            whole_out[t].append(out)
    share_calls = [after(call, *whole_out[0]) for call in share_calls]
    for n in range(share_count):
        out, lse = attention_forward(share_calls[n], *share_tables[n])
        saved[n] = (share_calls[n], out, lse)
        parts = exchange_tp([share_rows(out, k) for k in halves])
        for t in halves:
            share_out[t].append(parts[t])
    attended = [jnp.concatenate(whole_out[t] + share_out[t], axis=0) for t in halves]
    cotangent = after(cotangent[:, 0], *attended)
    cotangent_came = [send(piece, "tp", n % (tp - 1) + 1) for n, piece in enumerate(outgoing(cotangent))]
    branch_a = sum(dot_nt(attended[t], full_out[t]) for t in halves)
    residual = x + norm_forward(branch_a, norm_gains[1], norm_biases[1])

    normed_f = norm_forward(residual, norm_gains[2], norm_biases[2]).astype(bf16)
    hidden = []
    slope = []
    for t in halves:
        values, bent = gelu_and_slope(dot_nn(normed_f, full_up[t]))
        values, bent = lax.optimization_barrier((values.astype(bf16), bent.astype(bf16)))
        hidden.append(values)
        slope.append(bent)
    crossing = []
    for n in range(share_count):
        start = split + n * own_rows
        near = after(normed[start : start + own_rows], hidden[0])
        crossing.append(exchange_tp([near] * tp))
    branch_f = sum(dot_nt(hidden[t], full_down[t]) for t in halves)
    out = (residual + norm_forward(branch_f, norm_gains[3], norm_biases[3])).astype(bf16)
    out_rows = rows_back(out)

    grad_out = whole_trees(cotangent, cotangent_came) + [cotangent[m] for m in shared]
    grad_out = lax.optimization_barrier(jnp.concatenate(grad_out, axis=0)).astype(f32)
    grad_branch_f, sums_3 = norm_backward(branch_f, norm_gains[3], grad_out)
    grad_branch_f = grad_branch_f.astype(bf16)
    core_down = [scatter_core(dot_tn(grad_branch_f, hidden[t]).astype(bf16)) for t in halves]
    grad_up = [
        (dot_nn(grad_branch_f, full_down[t]) * slope[t].astype(f32)).astype(bf16) for t in halves
    ]
    grad_up = [after(values, *core_down) for values in grad_up]
    straight_down, across_down = scatter_plane(core_down, 2)
    dw_up = [dot_tn(normed_f, grad_up[0]).astype(bf16)]
    ready = [*dw_up, *straight_down[0]]
    dw_up += [dot_tn(after(normed_f, *ready), grad_up[t]).astype(bf16) for t in halves[1:]]
    core_up = [scatter_core(part) for part in dw_up]
    grad_up = [after(values, *dw_up, *straight_down[1]) for values in grad_up]
    grad_up[1:] = [after(values, *across_down[0]) for values in grad_up[1:]]
    grad_normed_f = sum(dot_nt(grad_up[t], full_up[t]) for t in halves)
    grad_part, sums_2 = norm_backward(residual, norm_gains[2], grad_normed_f)
    grad_residual = grad_out + grad_part

    grad_branch_a, sums_1 = norm_backward(branch_a, norm_gains[1], grad_residual)
    grad_branch_a = after(grad_branch_a.astype(bf16), *core_up, *across_down[1])
    up_y = {t: over_y(core_up[t]) for t in reversed(halves)}
    up_x = over_tp([up_y[t] for t in halves[1:]])
    share_grad = [dot_nn(grad_branch_a[split:], w).astype(bf16) for w in full_out]
    whole_grad = [dot_nn(grad_branch_a[:split], w).astype(bf16) for w in full_out] if whole else []
    share_do = []
    for n in range(share_count):
        cut = slice(n * own_rows, (n + 1) * own_rows)
        share_do.append(in_place_order(exchange_tp([part[cut] for part in share_grad])))
    grad_qkv = [[] for _ in halves]

    def whole_backward(t, *others):
        for n in range(whole):
            qkv, att, lse = saved[n, t]
            do = after(whole_grad[t][n * tree_len : (n + 1) * tree_len], *share_grad)
            made = attention_backward(qkv, after(do, *others), att, lse, *whole_tables[n])
            grad_qkv[t].append(made)
        return grad_qkv[t]

    made = []
    dw_qkv = [None] * tp
    down = total(straight_down, across_down)
    for t in range(1, tp):
        made += whole_backward(t)
        if whole:
            dw_qkv[t] = dot_tn(normed_whole, jnp.concatenate(grad_qkv[t], axis=0)).astype(bf16)
        else:
            dw_qkv[t] = jnp.zeros(full_qkv[t].shape, bf16)
    z_down = scatter_z(down, *made)
    core_qkv = [None] + [scatter_core(part) for part in dw_qkv[1:]]
    late_grad = after(grad_branch_a, *made)
    core_out = [scatter_core(dot_tn(late_grad, part).astype(bf16)) for part in attended]
    grad_shared = []
    own_part = []
    early_y = [up_y[t][1] for t in halves[1:]]
    for n in range(share_count):
        qkv, att, lse = saved[n]
        do = after(share_do[n], *made, *early_y)
        dx = attention_backward(qkv, do, att, lse, *share_tables[n])
        made = [dx]
        grad_shared.append(dx)
    whole_backward(0, *core_out, *up_x, up_y[0][1], *core_qkv[1:], *made)
    for n in range(share_count):
        part = dot_nt(grad_shared[n], full_qkv[0])
        pieces = exchange_tp([share_rows(part, 0)] + [share_rows(part, k).astype(bf16) for k in halves[1:]])
        own_part.append(sum([piece.astype(f32) for piece in pieces[1:]], pieces[0]))
    qkv_y = {t: over_y(core_qkv[t]) for t in halves[1:]}
    out_y = {t: over_y(core_out[t]) for t in reversed(halves)}
    ready = [qkv_y[t][1] for t in halves[1:]]
    owned = [after(rows, *ready) for rows in grad_shared]
    qkv_x = over_tp([qkv_y[t] for t in halves[1:]])
    out_x = over_tp([out_y[t] for t in halves[1:]])
    near = in_place_order
    normed_shared = [near([pieces[0]] + [after(piece, *made) for piece in pieces[1:]]) for pieces in crossing]
    owned = [dot_tn(rows, grad) for rows, grad in zip(normed_shared, owned)]
    if whole:
        owned.append(dot_tn(normed_whole, jnp.concatenate(grad_qkv[0], axis=0)))
    dw_qkv[0] = sum(owned).astype(bf16)
    core_qkv[0] = scatter_core(dw_qkv[0])
    z_up_part = after(total([[*up_y[0], *up_x]], [[]]), dw_qkv[0])
    z_out_part = after(total([[*out_y[0], *out_x]], [[]]), dw_qkv[0])
    qkv_y[0] = over_y(core_qkv[0])
    z_qkv = scatter_z(total([[*qkv_y[0], *qkv_x]], [[]]))
    ready = [dw_qkv[0]]
    grad_normed = list(own_part)
    if whole:
        trees = [after(jnp.concatenate(grad_qkv[t], axis=0), *ready) for t in halves]
        trees[1:] = [after(rows, core_qkv[0]) for rows in trees[1:]]
        grad_normed = [sum(dot_nt(trees[t], full_qkv[t]) for t in halves)] + grad_normed
    grad_normed = jnp.concatenate(grad_normed, axis=0)
    grad_part, sums_0 = norm_backward(x, norm_gains[0], grad_normed)
    grad_x = grad_residual + grad_part
    input_rows = rows_back(grad_x)
    z_up = scatter_z(z_up_part, grad_x)
    z_out = scatter_z(z_out_part, grad_x)
    sums = after(jnp.concatenate([sums_0, sums_1, sums_2, sums_3]), grad_x)
    sums = sum_everywhere(sums).reshape(4, 2, width)
    return (
        out_rows,
        input_rows,
        z_qkv.reshape(w_qkv.shape),
        z_out.T,
        z_up,
        z_down.T,
        sums[:, 0],
        sums[:, 1],
    )


def solution(mesh):
    groups, tp = mesh.devices.shape
    fine = jax.sharding.Mesh(mesh.devices.reshape(groups // 4, 2, 2, tp), ("z", "y", "core", "tp"))
    fsdp = ("z", "y", "core")
    in_specs = (
        P(None, fsdp, "tp", None),
        P(None, fsdp, "tp"),
        P(None, fsdp, None),
        P(),
        P(),
        P(fsdp, None, "tp"),
        P("tp", fsdp),
        P(fsdp, "tp"),
        P("tp", fsdp),
        P(None, fsdp, "tp", None),
    )
    out_specs = (
        P(None, fsdp, "tp", None),
        P(None, fsdp, "tp", None),
        P(fsdp, None, "tp"),
        P("tp", fsdp),
        P(fsdp, "tp"),
        P("tp", fsdp),
        P(),
        P(),
    )
    return jax.shard_map(
        on_device, mesh=fine, in_specs=in_specs, out_specs=out_specs, check_vma=False
    )
```

```python
import functools
import math

import jax
import jax.numpy as jnp
from jax import lax
from jax.experimental import pallas as pl
from jax.experimental.pallas import tpu as pltpu
from jax.sharding import PartitionSpec as P

HEAD_DIM = 64
norm_eps = 1e-05
masked_value = -1e30
f32 = jnp.float32
bf16 = jnp.bfloat16
exp2_scale = math.log2(math.e) / math.sqrt(HEAD_DIM)
grad_scale = 1.0 / math.sqrt(HEAD_DIM)
gelu_scale = math.sqrt(2.0 / math.pi)
gelu_cubic = 0.044715


def dot_nn(a, b):
    return lax.dot_general(a, b, (((1,), (0,)), ((), ())), preferred_element_type=f32)


def dot_nt(a, b):
    return lax.dot_general(a, b, (((1,), (1,)), ((), ())), preferred_element_type=f32)


def dot_tn(a, b):
    return lax.dot_general(a, b, (((0,), (0,)), ((), ())), preferred_element_type=f32)


def split_heads(x):
    lane = lax.broadcasted_iota(jnp.int32, x.shape, 1)
    zero = jnp.zeros_like(x)
    return jnp.where(lane < HEAD_DIM, x, zero), jnp.where(lane >= HEAD_DIM, x, zero)


def block_rows(tree_len):
    return 256 if tree_len % 256 == 0 else 128


def attention_forward_kernel(q_ref, k_ref, v_ref, col_ref, row_ref, o_ref, lse_ref, bias):
    tree_len = q_ref.shape[0]
    rows = block_rows(tree_len)

    @pl.when(pl.program_id(0) == 0)
    def _():
        for start in range(0, tree_len, rows):
            stop = start + rows
            key_seg = row_ref[0:1, :stop]
            ok = col_ref[start:stop, 0:1] == key_seg
            ok = ok | (col_ref[start:stop, 1:2] == key_seg)
            ok = ok | (col_ref[start:stop, 2:3] == key_seg)
            i = lax.broadcasted_iota(jnp.int32, (rows, stop), 0) + start
            j = lax.broadcasted_iota(jnp.int32, (rows, stop), 1)
            bias[start:stop, :stop] = jnp.where(ok & (j <= i), 0.0, masked_value).astype(f32)

    for start in range(0, tree_len, rows):
        stop = start + rows
        queries = split_heads(q_ref[start:stop, :])
        outs = []
        for h in range(2):
            scores = dot_nt(queries[h], k_ref[:stop, :]) + bias[start:stop, :stop]
            top = jnp.max(scores, axis=1, keepdims=True)
            weights = jnp.exp2((scores - top) * exp2_scale)
            total = jnp.sum(weights, axis=1, keepdims=True)
            outs.append(dot_nn(weights.astype(bf16), v_ref[:stop, :]) / total)
            lse = jnp.broadcast_to(top * exp2_scale + jnp.log2(total), (rows, 128))
            lse_ref[0, h : h + 1, start:stop] = jnp.transpose(lse)[0:1, :]
        lane = lax.broadcasted_iota(jnp.int32, (rows, 128), 1)
        o_ref[start:stop, :] = jnp.where(lane < HEAD_DIM, outs[0], outs[1]).astype(bf16)


def attention_forward(qkv, cols, rows):
    tree_len, width = qkv.shape
    pairs = width // 384
    tile = (tree_len, 128)
    return pl.pallas_call(
        attention_forward_kernel,
        name="attention_forward",
        out_shape=(
            jax.ShapeDtypeStruct((tree_len, width // 3), bf16),
            jax.ShapeDtypeStruct((pairs, 8, tree_len), f32),
        ),
        grid=(pairs,),
        in_specs=[
            pl.BlockSpec(tile, lambda p: (0, p)),
            pl.BlockSpec(tile, lambda p: (0, pairs + p)),
            pl.BlockSpec(tile, lambda p: (0, 2 * pairs + p)),
            pl.BlockSpec(cols.shape, lambda p: (0, 0)),
            pl.BlockSpec(rows.shape, lambda p: (0, 0)),
        ],
        out_specs=(
            pl.BlockSpec(tile, lambda p: (0, p)),
            pl.BlockSpec((1, 8, tree_len), lambda p: (p, 0, 0)),
        ),
        scratch_shapes=[pltpu.VMEM((tree_len, tree_len), f32)],
        compiler_params=pltpu.CompilerParams(vmem_limit_bytes=40 << 20),
        cost_estimate=pl.CostEstimate(
            flops=int(0.6 * 2 * pairs * 4 * tree_len * tree_len * 256),
            bytes_accessed=tree_len * width * 3,
            transcendentals=pairs * tree_len * tree_len,
        ),
    )(qkv, qkv, qkv, cols, rows)


def attention_backward_kernel(
    q_ref, k_ref, v_ref, do_ref, o_ref, lse_ref, col_ref, row_ref, dx_ref, bias, split_k, dk, dv
):
    tree_len = q_ref.shape[0]
    rows = block_rows(tree_len)
    pair = pl.program_id(0)
    pairs = pl.num_programs(0)

    @pl.when(pair == 0)
    def _():
        for start in range(0, tree_len, rows):
            stop = start + rows
            key_seg = col_ref[:stop, 0:1]
            ok = row_ref[0:1, start:stop] == key_seg
            ok = ok | (row_ref[1:2, start:stop] == key_seg)
            ok = ok | (row_ref[2:3, start:stop] == key_seg)
            j = lax.broadcasted_iota(jnp.int32, (stop, rows), 0)
            i = lax.broadcasted_iota(jnp.int32, (stop, rows), 1) + start
            bias[:stop, start:stop] = jnp.where(ok & (j <= i), 0.0, masked_value).astype(f32)

    split_k[0], split_k[1] = split_heads(k_ref[...])
    dk[...] = jnp.zeros_like(dk)
    dv[...] = jnp.zeros_like(dv)
    sub = lax.broadcasted_iota(jnp.int32, (8, 128), 0)
    lane = lax.broadcasted_iota(jnp.int32, (8, 128), 1)
    own = jnp.where(lane // HEAD_DIM == sub, 1.0, 0.0).astype(f32)
    for start in range(0, tree_len, rows):
        stop = start + rows
        queries = split_heads(q_ref[start:stop, :])
        grads = split_heads(do_ref[start:stop, :])
        product = do_ref[start:stop, :].astype(f32) * o_ref[start:stop, :].astype(f32)
        row_dot = lax.dot_general(
            own,
            product,
            (((1,), (1,)), ((), ())),
            precision=lax.Precision.HIGHEST,
            preferred_element_type=f32,
        )
        probs_low = []
        grad_scores = []
        for h in range(2):
            shift = bias[:stop, start:stop] - lse_ref[0, h : h + 1, start:stop]
            probs = jnp.exp2(dot_nt(k_ref[:stop, :], queries[h]) * exp2_scale + shift)
            grad_probs = dot_nt(v_ref[:stop, :], grads[h])
            probs_low.append(probs.astype(bf16))
            grad_scores.append((probs * (grad_probs - row_dot[h : h + 1, :])).astype(bf16))
        dv[:stop, :] += dot_nn(jnp.concatenate(probs_low, 1), jnp.concatenate(grads, 0))
        dk[:stop, :] += dot_nn(jnp.concatenate(grad_scores, 1), jnp.concatenate(queries, 0))
        dq = dot_tn(grad_scores[0], split_k[0, :stop, :])
        dq = dq + dot_tn(grad_scores[1], split_k[1, :stop, :])
        dq = (dq.astype(bf16).astype(f32) * grad_scale).astype(bf16)
        dx_ref[start:stop, pl.ds(pl.multiple_of(pair * 128, 128), 128)] = dq
    dx_ref[:, pl.ds(pl.multiple_of((pairs + pair) * 128, 128), 128)] = (
        dk[...] * grad_scale
    ).astype(bf16)
    dx_ref[:, pl.ds(pl.multiple_of((2 * pairs + pair) * 128, 128), 128)] = dv[...].astype(bf16)


def attention_backward(qkv, grad, out, lse, cols, rows):
    tree_len, width = qkv.shape
    pairs = width // 384
    tile = (tree_len, 128)
    return pl.pallas_call(
        attention_backward_kernel,
        name="attention_backward",
        out_shape=jax.ShapeDtypeStruct((tree_len, width), bf16),
        grid=(pairs,),
        in_specs=[
            pl.BlockSpec(tile, lambda p: (0, p)),
            pl.BlockSpec(tile, lambda p: (0, pairs + p)),
            pl.BlockSpec(tile, lambda p: (0, 2 * pairs + p)),
            pl.BlockSpec(tile, lambda p: (0, p)),
            pl.BlockSpec(tile, lambda p: (0, p)),
            pl.BlockSpec((1, 8, tree_len), lambda p: (p, 0, 0)),
            pl.BlockSpec(cols.shape, lambda p: (0, 0)),
            pl.BlockSpec(rows.shape, lambda p: (0, 0)),
        ],
        out_specs=pl.BlockSpec((tree_len, width), lambda p: (0, 0)),
        scratch_shapes=[
            pltpu.VMEM((tree_len, tree_len), f32),
            pltpu.VMEM((2, tree_len, 128), bf16),
            pltpu.VMEM(tile, f32),
            pltpu.VMEM(tile, f32),
        ],
        compiler_params=pltpu.CompilerParams(vmem_limit_bytes=40 << 20),
        cost_estimate=pl.CostEstimate(
            flops=int(0.6 * 5 * pairs * 4 * tree_len * tree_len * 256),
            bytes_accessed=tree_len * width * 6,
            transcendentals=pairs * tree_len * tree_len,
        ),
    )(qkv, qkv, qkv, grad, out, lse, cols, rows)


def norm_parts(values):
    centered = values - jnp.mean(values, axis=-1, keepdims=True)
    scale = lax.rsqrt(jnp.mean(centered * centered, axis=-1, keepdims=True) + norm_eps)
    return centered * scale, scale


def norm_forward(values, gain, shift):
    return norm_parts(values)[0] * gain + shift


def norm_backward(values, gain, grad):
    xhat, scale = norm_parts(values)
    h = grad * gain
    inner = h - jnp.mean(h, axis=-1, keepdims=True)
    inner = inner - xhat * jnp.mean(h * xhat, axis=-1, keepdims=True)
    return scale * inner, jnp.stack([jnp.sum(grad * xhat, axis=0), jnp.sum(grad, axis=0)])


def gelu_and_slope(values):
    square = values * values
    bent = jnp.tanh(values * (gelu_scale + gelu_scale * gelu_cubic * square))
    half = 0.5 + 0.5 * bent
    made = values * half
    slope = half + made * (1.0 - half) * (2.0 * gelu_scale + 6.0 * gelu_scale * gelu_cubic * square)
    return made, slope


def apart(position, distance):
    bit = 1
    while bit <= distance:
        if distance & bit:
            position = position + bit - 2 * bit * (position // bit % 2)
        bit *= 2
    return position


def gather_kernel(chunks, weights, moved, *refs):
    shards, refs = refs[:weights], refs[weights:]
    tokens, segments, refs = refs[0], refs[1], refs[2:]
    tp = lax.axis_size("tp")
    depth = lax.axis_size("z")
    outs, refs = refs[: weights * tp], refs[weights * tp :]
    segments_out, refs = refs[0], refs[1:]
    tokens_out, refs = (refs[0], refs[1:]) if moved else (None, refs)
    send_sems, recv_sems, local_sems = refs
    z, y, core, x = (lax.axis_index(name) for name in ("z", "y", "core", "tp"))

    barrier = pltpu.get_barrier_semaphore()
    partners = [{"z": apart(z, k)} for k in range(1, depth)]
    partners += [{"tp": apart(x, k)} for k in range(1, tp)]
    partners += [{"y": 1 - y}, {"core": 1 - core}]
    for partner in partners:
        pl.semaphore_signal(barrier, inc=1, device_id=partner, device_id_type=pl.DeviceIdType.MESH)
    pl.semaphore_wait(barrier, len(partners))

    half = depth // 2
    first = pl.ds(z // half * half, half)
    second = pl.ds(half - z // half * half, half)
    started = []

    def copy(source, target, partner):
        slot = len(started)
        made = pltpu.make_async_remote_copy(
            src_ref=source,
            dst_ref=target,
            send_sem=send_sems.at[slot],
            recv_sem=recv_sems.at[slot],
            device_id=partner,
            device_id_type=pl.DeviceIdType.MESH,
        )
        made.start()
        started.append(made)
        return made

    crossed = []
    for k in range(1, tp):
        partner = {"tp": apart(x, k)}
        crossed.append(copy(segments, segments_out.at[k - 1], partner))
        for n in range(moved):
            target = tokens_out.at[n * (tp - 1) + k - 1]
            crossed.append(copy(tokens.at[n * tp + apart(x, k)], target, partner))

    def part(number, t, at_y, span):
        weight, low, rows = chunks[number]
        return outs[weight * tp + t].at[span, at_y, core, pl.ds(low, rows)]

    def along_z(number):
        weight, low, rows = chunks[number]
        own = shards[weight].at[pl.ds(low, rows)]
        target = outs[weight * tp].at[z, y, core, pl.ds(low, rows)]
        keep = pltpu.make_async_copy(own, target, local_sems.at[number])
        keep.start()
        return keep, [copy(own, target, {"z": apart(z, k)}) for k in range(1, depth)]

    def over(number, t, target_t, at_y, span, partner):
        return copy(part(number, t, at_y, span), part(number, target_t, at_y, span), partner)

    def to_core(number, t, at_y, span):
        crossed.append(over(number, t, t, at_y, span, {"core": 1 - core}))

    def plane_start(number, keep, sent):
        keep.wait()
        for k in range(1, half):
            sent[k - 1].wait_recv()
        over_x = [over(number, 0, k, y, first, {"tp": apart(x, k)}) for k in range(1, tp)]
        for k in range(half, depth):
            sent[k - 1].wait_recv()
        over_y = over(number, 0, 0, y, second, {"y": 1 - y})
        last = [(over(number, 0, 0, y, first, {"y": 1 - y}), 0, 1 - y, first)]
        for k in range(1, tp):
            made = over(number, 0, k, y, second, {"tp": apart(x, k)})
            last.append((made, k, y, second))
        to_core(number, 0, y, first)
        to_core(number, 0, y, second)
        return over_x, over_y, last

    def plane_turn(number, over_x, over_y, last):
        for k in range(1, tp):
            over_x[k - 1].wait_recv()
            made = over(number, k, k, y, first, {"y": 1 - y})
            last.append((made, k, 1 - y, first))
            to_core(number, k, y, first)
        over_y.wait_recv()
        for k in range(1, tp):
            made = over(number, 0, k, 1 - y, second, {"tp": apart(x, k)})
            last.append((made, k, 1 - y, second))
        to_core(number, 0, 1 - y, second)
        return last

    def plane_end(number, last):
        for made, t, at_y, span in last:
            made.wait_recv()
            to_core(number, t, at_y, span)

    count = len(chunks)
    state = {0: along_z(0)}
    for step in range(count + 2):
        if step < count:
            state[step] = plane_start(step, *state[step])
            if step + 1 < count:
                state[step + 1] = along_z(step + 1)
        if 0 <= step - 1 < count:
            state[step - 1] = plane_turn(step - 1, *state[step - 1])
        if 0 <= step - 2 < count:
            plane_end(step - 2, state[step - 2])
    for made in crossed:
        made.wait_recv()
    for made in started:
        made.wait_send()


def gather_weights(shards, pieces, tokens, segments):
    tp = lax.axis_size("tp")
    depth = lax.axis_size("z")
    moved = tokens.shape[0] // tp
    chunks = []
    for number, (shard, split) in enumerate(zip(shards, pieces)):
        rows = shard.shape[0] // split
        chunks += [(number, piece * rows, rows) for piece in range(split)]
    copies = len(chunks) * (depth + 1 + 4 * (tp - 1) + 4 * tp)
    copies += (moved + 1) * (tp - 1)
    shapes = [
        jax.ShapeDtypeStruct((depth, 2, 2) + shard.shape, shard.dtype)
        for shard in shards
        for _ in range(tp)
    ]
    sent = sum(shape.size for shape in shapes) * 2
    shapes += [jax.ShapeDtypeStruct((tp - 1,) + segments.shape, segments.dtype)]
    if moved:
        shapes += [jax.ShapeDtypeStruct((moved * (tp - 1),) + tokens.shape[1:], tokens.dtype)]
    inside = pl.BlockSpec(memory_space=pltpu.VMEM)
    outside = pl.BlockSpec(memory_space=pl.ANY)
    made = pl.pallas_call(
        functools.partial(gather_kernel, chunks, len(shards), moved),
        name="gather_weights",
        out_shape=shapes,
        in_specs=[inside] * len(shards) + [outside, inside],
        out_specs=[outside] * len(shapes),
        scratch_shapes=[
            pltpu.SemaphoreType.DMA((copies,)),
            pltpu.SemaphoreType.DMA((copies,)),
            pltpu.SemaphoreType.DMA((len(chunks),)),
        ],
        compiler_params=pltpu.CompilerParams(collective_id=0, has_side_effects=True),
        cost_estimate=pl.CostEstimate(flops=0, bytes_accessed=2 * sent, transcendentals=0),
    )(*shards, tokens, segments)
    count = len(shards) * tp
    full = [array.reshape(-1, array.shape[-1]) for array in made[:count]]
    full = [full[number * tp : (number + 1) * tp] for number in range(len(shards))]
    crossed = made[count:]
    came = [crossed[1][number] for number in range(moved * (tp - 1))] if moved else []
    return full, [crossed[0][k] for k in range(tp - 1)], came


def send(values, axes, distance):
    count = 1
    for axis in (axes,) if isinstance(axes, str) else axes:
        count *= lax.axis_size(axis)
    return lax.ppermute(values, axes, [(s, s ^ distance) for s in range(count)])


def after(values, *others):
    return lax.optimization_barrier((values,) + others)[0]


def pick(pieces, position):
    chosen = pieces[0]
    for number in range(1, len(pieces)):
        chosen = jnp.where(position == number, pieces[number], chosen)
    return chosen


def exchange_tp(pieces):
    return pieces[:1] + [send(pieces[k], "tp", k) for k in range(1, len(pieces))]


def in_place_order(pieces):
    here = lax.axis_index("tp")
    return jnp.concatenate([pick(pieces, here ^ s) for s in range(len(pieces))], axis=0)


def sum_everywhere(values):
    for axes in (("y", "tp"), ("z",), ("core",)):
        count = 1
        for axis in axes:
            count *= lax.axis_size(axis)
        values = sum([send(values, axes, k) for k in range(1, count)], values)
    return values


def block_at(values, axis, index):
    return lax.dynamic_index_in_dim(values, index, axis, keepdims=False)


def scatter_core(part):
    depth, core = lax.axis_size("z"), lax.axis_index("core")
    blocks = part.reshape(depth, 2, 2, -1, part.shape[1])
    came = send(block_at(blocks, 2, 1 - core), "core", 1)
    return (block_at(blocks, 2, core).astype(f32) + came.astype(f32)).astype(bf16)


def scatter_plane(parts, pieces=1):
    y = lax.axis_index("y")
    straight, across = [[] for _ in range(pieces)], [[] for _ in range(pieces)]
    size = parts[0].shape[0] // pieces
    for piece in range(pieces):
        rows = [part[piece * size : (piece + 1) * size] for part in parts]
        straight[piece].append(block_at(rows[0], 1, y))
        for t in range(len(parts)):
            for j in range(2):
                if t or j:
                    came = send(block_at(rows[t], 1, y ^ j), ("y", "tp"), j * len(parts) + t)
                    (across if t and j else straight)[piece].append(came)
    return straight, across


def flat(pieces):
    return [value for piece in pieces for value in piece]


def over_y(part):
    y = lax.axis_index("y")
    return block_at(part, 1, y), send(block_at(part, 1, 1 - y), "y", 1)


def over_tp(pairs):
    return [send(total([list(pair)], [[]]), "tp", t + 1) for t, pair in enumerate(pairs)]


def total(straight, across):
    sums = []
    for near, far in zip(straight, across):
        pieces = near + far
        made = sum([piece.astype(f32) for piece in pieces[1:]], pieces[0].astype(f32))
        sums.append(made.astype(bf16))
    return jnp.concatenate(sums, axis=0)


def scatter_z(part, *late):
    z = lax.axis_index("z")
    made = block_at(part, 0, z).astype(f32)
    for k in range(1, part.shape[0]):
        came = send(block_at(part, 0, z ^ k), "z", k)
        made = made + (after(came, *late) if late else came).astype(f32)
    return made


def segment_tables(segments, parents):
    labels = jnp.arange(parents.shape[0], dtype=jnp.int32)
    up = lambda seg: jnp.sum(jnp.where(seg[:, None] == labels, parents, 0), axis=1)
    parent = up(segments)
    table = jnp.stack([segments, parent, up(parent)])
    return jnp.pad(table.T, ((0, 0), (0, 5))), jnp.pad(table, ((0, 5), (0, 0)))


def on_device(
    tokens, segments, parents, norm_gains, norm_biases, w_qkv, w_out, w_up, w_down, cotangent
):
    tp = lax.axis_size("tp")
    here = lax.axis_index("tp")
    micro = tokens.shape[0]
    own_rows = tokens.shape[2]
    width = tokens.shape[3]
    head_width = w_out.shape[0]
    tree_len = own_rows * tp
    whole = micro // tp
    shared = list(range(whole * tp, micro))
    share_count = len(shared)
    halves = range(tp)
    split = whole * tree_len

    def outgoing(values):
        return [block_at(values, 0, n * tp + (here ^ k)) for n in range(whole) for k in range(1, tp)]

    def whole_trees(values, came):
        rows = []
        for n in range(whole):
            near = [block_at(values, 0, n * tp + here)]
            rows.append(in_place_order(near + came[n * (tp - 1) : (n + 1) * (tp - 1)]))
        return rows

    def rows_back(values):
        trees = values.reshape(micro, own_rows, width)
        back = []
        for n in range(whole):
            pieces = [block_at(trees, 0, n * tp + here)]
            for k in range(1, tp):
                low = block_at(trees, 0, n * tp + (here ^ k)).astype(bf16)
                pieces.append(send(low, "tp", k).astype(values.dtype))
            back += [pick(pieces, here ^ s) for s in halves]
        return jnp.stack(back + [trees[m] for m in shared])[:, None]

    def share_rows(values, k):
        return lax.dynamic_slice_in_dim(values, (here ^ k) * own_rows, own_rows)

    shard_qkv = w_qkv.reshape(w_qkv.shape[0], -1)
    (full_qkv, full_out, full_up), seg_came, tokens_came = gather_weights(
        [shard_qkv, w_out.T, w_up], [4, 1, 4], tokens[:, 0], segments[:, 0]
    )
    down = lax.all_gather(
        after(w_down.T, full_qkv[0]), ("tp", "z", "y", "core"), axis=0, tiled=True
    ).reshape(tp, width, -1)
    full_down = [pick([down[s] for s in halves], here ^ t) for t in halves]
    seg_came = [segments[:, 0]] + seg_came
    seg_all = jnp.concatenate([pick(seg_came, here ^ s) for s in halves], axis=1)
    rows = whole_trees(tokens[:, 0], tokens_came) + [tokens[m, 0] for m in shared]
    x = lax.optimization_barrier(jnp.concatenate(rows, axis=0)).astype(f32)
    whole_tables = []
    for n in range(whole):
        seg = pick([seg_all[n * tp + s] for s in halves], here)
        par = pick([parents[n * tp + s, 0] for s in halves], here)
        whole_tables.append(segment_tables(seg, par))
    share_tables = [segment_tables(seg_all[m], parents[m, 0]) for m in shared]

    normed = norm_forward(x, norm_gains[0], norm_biases[0]).astype(bf16)
    normed_whole = normed[:split]
    share_qkv = [dot_nn(normed[split:], w).astype(bf16) for w in full_qkv]
    whole_qkv = [dot_nn(normed_whole, w).astype(bf16) for w in full_qkv] if whole else []
    share_calls = []
    for n in range(share_count):
        cut = slice(n * own_rows, (n + 1) * own_rows)
        share_calls.append(in_place_order(exchange_tp([part[cut] for part in share_qkv])))
    whole_out = [[] for _ in halves]
    share_out = [[] for _ in halves]
    saved = {}
    for n in range(whole):
        for t in halves:
            qkv = whole_qkv[t][n * tree_len : (n + 1) * tree_len]
            out, lse = attention_forward(qkv, *whole_tables[n])
            saved[n, t] = (qkv, out, lse)
            whole_out[t].append(out)
    share_calls = [after(call, *whole_out[0]) for call in share_calls]
    for n in range(share_count):
        out, lse = attention_forward(share_calls[n], *share_tables[n])
        saved[n] = (share_calls[n], out, lse)
        parts = exchange_tp([share_rows(out, k) for k in halves])
        for t in halves:
            share_out[t].append(parts[t])
    attended = [jnp.concatenate(whole_out[t] + share_out[t], axis=0) for t in halves]
    cotangent = after(cotangent[:, 0], *attended)
    cotangent_came = [send(piece, "tp", n % (tp - 1) + 1) for n, piece in enumerate(outgoing(cotangent))]
    branch_a = sum(dot_nt(attended[t], full_out[t]) for t in halves)
    residual = x + norm_forward(branch_a, norm_gains[1], norm_biases[1])

    normed_f = norm_forward(residual, norm_gains[2], norm_biases[2]).astype(bf16)
    hidden = []
    slope = []
    for t in halves:
        values, bent = gelu_and_slope(dot_nn(normed_f, full_up[t]))
        values, bent = lax.optimization_barrier((values.astype(bf16), bent.astype(bf16)))
        hidden.append(values)
        slope.append(bent)
    crossing = []
    for n in range(share_count):
        start = split + n * own_rows
        near = after(normed[start : start + own_rows], hidden[0])
        crossing.append(exchange_tp([near] * tp))
    branch_f = sum(dot_nt(hidden[t], full_down[t]) for t in halves)
    out = (residual + norm_forward(branch_f, norm_gains[3], norm_biases[3])).astype(bf16)
    out_rows = rows_back(out)

    grad_out = whole_trees(cotangent, cotangent_came) + [cotangent[m] for m in shared]
    grad_out = lax.optimization_barrier(jnp.concatenate(grad_out, axis=0)).astype(f32)
    grad_branch_f, sums_3 = norm_backward(branch_f, norm_gains[3], grad_out)
    grad_branch_f = grad_branch_f.astype(bf16)
    core_down = [scatter_core(dot_tn(grad_branch_f, hidden[t]).astype(bf16)) for t in halves]
    grad_up = [
        (dot_nn(grad_branch_f, full_down[t]) * slope[t].astype(f32)).astype(bf16) for t in halves
    ]
    grad_up = [after(values, *core_down) for values in grad_up]
    straight_down, across_down = scatter_plane(core_down, 2)
    dw_up = [dot_tn(normed_f, grad_up[0]).astype(bf16)]
    ready = [*dw_up, *straight_down[0]]
    dw_up += [dot_tn(after(normed_f, *ready), grad_up[t]).astype(bf16) for t in halves[1:]]
    core_up = [scatter_core(part) for part in dw_up]
    grad_up = [after(values, *dw_up, *straight_down[1]) for values in grad_up]
    grad_up[1:] = [after(values, *across_down[0]) for values in grad_up[1:]]
    grad_normed_f = sum(dot_nt(grad_up[t], full_up[t]) for t in halves)
    grad_part, sums_2 = norm_backward(residual, norm_gains[2], grad_normed_f)
    grad_residual = grad_out + grad_part

    grad_branch_a, sums_1 = norm_backward(branch_a, norm_gains[1], grad_residual)
    grad_branch_a = after(grad_branch_a.astype(bf16), *core_up, *across_down[1])
    up_y = {t: over_y(core_up[t]) for t in halves[1:]}
    share_grad = [dot_nn(grad_branch_a[split:], w).astype(bf16) for w in full_out]
    whole_grad = [dot_nn(grad_branch_a[:split], w).astype(bf16) for w in full_out] if whole else []
    share_do = []
    for n in range(share_count):
        cut = slice(n * own_rows, (n + 1) * own_rows)
        share_do.append(in_place_order(exchange_tp([part[cut] for part in share_grad])))
    grad_qkv = [[] for _ in halves]

    def whole_backward(t, *others):
        for n in range(whole):
            qkv, att, lse = saved[n, t]
            do = after(whole_grad[t][n * tree_len : (n + 1) * tree_len], *share_grad)
            made = attention_backward(qkv, after(do, *others), att, lse, *whole_tables[n])
            grad_qkv[t].append(made)
        return grad_qkv[t]

    made = []
    dw_qkv = [None] * tp
    down = total(straight_down, across_down)
    for t in range(1, tp):
        made += whole_backward(t)
        if whole:
            dw_qkv[t] = dot_tn(normed_whole, jnp.concatenate(grad_qkv[t], axis=0)).astype(bf16)
        else:
            dw_qkv[t] = jnp.zeros(full_qkv[t].shape, bf16)
    z_down = scatter_z(down, *made)
    core_qkv = [None] + [scatter_core(part) for part in dw_qkv[1:]]
    late_grad = after(grad_branch_a, *made)
    up_x = over_tp([up_y[t] for t in halves[1:]])
    core_out = [scatter_core(dot_tn(late_grad, part).astype(bf16)) for part in attended]
    grad_shared = []
    own_part = []
    for n in range(share_count):
        qkv, att, lse = saved[n]
        do = after(share_do[n], *made)
        dx = attention_backward(qkv, do, att, lse, *share_tables[n])
        made = [dx]
        grad_shared.append(dx)
    up_y[0] = over_y(after(core_up[0], *made))
    last = whole_backward(0, *core_qkv[1:], *made) + made
    core_out = [after(part, *last) for part in core_out]
    for n in range(share_count):
        part = dot_nt(grad_shared[n], full_qkv[0])
        pieces = exchange_tp([share_rows(part, 0)] + [share_rows(part, k).astype(bf16) for k in halves[1:]])
        own_part.append(sum([piece.astype(f32) for piece in pieces[1:]], pieces[0]))
    qkv_y = {t: over_y(core_qkv[t]) for t in halves[1:]}
    out_y = {t: over_y(core_out[t]) for t in reversed(halves)}
    ready = [qkv_y[t][1] for t in halves[1:]]
    owned = [after(rows, *ready) for rows in grad_shared]
    qkv_x = over_tp([qkv_y[t] for t in halves[1:]])
    out_x = over_tp([out_y[t] for t in halves[1:]])
    near = in_place_order
    normed_shared = [near([pieces[0]] + [after(piece, *made) for piece in pieces[1:]]) for pieces in crossing]
    owned = [dot_tn(rows, grad) for rows, grad in zip(normed_shared, owned)]
    if whole:
        owned.append(dot_tn(normed_whole, jnp.concatenate(grad_qkv[0], axis=0)))
    dw_qkv[0] = sum(owned).astype(bf16)
    core_qkv[0] = scatter_core(dw_qkv[0])
    z_up_part = after(total([[*up_y[0], *up_x]], [[]]), dw_qkv[0])
    z_out_part = after(total([[*out_y[0], *out_x]], [[]]), dw_qkv[0])
    qkv_y[0] = over_y(core_qkv[0])
    z_qkv = scatter_z(total([[*qkv_y[0], *qkv_x]], [[]]))
    ready = [dw_qkv[0], *up_x, up_y[0][1]]
    grad_normed = list(own_part)
    if whole:
        trees = [after(jnp.concatenate(grad_qkv[t], axis=0), *ready) for t in halves]
        trees[1:] = [after(rows, core_qkv[0]) for rows in trees[1:]]
        grad_normed = [sum(dot_nt(trees[t], full_qkv[t]) for t in halves)] + grad_normed
    grad_normed = jnp.concatenate(grad_normed, axis=0)
    grad_part, sums_0 = norm_backward(x, norm_gains[0], grad_normed)
    grad_x = grad_residual + grad_part
    input_rows = rows_back(grad_x)
    z_up = scatter_z(z_up_part, grad_x)
    z_out = scatter_z(z_out_part, grad_x)
    sums = after(jnp.concatenate([sums_0, sums_1, sums_2, sums_3]), grad_x)
    sums = sum_everywhere(sums).reshape(4, 2, width)
    return (
        out_rows,
        input_rows,
        z_qkv.reshape(w_qkv.shape),
        z_out.T,
        z_up,
        z_down.T,
        sums[:, 0],
        sums[:, 1],
    )


def solution(mesh):
    groups, tp = mesh.devices.shape
    fine = jax.sharding.Mesh(mesh.devices.reshape(groups // 4, 2, 2, tp), ("z", "y", "core", "tp"))
    fsdp = ("z", "y", "core")
    in_specs = (
        P(None, fsdp, "tp", None),
        P(None, fsdp, "tp"),
        P(None, fsdp, None),
        P(),
        P(),
        P(fsdp, None, "tp"),
        P("tp", fsdp),
        P(fsdp, "tp"),
        P("tp", fsdp),
        P(None, fsdp, "tp", None),
    )
    out_specs = (
        P(None, fsdp, "tp", None),
        P(None, fsdp, "tp", None),
        P(fsdp, None, "tp"),
        P("tp", fsdp),
        P(fsdp, "tp"),
        P("tp", fsdp),
        P(),
        P(),
    )
    return jax.shard_map(
        on_device, mesh=fine, in_specs=in_specs, out_specs=out_specs, check_vma=False
    )
```

```python
import functools
import math

import jax
import jax.numpy as jnp
from jax import lax
from jax.experimental import pallas as pl
from jax.experimental.pallas import tpu as pltpu
from jax.sharding import PartitionSpec as P

HEAD_DIM = 64
norm_eps = 1e-05
masked_value = -1e30
f32 = jnp.float32
bf16 = jnp.bfloat16
exp2_scale = math.log2(math.e) / math.sqrt(HEAD_DIM)
grad_scale = 1.0 / math.sqrt(HEAD_DIM)
gelu_scale = math.sqrt(2.0 / math.pi)
gelu_cubic = 0.044715


def dot_nn(a, b):
    return lax.dot_general(a, b, (((1,), (0,)), ((), ())), preferred_element_type=f32)


def dot_nt(a, b):
    return lax.dot_general(a, b, (((1,), (1,)), ((), ())), preferred_element_type=f32)


def dot_tn(a, b):
    return lax.dot_general(a, b, (((0,), (0,)), ((), ())), preferred_element_type=f32)


def split_heads(x):
    lane = lax.broadcasted_iota(jnp.int32, x.shape, 1)
    zero = jnp.zeros_like(x)
    return jnp.where(lane < HEAD_DIM, x, zero), jnp.where(lane >= HEAD_DIM, x, zero)


def block_rows(tree_len):
    return 256 if tree_len % 256 == 0 else 128


def attention_forward_kernel(q_ref, k_ref, v_ref, col_ref, row_ref, o_ref, lse_ref, bias):
    tree_len = q_ref.shape[0]
    rows = block_rows(tree_len)

    @pl.when(pl.program_id(0) == 0)
    def _():
        for start in range(0, tree_len, rows):
            stop = start + rows
            key_seg = row_ref[0:1, :stop]
            ok = col_ref[start:stop, 0:1] == key_seg
            ok = ok | (col_ref[start:stop, 1:2] == key_seg)
            ok = ok | (col_ref[start:stop, 2:3] == key_seg)
            i = lax.broadcasted_iota(jnp.int32, (rows, stop), 0) + start
            j = lax.broadcasted_iota(jnp.int32, (rows, stop), 1)
            bias[start:stop, :stop] = jnp.where(ok & (j <= i), 0.0, masked_value).astype(f32)

    for start in range(0, tree_len, rows):
        stop = start + rows
        queries = split_heads(q_ref[start:stop, :])
        outs = []
        for h in range(2):
            scores = dot_nt(queries[h], k_ref[:stop, :]) + bias[start:stop, :stop]
            top = jnp.max(scores, axis=1, keepdims=True)
            weights = jnp.exp2((scores - top) * exp2_scale)
            total = jnp.sum(weights, axis=1, keepdims=True)
            outs.append(dot_nn(weights.astype(bf16), v_ref[:stop, :]) / total)
            lse = jnp.broadcast_to(top * exp2_scale + jnp.log2(total), (rows, 128))
            lse_ref[0, h : h + 1, start:stop] = jnp.transpose(lse)[0:1, :]
        lane = lax.broadcasted_iota(jnp.int32, (rows, 128), 1)
        o_ref[start:stop, :] = jnp.where(lane < HEAD_DIM, outs[0], outs[1]).astype(bf16)


def attention_forward(qkv, cols, rows):
    tree_len, width = qkv.shape
    pairs = width // 384
    tile = (tree_len, 128)
    return pl.pallas_call(
        attention_forward_kernel,
        name="attention_forward",
        out_shape=(
            jax.ShapeDtypeStruct((tree_len, width // 3), bf16),
            jax.ShapeDtypeStruct((pairs, 8, tree_len), f32),
        ),
        grid=(pairs,),
        in_specs=[
            pl.BlockSpec(tile, lambda p: (0, p)),
            pl.BlockSpec(tile, lambda p: (0, pairs + p)),
            pl.BlockSpec(tile, lambda p: (0, 2 * pairs + p)),
            pl.BlockSpec(cols.shape, lambda p: (0, 0)),
            pl.BlockSpec(rows.shape, lambda p: (0, 0)),
        ],
        out_specs=(
            pl.BlockSpec(tile, lambda p: (0, p)),
            pl.BlockSpec((1, 8, tree_len), lambda p: (p, 0, 0)),
        ),
        scratch_shapes=[pltpu.VMEM((tree_len, tree_len), f32)],
        compiler_params=pltpu.CompilerParams(vmem_limit_bytes=40 << 20),
        cost_estimate=pl.CostEstimate(
            flops=int(0.6 * 2 * pairs * 4 * tree_len * tree_len * 256),
            bytes_accessed=tree_len * width * 3,
            transcendentals=pairs * tree_len * tree_len,
        ),
    )(qkv, qkv, qkv, cols, rows)


def attention_backward_kernel(
    q_ref, k_ref, v_ref, do_ref, o_ref, lse_ref, col_ref, row_ref, dx_ref, bias, split_k, dk, dv
):
    tree_len = q_ref.shape[0]
    rows = block_rows(tree_len)
    pair = pl.program_id(0)
    pairs = pl.num_programs(0)

    @pl.when(pair == 0)
    def _():
        for start in range(0, tree_len, rows):
            stop = start + rows
            key_seg = col_ref[:stop, 0:1]
            ok = row_ref[0:1, start:stop] == key_seg
            ok = ok | (row_ref[1:2, start:stop] == key_seg)
            ok = ok | (row_ref[2:3, start:stop] == key_seg)
            j = lax.broadcasted_iota(jnp.int32, (stop, rows), 0)
            i = lax.broadcasted_iota(jnp.int32, (stop, rows), 1) + start
            bias[:stop, start:stop] = jnp.where(ok & (j <= i), 0.0, masked_value).astype(f32)

    split_k[0], split_k[1] = split_heads(k_ref[...])
    dk[...] = jnp.zeros_like(dk)
    dv[...] = jnp.zeros_like(dv)
    sub = lax.broadcasted_iota(jnp.int32, (8, 128), 0)
    lane = lax.broadcasted_iota(jnp.int32, (8, 128), 1)
    own = jnp.where(lane // HEAD_DIM == sub, 1.0, 0.0).astype(f32)
    for start in range(0, tree_len, rows):
        stop = start + rows
        queries = split_heads(q_ref[start:stop, :])
        grads = split_heads(do_ref[start:stop, :])
        product = do_ref[start:stop, :].astype(f32) * o_ref[start:stop, :].astype(f32)
        row_dot = lax.dot_general(
            own,
            product,
            (((1,), (1,)), ((), ())),
            precision=lax.Precision.HIGHEST,
            preferred_element_type=f32,
        )
        probs_low = []
        grad_scores = []
        for h in range(2):
            shift = bias[:stop, start:stop] - lse_ref[0, h : h + 1, start:stop]
            probs = jnp.exp2(dot_nt(k_ref[:stop, :], queries[h]) * exp2_scale + shift)
            grad_probs = dot_nt(v_ref[:stop, :], grads[h])
            probs_low.append(probs.astype(bf16))
            grad_scores.append((probs * (grad_probs - row_dot[h : h + 1, :])).astype(bf16))
        dv[:stop, :] += dot_nn(jnp.concatenate(probs_low, 1), jnp.concatenate(grads, 0))
        dk[:stop, :] += dot_nn(jnp.concatenate(grad_scores, 1), jnp.concatenate(queries, 0))
        dq = dot_tn(grad_scores[0], split_k[0, :stop, :])
        dq = dq + dot_tn(grad_scores[1], split_k[1, :stop, :])
        dq = (dq.astype(bf16).astype(f32) * grad_scale).astype(bf16)
        dx_ref[start:stop, pl.ds(pl.multiple_of(pair * 128, 128), 128)] = dq
    dx_ref[:, pl.ds(pl.multiple_of((pairs + pair) * 128, 128), 128)] = (
        dk[...] * grad_scale
    ).astype(bf16)
    dx_ref[:, pl.ds(pl.multiple_of((2 * pairs + pair) * 128, 128), 128)] = dv[...].astype(bf16)


def attention_backward(qkv, grad, out, lse, cols, rows):
    tree_len, width = qkv.shape
    pairs = width // 384
    tile = (tree_len, 128)
    return pl.pallas_call(
        attention_backward_kernel,
        name="attention_backward",
        out_shape=jax.ShapeDtypeStruct((tree_len, width), bf16),
        grid=(pairs,),
        in_specs=[
            pl.BlockSpec(tile, lambda p: (0, p)),
            pl.BlockSpec(tile, lambda p: (0, pairs + p)),
            pl.BlockSpec(tile, lambda p: (0, 2 * pairs + p)),
            pl.BlockSpec(tile, lambda p: (0, p)),
            pl.BlockSpec(tile, lambda p: (0, p)),
            pl.BlockSpec((1, 8, tree_len), lambda p: (p, 0, 0)),
            pl.BlockSpec(cols.shape, lambda p: (0, 0)),
            pl.BlockSpec(rows.shape, lambda p: (0, 0)),
        ],
        out_specs=pl.BlockSpec((tree_len, width), lambda p: (0, 0)),
        scratch_shapes=[
            pltpu.VMEM((tree_len, tree_len), f32),
            pltpu.VMEM((2, tree_len, 128), bf16),
            pltpu.VMEM(tile, f32),
            pltpu.VMEM(tile, f32),
        ],
        compiler_params=pltpu.CompilerParams(vmem_limit_bytes=40 << 20),
        cost_estimate=pl.CostEstimate(
            flops=int(0.6 * 5 * pairs * 4 * tree_len * tree_len * 256),
            bytes_accessed=tree_len * width * 6,
            transcendentals=pairs * tree_len * tree_len,
        ),
    )(qkv, qkv, qkv, grad, out, lse, cols, rows)


def norm_parts(values):
    centered = values - jnp.mean(values, axis=-1, keepdims=True)
    scale = lax.rsqrt(jnp.mean(centered * centered, axis=-1, keepdims=True) + norm_eps)
    return centered * scale, scale


def norm_forward(values, gain, shift):
    return norm_parts(values)[0] * gain + shift


def norm_backward(values, gain, grad):
    xhat, scale = norm_parts(values)
    h = grad * gain
    inner = h - jnp.mean(h, axis=-1, keepdims=True)
    inner = inner - xhat * jnp.mean(h * xhat, axis=-1, keepdims=True)
    return scale * inner, jnp.stack([jnp.sum(grad * xhat, axis=0), jnp.sum(grad, axis=0)])


def gelu_and_slope(values):
    square = values * values
    bent = jnp.tanh(values * (gelu_scale + gelu_scale * gelu_cubic * square))
    half = 0.5 + 0.5 * bent
    made = values * half
    slope = half + made * (1.0 - half) * (2.0 * gelu_scale + 6.0 * gelu_scale * gelu_cubic * square)
    return made, slope


def apart(position, distance):
    bit = 1
    while bit <= distance:
        if distance & bit:
            position = position + bit - 2 * bit * (position // bit % 2)
        bit *= 2
    return position


def gather_kernel(chunks, weights, moved, *refs):
    shards, refs = refs[:weights], refs[weights:]
    tokens, segments, refs = refs[0], refs[1], refs[2:]
    tp = lax.axis_size("tp")
    depth = lax.axis_size("z")
    outs, refs = refs[: weights * tp], refs[weights * tp :]
    segments_out, refs = refs[0], refs[1:]
    tokens_out, refs = (refs[0], refs[1:]) if moved else (None, refs)
    send_sems, recv_sems, local_sems = refs
    z, y, core, x = (lax.axis_index(name) for name in ("z", "y", "core", "tp"))

    barrier = pltpu.get_barrier_semaphore()
    partners = [{"z": apart(z, k)} for k in range(1, depth)]
    partners += [{"tp": apart(x, k)} for k in range(1, tp)]
    partners += [{"y": 1 - y}, {"core": 1 - core}]
    for partner in partners:
        pl.semaphore_signal(barrier, inc=1, device_id=partner, device_id_type=pl.DeviceIdType.MESH)
    pl.semaphore_wait(barrier, len(partners))

    half = depth // 2
    first = pl.ds(z // half * half, half)
    second = pl.ds(half - z // half * half, half)
    started = []

    def copy(source, target, partner):
        slot = len(started)
        made = pltpu.make_async_remote_copy(
            src_ref=source,
            dst_ref=target,
            send_sem=send_sems.at[slot],
            recv_sem=recv_sems.at[slot],
            device_id=partner,
            device_id_type=pl.DeviceIdType.MESH,
        )
        made.start()
        started.append(made)
        return made

    crossed = []
    for k in range(1, tp):
        partner = {"tp": apart(x, k)}
        crossed.append(copy(segments, segments_out.at[k - 1], partner))
        for n in range(moved):
            target = tokens_out.at[n * (tp - 1) + k - 1]
            crossed.append(copy(tokens.at[n * tp + apart(x, k)], target, partner))

    def part(number, t, at_y, span):
        weight, low, rows = chunks[number]
        return outs[weight * tp + t].at[span, at_y, core, pl.ds(low, rows)]

    def along_z(number):
        weight, low, rows = chunks[number]
        own = shards[weight].at[pl.ds(low, rows)]
        target = outs[weight * tp].at[z, y, core, pl.ds(low, rows)]
        keep = pltpu.make_async_copy(own, target, local_sems.at[number])
        keep.start()
        return keep, [copy(own, target, {"z": apart(z, k)}) for k in range(1, depth)]

    def over(number, t, target_t, at_y, span, partner):
        return copy(part(number, t, at_y, span), part(number, target_t, at_y, span), partner)

    def to_core(number, t, at_y, span):
        crossed.append(over(number, t, t, at_y, span, {"core": 1 - core}))

    def plane_start(number, keep, sent):
        keep.wait()
        for k in range(1, half):
            sent[k - 1].wait_recv()
        over_x = [over(number, 0, k, y, first, {"tp": apart(x, k)}) for k in range(1, tp)]
        for k in range(half, depth):
            sent[k - 1].wait_recv()
        over_y = over(number, 0, 0, y, second, {"y": 1 - y})
        last = [(over(number, 0, 0, y, first, {"y": 1 - y}), 0, 1 - y, first)]
        for k in range(1, tp):
            made = over(number, 0, k, y, second, {"tp": apart(x, k)})
            last.append((made, k, y, second))
        to_core(number, 0, y, first)
        to_core(number, 0, y, second)
        return over_x, over_y, last

    def plane_turn(number, over_x, over_y, last):
        for k in range(1, tp):
            over_x[k - 1].wait_recv()
            made = over(number, k, k, y, first, {"y": 1 - y})
            last.append((made, k, 1 - y, first))
            to_core(number, k, y, first)
        over_y.wait_recv()
        for k in range(1, tp):
            made = over(number, 0, k, 1 - y, second, {"tp": apart(x, k)})
            last.append((made, k, 1 - y, second))
        to_core(number, 0, 1 - y, second)
        return last

    def plane_end(number, last):
        for made, t, at_y, span in last:
            made.wait_recv()
            to_core(number, t, at_y, span)

    count = len(chunks)
    state = {0: along_z(0)}
    for step in range(count + 2):
        if step < count:
            state[step] = plane_start(step, *state[step])
            if step + 1 < count:
                state[step + 1] = along_z(step + 1)
        if 0 <= step - 1 < count:
            state[step - 1] = plane_turn(step - 1, *state[step - 1])
        if 0 <= step - 2 < count:
            plane_end(step - 2, state[step - 2])
    for made in crossed:
        made.wait_recv()
    for made in started:
        made.wait_send()


def gather_weights(shards, pieces, tokens, segments):
    tp = lax.axis_size("tp")
    depth = lax.axis_size("z")
    moved = tokens.shape[0] // tp
    chunks = []
    for number, (shard, split) in enumerate(zip(shards, pieces)):
        rows = shard.shape[0] // split
        chunks += [(number, piece * rows, rows) for piece in range(split)]
    copies = len(chunks) * (depth + 1 + 4 * (tp - 1) + 4 * tp)
    copies += (moved + 1) * (tp - 1)
    shapes = [
        jax.ShapeDtypeStruct((depth, 2, 2) + shard.shape, shard.dtype)
        for shard in shards
        for _ in range(tp)
    ]
    sent = sum(shape.size for shape in shapes) * 2
    shapes += [jax.ShapeDtypeStruct((tp - 1,) + segments.shape, segments.dtype)]
    if moved:
        shapes += [jax.ShapeDtypeStruct((moved * (tp - 1),) + tokens.shape[1:], tokens.dtype)]
    inside = pl.BlockSpec(memory_space=pltpu.VMEM)
    outside = pl.BlockSpec(memory_space=pl.ANY)
    made = pl.pallas_call(
        functools.partial(gather_kernel, chunks, len(shards), moved),
        name="gather_weights",
        out_shape=shapes,
        in_specs=[inside] * len(shards) + [outside, inside],
        out_specs=[outside] * len(shapes),
        scratch_shapes=[
            pltpu.SemaphoreType.DMA((copies,)),
            pltpu.SemaphoreType.DMA((copies,)),
            pltpu.SemaphoreType.DMA((len(chunks),)),
        ],
        compiler_params=pltpu.CompilerParams(collective_id=0, has_side_effects=True),
        cost_estimate=pl.CostEstimate(flops=0, bytes_accessed=2 * sent, transcendentals=0),
    )(*shards, tokens, segments)
    count = len(shards) * tp
    full = [array.reshape(-1, array.shape[-1]) for array in made[:count]]
    full = [full[number * tp : (number + 1) * tp] for number in range(len(shards))]
    crossed = made[count:]
    came = [crossed[1][number] for number in range(moved * (tp - 1))] if moved else []
    return full, [crossed[0][k] for k in range(tp - 1)], came


def send(values, axes, distance):
    count = 1
    for axis in (axes,) if isinstance(axes, str) else axes:
        count *= lax.axis_size(axis)
    return lax.ppermute(values, axes, [(s, s ^ distance) for s in range(count)])


def after(values, *others):
    return lax.optimization_barrier((values,) + others)[0]


def pick(pieces, position):
    chosen = pieces[0]
    for number in range(1, len(pieces)):
        chosen = jnp.where(position == number, pieces[number], chosen)
    return chosen


def exchange_tp(pieces):
    return pieces[:1] + [send(pieces[k], "tp", k) for k in range(1, len(pieces))]


def in_place_order(pieces):
    here = lax.axis_index("tp")
    return jnp.concatenate([pick(pieces, here ^ s) for s in range(len(pieces))], axis=0)


def sum_everywhere(values):
    for axes in (("y", "tp"), ("z",), ("core",)):
        count = 1
        for axis in axes:
            count *= lax.axis_size(axis)
        values = sum([send(values, axes, k) for k in range(1, count)], values)
    return values


def block_at(values, axis, index):
    return lax.dynamic_index_in_dim(values, index, axis, keepdims=False)


def scatter_core(part):
    depth, core = lax.axis_size("z"), lax.axis_index("core")
    blocks = part.reshape(depth, 2, 2, -1, part.shape[1])
    came = send(block_at(blocks, 2, 1 - core), "core", 1)
    return (block_at(blocks, 2, core).astype(f32) + came.astype(f32)).astype(bf16)


def scatter_plane(parts, pieces=1):
    y = lax.axis_index("y")
    straight, across = [[] for _ in range(pieces)], [[] for _ in range(pieces)]
    size = parts[0].shape[0] // pieces
    for piece in range(pieces):
        rows = [part[piece * size : (piece + 1) * size] for part in parts]
        straight[piece].append(block_at(rows[0], 1, y))
        for t in range(len(parts)):
            for j in range(2):
                if t or j:
                    came = send(block_at(rows[t], 1, y ^ j), ("y", "tp"), j * len(parts) + t)
                    (across if t and j else straight)[piece].append(came)
    return straight, across


def flat(pieces):
    return [value for piece in pieces for value in piece]


def over_y(part):
    y = lax.axis_index("y")
    return block_at(part, 1, y), send(block_at(part, 1, 1 - y), "y", 1)


def over_tp(pairs):
    return [send(total([list(pair)], [[]]), "tp", t + 1) for t, pair in enumerate(pairs)]


def total(straight, across):
    sums = []
    for near, far in zip(straight, across):
        pieces = near + far
        made = sum([piece.astype(f32) for piece in pieces[1:]], pieces[0].astype(f32))
        sums.append(made.astype(bf16))
    return jnp.concatenate(sums, axis=0)


def scatter_z(part, *late):
    z = lax.axis_index("z")
    made = block_at(part, 0, z).astype(f32)
    for k in range(1, part.shape[0]):
        came = send(block_at(part, 0, z ^ k), "z", k)
        made = made + (after(came, *late) if late else came).astype(f32)
    return made


def segment_tables(segments, parents):
    labels = jnp.arange(parents.shape[0], dtype=jnp.int32)
    up = lambda seg: jnp.sum(jnp.where(seg[:, None] == labels, parents, 0), axis=1)
    parent = up(segments)
    table = jnp.stack([segments, parent, up(parent)])
    return jnp.pad(table.T, ((0, 0), (0, 5))), jnp.pad(table, ((0, 5), (0, 0)))


def on_device(
    tokens, segments, parents, norm_gains, norm_biases, w_qkv, w_out, w_up, w_down, cotangent
):
    tp = lax.axis_size("tp")
    here = lax.axis_index("tp")
    micro = tokens.shape[0]
    own_rows = tokens.shape[2]
    width = tokens.shape[3]
    head_width = w_out.shape[0]
    tree_len = own_rows * tp
    whole = micro // tp
    shared = list(range(whole * tp, micro))
    share_count = len(shared)
    halves = range(tp)
    split = whole * tree_len

    def outgoing(values):
        return [block_at(values, 0, n * tp + (here ^ k)) for n in range(whole) for k in range(1, tp)]

    def whole_trees(values, came):
        rows = []
        for n in range(whole):
            near = [block_at(values, 0, n * tp + here)]
            rows.append(in_place_order(near + came[n * (tp - 1) : (n + 1) * (tp - 1)]))
        return rows

    def rows_back(values):
        trees = values.reshape(micro, own_rows, width)
        back = []
        for n in range(whole):
            pieces = [block_at(trees, 0, n * tp + here)]
            for k in range(1, tp):
                low = block_at(trees, 0, n * tp + (here ^ k)).astype(bf16)
                pieces.append(send(low, "tp", k).astype(values.dtype))
            back += [pick(pieces, here ^ s) for s in halves]
        return jnp.stack(back + [trees[m] for m in shared])[:, None]

    def share_rows(values, k):
        return lax.dynamic_slice_in_dim(values, (here ^ k) * own_rows, own_rows)

    shard_qkv = w_qkv.reshape(w_qkv.shape[0], -1)
    (full_qkv, full_out, full_up), seg_came, tokens_came = gather_weights(
        [shard_qkv, w_out.T, w_up], [4, 1, 4], tokens[:, 0], segments[:, 0]
    )
    down = lax.all_gather(
        after(w_down.T, full_qkv[0]), ("tp", "z", "y", "core"), axis=0, tiled=True
    ).reshape(tp, width, -1)
    full_down = [pick([down[s] for s in halves], here ^ t) for t in halves]
    seg_came = [segments[:, 0]] + seg_came
    seg_all = jnp.concatenate([pick(seg_came, here ^ s) for s in halves], axis=1)
    rows = whole_trees(tokens[:, 0], tokens_came) + [tokens[m, 0] for m in shared]
    x = lax.optimization_barrier(jnp.concatenate(rows, axis=0)).astype(f32)
    whole_tables = []
    for n in range(whole):
        seg = pick([seg_all[n * tp + s] for s in halves], here)
        par = pick([parents[n * tp + s, 0] for s in halves], here)
        whole_tables.append(segment_tables(seg, par))
    share_tables = [segment_tables(seg_all[m], parents[m, 0]) for m in shared]

    normed = norm_forward(x, norm_gains[0], norm_biases[0]).astype(bf16)
    normed_whole = normed[:split]
    share_qkv = [dot_nn(normed[split:], w).astype(bf16) for w in full_qkv]
    whole_qkv = [dot_nn(normed_whole, w).astype(bf16) for w in full_qkv] if whole else []
    share_calls = []
    for n in range(share_count):
        cut = slice(n * own_rows, (n + 1) * own_rows)
        share_calls.append(in_place_order(exchange_tp([part[cut] for part in share_qkv])))
    whole_out = [[] for _ in halves]
    share_out = [[] for _ in halves]
    saved = {}
    for n in range(whole):
        for t in halves:
            qkv = whole_qkv[t][n * tree_len : (n + 1) * tree_len]
            out, lse = attention_forward(qkv, *whole_tables[n])
            saved[n, t] = (qkv, out, lse)
            whole_out[t].append(out)
    share_calls = [after(call, *whole_out[0]) for call in share_calls]
    for n in range(share_count):
        out, lse = attention_forward(share_calls[n], *share_tables[n])
        saved[n] = (share_calls[n], out, lse)
        parts = exchange_tp([share_rows(out, k) for k in halves])
        for t in halves:
            share_out[t].append(parts[t])
    attended = [jnp.concatenate(whole_out[t] + share_out[t], axis=0) for t in halves]
    cotangent = after(cotangent[:, 0], *attended)
    cotangent_came = [send(piece, "tp", n % (tp - 1) + 1) for n, piece in enumerate(outgoing(cotangent))]
    branch_a = sum(dot_nt(attended[t], full_out[t]) for t in halves)
    residual = x + norm_forward(branch_a, norm_gains[1], norm_biases[1])

    normed_f = norm_forward(residual, norm_gains[2], norm_biases[2]).astype(bf16)
    hidden = []
    slope = []
    for t in halves:
        values, bent = gelu_and_slope(dot_nn(normed_f, full_up[t]))
        values, bent = lax.optimization_barrier((values.astype(bf16), bent.astype(bf16)))
        hidden.append(values)
        slope.append(bent)
    crossing = []
    for n in range(share_count):
        start = split + n * own_rows
        near = after(normed[start : start + own_rows], hidden[0])
        crossing.append(exchange_tp([near] * tp))
    branch_f = sum(dot_nt(hidden[t], full_down[t]) for t in halves)
    out = (residual + norm_forward(branch_f, norm_gains[3], norm_biases[3])).astype(bf16)
    out_rows = rows_back(out)

    grad_out = whole_trees(cotangent, cotangent_came) + [cotangent[m] for m in shared]
    grad_out = lax.optimization_barrier(jnp.concatenate(grad_out, axis=0)).astype(f32)
    grad_branch_f, sums_3 = norm_backward(branch_f, norm_gains[3], grad_out)
    grad_branch_f = grad_branch_f.astype(bf16)
    core_down = [scatter_core(dot_tn(grad_branch_f, hidden[t]).astype(bf16)) for t in halves]
    grad_up = [
        (dot_nn(grad_branch_f, full_down[t]) * slope[t].astype(f32)).astype(bf16) for t in halves
    ]
    grad_up = [after(values, *core_down) for values in grad_up]
    straight_down, across_down = scatter_plane(core_down, 2)
    dw_up = [dot_tn(normed_f, grad_up[0]).astype(bf16)]
    ready = [*dw_up, *straight_down[0]]
    dw_up += [dot_tn(after(normed_f, *ready), grad_up[t]).astype(bf16) for t in halves[1:]]
    core_up = [scatter_core(part) for part in dw_up]
    grad_up = [after(values, *dw_up, *straight_down[1]) for values in grad_up]
    grad_up[1:] = [after(values, *across_down[0]) for values in grad_up[1:]]
    grad_normed_f = sum(dot_nt(grad_up[t], full_up[t]) for t in halves)
    grad_part, sums_2 = norm_backward(residual, norm_gains[2], grad_normed_f)
    grad_residual = grad_out + grad_part

    grad_branch_a, sums_1 = norm_backward(branch_a, norm_gains[1], grad_residual)
    grad_branch_a = after(grad_branch_a.astype(bf16), *core_up, *across_down[1])
    up_y = {t: over_y(core_up[t]) for t in halves[1:]}
    share_grad = [dot_nn(grad_branch_a[split:], w).astype(bf16) for w in full_out]
    whole_grad = [dot_nn(grad_branch_a[:split], w).astype(bf16) for w in full_out] if whole else []
    share_do = []
    for n in range(share_count):
        cut = slice(n * own_rows, (n + 1) * own_rows)
        share_do.append(in_place_order(exchange_tp([part[cut] for part in share_grad])))
    grad_qkv = [[] for _ in halves]

    def whole_backward(t, *others):
        for n in range(whole):
            qkv, att, lse = saved[n, t]
            do = after(whole_grad[t][n * tree_len : (n + 1) * tree_len], *share_grad)
            made = attention_backward(qkv, after(do, *others), att, lse, *whole_tables[n])
            grad_qkv[t].append(made)
        return grad_qkv[t]

    made = []
    dw_qkv = [None] * tp
    down = total(straight_down, across_down)
    for t in range(1, tp):
        made += whole_backward(t)
        if whole:
            dw_qkv[t] = dot_tn(normed_whole, jnp.concatenate(grad_qkv[t], axis=0)).astype(bf16)
        else:
            dw_qkv[t] = jnp.zeros(full_qkv[t].shape, bf16)
    z_down = scatter_z(down, *made)
    core_qkv = [None] + [scatter_core(part) for part in dw_qkv[1:]]
    late_grad = after(grad_branch_a, *made)
    up_x = over_tp([up_y[t] for t in halves[1:]])
    core_out = [scatter_core(dot_tn(late_grad, part).astype(bf16)) for part in attended]
    grad_shared = []
    own_part = []
    for n in range(share_count):
        qkv, att, lse = saved[n]
        do = after(share_do[n], *made)
        dx = attention_backward(qkv, do, att, lse, *share_tables[n])
        made = [dx]
        grad_shared.append(dx)
    up_y[0] = over_y(after(core_up[0], *made))
    last = whole_backward(0, *core_qkv[1:], *made) + made
    core_out = [after(part, *last) for part in core_out]
    for n in range(share_count):
        part = dot_nt(grad_shared[n], full_qkv[0])
        pieces = exchange_tp([share_rows(part, 0)] + [share_rows(part, k).astype(bf16) for k in halves[1:]])
        own_part.append(sum([piece.astype(f32) for piece in pieces[1:]], pieces[0]))
    qkv_y = {t: over_y(core_qkv[t]) for t in halves[1:]}
    out_y = {t: over_y(core_out[t]) for t in reversed(halves)}
    ready = [qkv_y[t][1] for t in halves[1:]]
    owned = [after(rows, *ready) for rows in grad_shared]
    qkv_x = over_tp([qkv_y[t] for t in halves[1:]])
    out_x = over_tp([out_y[t] for t in halves[1:]])
    near = in_place_order
    normed_shared = [near([pieces[0]] + [after(piece, *made) for piece in pieces[1:]]) for pieces in crossing]
    owned = [dot_tn(rows, grad) for rows, grad in zip(normed_shared, owned)]
    if whole:
        owned.append(dot_tn(normed_whole, jnp.concatenate(grad_qkv[0], axis=0)))
    dw_qkv[0] = sum(owned).astype(bf16)
    core_qkv[0] = scatter_core(dw_qkv[0])
    z_up_part = after(total([[*up_y[0], *up_x]], [[]]), dw_qkv[0])
    z_out_part = after(total([[*out_y[0], *out_x]], [[]]), dw_qkv[0])
    qkv_y[0] = over_y(core_qkv[0])
    z_qkv = scatter_z(total([[*qkv_y[0], *qkv_x]], [[]]))
    ready = [dw_qkv[0], *up_x, up_y[0][1]]
    grad_normed = list(own_part)
    if whole:
        trees = [after(jnp.concatenate(grad_qkv[t], axis=0), *ready) for t in halves]
        trees[1:] = [after(rows, core_qkv[0]) for rows in trees[1:]]
        grad_normed = [sum(dot_nt(trees[t], full_qkv[t]) for t in halves)] + grad_normed
    grad_normed = jnp.concatenate(grad_normed, axis=0)
    grad_part, sums_0 = norm_backward(x, norm_gains[0], grad_normed)
    grad_x = grad_residual + grad_part
    input_rows = rows_back(grad_x)
    z_up = scatter_z(z_up_part, grad_x)
    z_out = scatter_z(z_out_part, grad_x)
    sums = after(jnp.concatenate([sums_0, sums_1, sums_2, sums_3]), qkv_y[0][1])
    sums = sum_everywhere(sums).reshape(4, 2, width)
    return (
        out_rows,
        input_rows,
        z_qkv.reshape(w_qkv.shape),
        z_out.T,
        z_up,
        z_down.T,
        sums[:, 0],
        sums[:, 1],
    )


def solution(mesh):
    groups, tp = mesh.devices.shape
    fine = jax.sharding.Mesh(mesh.devices.reshape(groups // 4, 2, 2, tp), ("z", "y", "core", "tp"))
    fsdp = ("z", "y", "core")
    in_specs = (
        P(None, fsdp, "tp", None),
        P(None, fsdp, "tp"),
        P(None, fsdp, None),
        P(),
        P(),
        P(fsdp, None, "tp"),
        P("tp", fsdp),
        P(fsdp, "tp"),
        P("tp", fsdp),
        P(None, fsdp, "tp", None),
    )
    out_specs = (
        P(None, fsdp, "tp", None),
        P(None, fsdp, "tp", None),
        P(fsdp, None, "tp"),
        P("tp", fsdp),
        P(fsdp, "tp"),
        P("tp", fsdp),
        P(),
        P(),
    )
    return jax.shard_map(
        on_device, mesh=fine, in_specs=in_specs, out_specs=out_specs, check_vma=False
    )
```
